32 devices in a mesh: seq: 8 (over z, core), tp: 4 (over y, x).
Axes of the slice: x: 2, y: 2, z: 4, core: 2. Of those that a mesh axis runs over, the one named last changes fastest.
Arguments:
- tokens: bfloat16 [6144, 1024], P('seq'), may hold values from -6 to 6
- scene_index: int32 [6144], replicated, may hold values from 0 to 2, never falling along the last dimension, each value on 1 to 3584 neighbouring positions
- inward_weight: bfloat16 [1, 3, 1024, 1024], P(None, None, None, 'tp'), may hold values from -0.25 to 0.25
- outward_weight: bfloat16 [1, 1024, 1024], P(None, 'tp'), may hold values from -0.75 to 0.75
- up_weight: bfloat16 [1, 1024, 4096], P(None, None, 'tp'), may hold values from -0.25 to 0.25
- down_weight: bfloat16 [1, 4096, 1024], P(None, 'tp'), may hold values from -0.125 to 0.125
- norm_gains: float32 [1, 2, 1024], replicated, may hold values from 0.1 to 1.9
- norm_shifts: float32 [1, 2, 1024], replicated, may hold values from -1.5 to 1.5
- cotangent: bfloat16 [6144, 1024], P('seq'), may hold values from -6 to 6
Outputs:
- activations: bfloat16 [6144, 1024], P('seq')
- token_gradient: float32 [6144, 1024], P('seq')
- inward_gradient: float32 [1, 3, 1024, 1024], P(None, None, 'seq', 'tp')
- outward_gradient: float32 [1, 1024, 1024], P(None, 'tp', 'seq')
- up_gradient: float32 [1, 1024, 4096], P(None, 'seq', 'tp')
- down_gradient: float32 [1, 4096, 1024], P(None, 'tp', 'seq')
- gain_gradient: float32 [1, 2, 1024], P(None, None, 'seq')
- shift_gradient: float32 [1, 2, 1024], P(None, None, 'seq')
The draws below stay inside these ranges and needn't reach their ends.
Inputs may be any that keep to these rules, and one draw needn't show every extreme that they name: `scene_index`: scene numbers never fall along the tokens; each scene is one run of 1 to 3584 tokens, one of exactly 3584, and every number from 0 to 2 names a scene.
All inputs are finite; a program needn't handle non-finite values.
Results may differ from the reference program's by a relative error of at most 0.018.
The reference program's roundings to bfloat16 on the way count: a program that leaves them out, or rounds other values in their place, can miss the bound.
Values may be sent and summed in bfloat16 or wider, within the bound.
No kernel may reach another device: no remote copies, remote signals or barrier semaphores. Data moves between devices by JAX's collectives and lax.ppermute only.
A program may use at most 128 MiB of HBM per device.

```python
import math
import jax
import jax.numpy as jnp
import numpy as np
from jax import lax

D = 1024
HEADS = 16
HEAD_DIM = 64
FF = 4096
LAYERS = 1
TOKENS = 6144
LONGEST = 3584
SCENES = 3


def spiked(values, rng, source, target, shards_of, factor):
    owner, partner = [(jnp.arange(values.shape[position]) // (values.shape[position] // shards_of)).reshape([-1 if axis == position else 1 for axis in range(values.ndim)]) for position in (source, target)]
    chosen = jax.random.permutation(rng, shards_of)[partner]
    strong = (owner == chosen) | (owner == (partner + shards_of // 2) % shards_of)
    return jnp.where(strong, factor * values, values)


def block_levels(rng, dims, shards, low, largest):
    def one(axis_at, parts):
        steps = jax.random.uniform(jax.random.fold_in(jax.random.fold_in(rng, 6), axis_at), (parts,), jnp.float32, low / len(shards), largest / len(shards))
        return jnp.repeat(jnp.exp(steps), dims[axis_at] // parts).reshape((-1,) + (1,) * (len(dims) - axis_at - 1))

    factor_of = one(*shards[0])
    for cut in shards[1:]:
        factor_of = factor_of * one(*cut)
    return factor_of


def profile(count, total, most, slope):
    portions = [(1 << 20) // math.isqrt(standing ** slope) + 1 for standing in range(2, count + 1)]
    spare, holding = total - most - (count - 1), [1] * (count - 1)
    while spare > 0:
        candidates = [i for i in range(count - 1) if holding[i] < most]
        whole, budget = sum([portions[i] for i in candidates]), spare
        for i in candidates:
            more = min(most - holding[i], max(1, budget * portions[i] // whole), spare)
            holding[i] = holding[i] + more
            spare = spare - more
    return np.array([most] + holding)


def ragged(key, count, total, limit, lean):
    if count == 2:
        one = jax.random.randint(key, (), max(1, total - limit), min(limit, total - 1) + 1)
        return jnp.stack([one, total - one])
    sizes = jnp.asarray(profile(count, total, limit, lean), jnp.int32)
    couples = (count - 1) // 2
    donor, taker = sizes[1:1 + 2 * couples:2], sizes[2:2 + 2 * couples:2]
    room = jnp.minimum(donor - 1, limit - taker)
    shifted = jax.random.randint(jax.random.fold_in(key, 1), (couples,), 0, 1 << 20) % (room + 1)
    sizes = sizes.at[1:1 + 2 * couples:2].set(donor - shifted).at[2:2 + 2 * couples:2].set(taker + shifted)
    return sizes[jax.random.permutation(jax.random.fold_in(key, 2), count)]


def scatter_about(rng, extent, spread, reach, pieces=(), held_as=jnp.bfloat16):
    values = spread * jax.random.normal(rng, extent, jnp.float32)
    if pieces:
        values = values * block_levels(rng, extent, pieces, -0.22, 0.18)
    return jnp.clip(values, -reach, reach).astype(held_as)


def noise_with(rng, dims, scale, bound, cuts, heavy, held_as=jnp.bfloat16):
    drawn = scale * jax.random.normal(rng, dims, jnp.float32)
    if cuts:
        drawn = drawn * block_levels(rng, dims, cuts, -0.22, 0.18)
    return jnp.clip(spiked(drawn, jax.random.fold_in(rng, 3), *heavy), -bound, bound).astype(held_as)


def setup_inputs(seed: int = 0) -> dict:
    seeds = jax.random.split(jax.random.key(seed), 10)
    return {
        "tokens": scatter_about(seeds[0], (TOKENS, D), 1.0, 6.0, ((0, 8),)),
        "scene_index": jnp.searchsorted(jnp.cumsum(ragged(seeds[1], SCENES, TOKENS, LONGEST, 1)), jnp.arange(TOKENS), side="right").astype(jnp.int32),
        "inward_weight": scatter_about(seeds[2], (LAYERS, 3, D, D), (D // 2) ** -0.5, 0.25, ((3, 4),)),
        "outward_weight": scatter_about(seeds[3], (LAYERS, D, D), (D // 16) ** -0.5, 0.75, ((1, 4),)),
        "up_weight": noise_with(seeds[4], (LAYERS, D, FF), D ** -0.5, 0.25, ((2, 4),), (2, 1, 4, 2.0)),
        "down_weight": noise_with(seeds[5], (LAYERS, FF, D), FF ** -0.5, 0.125, ((1, 4),), (1, 2, 4, 2.0)),
        "norm_gains": jnp.clip(1.0 + 0.18 * jax.random.normal(seeds[6], (LAYERS, 2, D), jnp.float32), 0.1, 1.9),
        "norm_shifts": scatter_about(seeds[7], (LAYERS, 2, D), 0.3, 1.5, (), jnp.float32),
        "cotangent": noise_with(seeds[8], (TOKENS, D), 1.0, 6.0, ((0, 8),), (0, 1, 8, 2.0)),
    }


@jax.custom_vjp
def low(v):
    return lax.optimization_barrier(v.astype(jnp.bfloat16)).astype(jnp.float32)

@jax.custom_vjp
def low_back(v):
    return v

def low_keep(v):
    return (low(v), None)

def low_pass(kept, grad):
    return (grad,)

def back_keep(v):
    return (v, None)

def back_low(kept, grad):
    return (low(grad),)
low.defvjp(low_keep, low_pass)
low_back.defvjp(back_keep, back_low)

def layer_norm(hidden, gain_row, shift_row):
    average = lax.optimization_barrier(jnp.mean(hidden, axis=-1, keepdims=True))
    centered = hidden - average
    variance = lax.optimization_barrier(jnp.mean(centered * centered, axis=-1, keepdims=True))
    return centered * lax.rsqrt(variance + 1e-05) * gain_row + shift_row

def gelu_tanh(preactivation):
    return jax.nn.gelu(preactivation, approximate=True)

def attend_rows(query_rows, row_scenes, key_heads, value_heads, scene_index):
    scores = jnp.einsum('qhd,khd->hqk', query_rows, key_heads, precision=lax.Precision.HIGHEST) * HEAD_DIM ** (-0.5)
    scores = low_back(scores)
    same_scene = (row_scenes[:, None] == scene_index[None, :])[None]
    masked = jnp.where(same_scene, scores, -1e+30)
    row_max = lax.optimization_barrier(jnp.max(masked, axis=-1, keepdims=True))
    weights = jnp.where(same_scene, jnp.exp(masked - row_max), 0.0)
    weights = low(weights / lax.optimization_barrier(jnp.sum(weights, axis=-1, keepdims=True)))
    return jnp.einsum('hqk,khd->qhd', weights, value_heads, precision=lax.Precision.HIGHEST)

def one_layer(hidden, scene_index, inward, outward, upward, downward, gain_pair, shift_pair):
    normed = low(layer_norm(hidden, gain_pair[0], shift_pair[0]))
    projected = jnp.einsum('td,cde->tce', normed, inward, precision=lax.Precision.HIGHEST)
    projected = low(low_back(projected))
    query_heads = projected[:, 0].reshape(TOKENS, HEADS, HEAD_DIM)
    key_heads = projected[:, 1].reshape(TOKENS, HEADS, HEAD_DIM)
    value_heads = projected[:, 2].reshape(TOKENS, HEADS, HEAD_DIM)
    block_rows = min(256, TOKENS)
    block_count = TOKENS // block_rows
    row_blocks = query_heads.reshape(block_count, block_rows, HEADS, HEAD_DIM)
    scene_blocks = scene_index.reshape(block_count, block_rows)

    def per_block(pair_in):
        return attend_rows(pair_in[0], pair_in[1], key_heads, value_heads, scene_index)
    attended = lax.map(jax.checkpoint(per_block), (row_blocks, scene_blocks))
    attended = low(low_back(attended.reshape(TOKENS, D)))
    mixed_sum = low_back(jnp.dot(attended, outward, precision=lax.Precision.HIGHEST))
    after_attention = hidden + mixed_sum
    normed_two = low(layer_norm(after_attention, gain_pair[1], shift_pair[1]))
    preactivation = low_back(jnp.dot(normed_two, upward, precision=lax.Precision.HIGHEST))
    activated = low(gelu_tanh(preactivation))
    branch = low_back(jnp.dot(activated, downward, precision=lax.Precision.HIGHEST))
    return after_attention + branch

def reference(tokens, scene_index, inward_weight, outward_weight, up_weight, down_weight, norm_gains, norm_shifts, cotangent):

    def forward(hidden, inward_all, outward_all, up_all, down_all, gains_all, shifts_all):
        for layer_number in range(LAYERS):
            hidden = one_layer(hidden, scene_index, inward_all[layer_number], outward_all[layer_number], up_all[layer_number], down_all[layer_number], gains_all[layer_number], shifts_all[layer_number])
        return hidden
    result, pullback = jax.vjp(forward, tokens.astype(jnp.float32), inward_weight.astype(jnp.float32), outward_weight.astype(jnp.float32), up_weight.astype(jnp.float32), down_weight.astype(jnp.float32), norm_gains.astype(jnp.float32), norm_shifts.astype(jnp.float32))
    gradients = pullback(cotangent.astype(jnp.float32))
    return (result.astype(jnp.bfloat16), gradients[0], gradients[1], gradients[2], gradients[3], gradients[4], gradients[5], gradients[6])
```

```python
import functools
import math
import jax
import jax.numpy as jnp
from jax import lax
from jax.experimental import pallas as pl
from jax.experimental.pallas import tpu as pltpu
from jax.sharding import PartitionSpec as P

HEAD_DIM = 64
LAYERS = 1
F32, BF16 = jnp.float32, jnp.bfloat16
NEG_FILL = -1e30
SCORE = HEAD_DIM ** -0.5
LOG2E = math.log2(math.e)
ANY = pl.BlockSpec(memory_space=pl.ANY)
VM = pl.BlockSpec(memory_space=pltpu.VMEM)
SM = pl.BlockSpec(memory_space=pltpu.SMEM)
PARAMS = pltpu.CompilerParams(vmem_limit_bytes=60 * 2**20)


def dot(a, b, dims):
    return lax.dot_general(a, b, (dims, ((), ())), preferred_element_type=F32)


def load_all(pairs, sems):
    copies = [pltpu.make_async_copy(s, d, sems.at[i]) for i, (s, d) in enumerate(pairs)]
    for c in copies:
        c.start()
    return copies


def tile_plan(first, last, starts, ends, bk):
    begin, stop = starts[first], ends[last]
    low, high = begin // bk, (stop + bk - 1) // bk
    alone = ends[first] == stop
    clear0 = jnp.where(alone, (begin + bk - 1) // bk, high)
    clear1 = jnp.where(alone, jnp.maximum(clear0, stop // bk), high)
    return low, high, clear0, clear1


def for_tiles(plan, masked, clear):
    low, high, clear0, clear1 = plan
    head = clear0 - low

    def edge(i, _):
        masked(jnp.where(i < head, low + i, clear1 + i - head))
        return 0

    def inner(j, _):
        clear(j)
        return 0

    lax.fori_loop(0, head + high - clear1, edge, 0)
    lax.fori_loop(clear0, clear1, inner, 0)


def low_half(x):
    lane = lax.broadcasted_iota(jnp.int32, x.shape, 1)
    return jnp.where(lane < HEAD_DIM, x, jnp.zeros_like(x))


def high_half(x):
    lane = lax.broadcasted_iota(jnp.int32, x.shape, 1)
    return jnp.where(lane < HEAD_DIM, jnp.zeros_like(x), x)


def swap_halves(x):
    return jnp.concatenate([x[:, HEAD_DIM:], x[:, :HEAD_DIM]], axis=1)


def fwd_kernel(n_kv, n_q, bk, place, starts, ends, begin_rows, stop_rows, *refs):
    kv_in, q_in, refs = refs[:n_kv], refs[n_kv : n_kv + n_q], refs[n_kv + n_q :]
    o_out, (of_out, lse_out, kv), refs = refs[:n_q], refs[n_q : n_q + 3], refs[n_q + 3 :]
    vt, qz, acc, top, ot, sems = refs
    rows, half = kv_in[0].shape[0], q_in[0].shape[0]
    copies = load_all(
        [(kv_in[i], kv.at[pl.ds(pl.multiple_of(place[i] * rows, 128), rows)]) for i in range(n_kv)],
        sems,
    )
    for k in range(n_q):
        q = q_in[k][...]
        qz[2 * k] = low_half(q)
        qz[2 * k + 1] = low_half(swap_halves(q))
    for c in copies:
        c.wait()

    def turn(j, _):
        spot = pl.ds(pl.multiple_of(j * 256, 256), 256)
        vt[:, spot] = kv[spot, :].T[HEAD_DIM:]
        return 0

    lax.fori_loop(0, kv.shape[0] // 256, turn, 0)
    factor = SCORE * LOG2E

    def one(i, _):
        first = place[i // 2] * rows + (i % 2) * half
        query = qz[i]
        acc[...] = jnp.zeros_like(acc)
        top[0:1] = jnp.full((1, half), NEG_FILL, F32)
        top[1:2] = jnp.zeros((1, half), F32)
        slab = first // half

        def visit(j, mask):
            spot = pl.ds(pl.multiple_of(j * bk, bk), bk)
            st = dot(kv[spot, :], query, ((1,), (1,)))
            if mask:
                at = j * bk + lax.broadcasted_iota(jnp.int32, st.shape, 0)
                st = jnp.where((at >= begin_rows[slab]) & (at < stop_rows[slab]), st, NEG_FILL)
            old = top[0:1]
            new = jnp.maximum(old, jnp.max(st, axis=0, keepdims=True))
            p = jnp.exp2(st * factor - new * factor)
            shrink = jnp.exp2((old - new) * factor)
            top[0:1] = new
            top[1:2] = top[1:2] * shrink + jnp.sum(p, axis=0, keepdims=True)
            acc[...] = acc[...] * shrink + dot(vt[:, spot], p.astype(BF16), ((1,), (0,)))

        for_tiles(
            tile_plan(first, first + half - 1, starts, ends, bk),
            lambda j: visit(j, True),
            lambda j: visit(j, False),
        )
        ot[i] = acc[...] / top[1:2]
        lse_out[i] = top[0:1] * factor + jnp.log2(top[1:2])
        return 0

    lax.fori_loop(0, 2 * n_q, one, 0)
    for k in range(n_q):
        joined = jnp.concatenate([ot[2 * k], ot[2 * k + 1]], axis=0).T
        of_out[k] = joined
        o_out[k][...] = joined.astype(BF16)


def attn_fwd(kvs, qs, place, starts, ends, bk=512):
    rows, half, total = kvs[0].shape[0], qs[0].shape[0], starts.shape[0]
    n_kv, n_q = len(kvs), len(qs)
    outs = pl.pallas_call(
        functools.partial(fwd_kernel, n_kv, n_q, bk),
        in_specs=[SM, SM, SM, VM, VM] + [ANY] * n_kv + [VM] * n_q,
        out_specs=[VM] * (n_q + 3),
        out_shape=[jax.ShapeDtypeStruct((half, 128), BF16)] * n_q
        + [
            jax.ShapeDtypeStruct((n_q, half, 128), F32),
            jax.ShapeDtypeStruct((2 * n_q, 1, half), F32),
            jax.ShapeDtypeStruct((total, 128), BF16),
        ],
        scratch_shapes=[
            pltpu.VMEM((HEAD_DIM, total), BF16),
            pltpu.VMEM((2 * n_q, half, 128), BF16),
            pltpu.VMEM((HEAD_DIM, half), F32),
            pltpu.VMEM((8, half), F32),
            pltpu.VMEM((2 * n_q, HEAD_DIM, half), F32),
            pltpu.SemaphoreType.DMA((n_kv,)),
        ],
        compiler_params=PARAMS,
        name="attend",
    )(place, starts, ends, starts.reshape(-1, 1, half), ends.reshape(-1, 1, half), *kvs, *qs)
    return outs[:n_q], outs[n_q], outs[n_q + 1], outs[n_q + 2]


def bwd_kernel(n_q, bk, place, starts, ends, begin_rows, stop_rows, kv_hbm, lse, of, *refs):
    q_in, g_in, refs = refs[:n_q], refs[n_q : 2 * n_q], refs[2 * n_q :]
    dq_out, dkv_out, theirs, refs = refs[:n_q], refs[n_q : 2 * n_q], refs[2 * n_q], refs[2 * n_q + 1 :]
    kv, kt, qz, gz, delta, dkv, dqt_all, acc, sems = refs
    half = q_in[0].shape[0]
    rows = 2 * half
    copies = load_all([(kv_hbm, kv)], sems)
    for k in range(n_q):
        q, g = q_in[k][...], g_in[k][...]
        qz[2 * k] = low_half(q)
        qz[2 * k + 1] = low_half(swap_halves(q))
        gz[2 * k] = high_half(swap_halves(g))
        gz[2 * k + 1] = high_half(g)
        prod = (g.astype(F32) * of[k]).T
        delta[2 * k] = jnp.sum(prod[:HEAD_DIM], axis=0, keepdims=True)
        delta[2 * k + 1] = jnp.sum(prod[HEAD_DIM:], axis=0, keepdims=True)
    copies[0].wait()

    def turn(j, _):
        spot = pl.ds(pl.multiple_of(j * 256, 256), 256)
        kt[:, spot] = kv[spot, :].T[:HEAD_DIM]
        dkv[spot, :] = jnp.zeros((256, 128), F32)
        return 0

    lax.fori_loop(0, kv.shape[0] // 256, turn, 0)
    factor = SCORE * LOG2E

    def one(i, _):
        first = place[i // 2] * rows + (i % 2) * half
        query, grad, lse_row, delta_row = qz[i], gz[i], lse[i], delta[i]
        acc[...] = jnp.zeros_like(acc)
        slab = first // half

        def visit(j, mask):
            spot = pl.ds(pl.multiple_of(j * bk, bk), bk)
            block = kv[spot, :]
            st = dot(block, query, ((1,), (1,)))
            p = jnp.exp2(st * factor - lse_row)
            if mask:
                at = j * bk + lax.broadcasted_iota(jnp.int32, st.shape, 0)
                p = jnp.where((at >= begin_rows[slab]) & (at < stop_rows[slab]), p, 0.0)
            dp = dot(block, grad, ((1,), (1,)))
            ds = (p * (dp - delta_row)).astype(BF16)
            dkv[spot, :] += dot(ds, query, ((1,), (0,))) + dot(p.astype(BF16), grad, ((1,), (0,)))
            acc[...] += dot(kt[:, spot], ds, ((1,), (0,)))

        for_tiles(
            tile_plan(first, first + half - 1, starts, ends, bk),
            lambda j: visit(j, True),
            lambda j: visit(j, False),
        )
        dqt_all[i] = acc[...] * SCORE
        return 0

    lax.fori_loop(0, 2 * n_q, one, 0)
    for k in range(n_q):
        joined = jnp.concatenate([dqt_all[2 * k], dqt_all[2 * k + 1]], axis=0).T
        dq_out[k][...] = joined.astype(BF16)
    for k in range(n_q):
        dkv_out[k][...] = dkv[pl.ds(pl.multiple_of(place[k] * rows, 128), rows), :]
        other = pl.ds(pl.multiple_of(place[n_q + k] * rows, 128), rows)
        theirs[k * rows : (k + 1) * rows, :] = dkv[other, :].astype(BF16)


def attn_bwd(kv, qs, gs, of, lse, place, starts, ends, bk=512):
    half, total = qs[0].shape[0], starts.shape[0]
    n_q = len(qs)
    outs = pl.pallas_call(
        functools.partial(bwd_kernel, n_q, bk),
        in_specs=[SM, SM, SM, VM, VM, ANY] + [VM] * (2 + 2 * n_q),
        out_specs=[VM] * (2 * n_q + 1),
        out_shape=[jax.ShapeDtypeStruct((half, 128), BF16)] * n_q
        + [jax.ShapeDtypeStruct((2 * half, 128), F32)] * n_q
        + [jax.ShapeDtypeStruct((2 * half * n_q, 128), BF16)],
        scratch_shapes=[
            pltpu.VMEM((total, 128), BF16),
            pltpu.VMEM((HEAD_DIM, total), BF16),
            pltpu.VMEM((2 * n_q, half, 128), BF16),
            pltpu.VMEM((2 * n_q, half, 128), BF16),
            pltpu.VMEM((2 * n_q, 1, half), F32),
            pltpu.VMEM((total, 128), F32),
            pltpu.VMEM((2 * n_q, HEAD_DIM, half), F32),
            pltpu.VMEM((HEAD_DIM, half), F32),
            pltpu.SemaphoreType.DMA((1,)),
        ],
        compiler_params=PARAMS,
        name="attend_back",
    )(place, starts, ends, starts.reshape(-1, 1, half), ends.reshape(-1, 1, half), kv, lse, of, *qs, *gs)
    return outs[:n_q], outs[n_q : 2 * n_q], outs[2 * n_q]


def place_of(axes):
    return jnp.stack([jnp.asarray(a, jnp.int32) for a in axes])


def stats(x):
    average = jnp.mean(x, axis=-1, keepdims=True)
    centered = x - average
    variance = jnp.mean(centered * centered, axis=-1, keepdims=True)
    return centered, lax.rsqrt(variance + 1e-05)


def norm_back(grad, xhat, rate, gain):
    scaled = grad * gain
    return rate * (
        scaled
        - jnp.mean(scaled, axis=-1, keepdims=True)
        - xhat * jnp.mean(scaled * xhat, axis=-1, keepdims=True)
    )


def column_sums(grad, xhat):
    return jnp.concatenate(
        [jnp.sum(grad * xhat, axis=0, keepdims=True), jnp.sum(grad, axis=0, keepdims=True)], axis=0
    )


def cost(flops, size):
    return pl.CostEstimate(flops=flops, bytes_accessed=size, transcendentals=0)


def shape_of(*dims, dtype=BF16):
    return jax.ShapeDtypeStruct(dims, dtype)


def project_kernel(n_z, here, x, gain, shift, weight, normed_out, *refs):
    kv_out, q_out = refs[:n_z], refs[n_z : 2 * n_z]
    kv_all, q_all, q_flat, sems = refs[2 * n_z :]
    rows = x.shape[0]
    half, tile = rows // 2, rows // 2
    for t in range(rows // tile):
        spot = slice(t * tile, (t + 1) * tile)
        centered, rate = stats(x[spot, :].astype(F32))
        normed = (centered * rate * gain[...] + shift[...]).astype(BF16)
        normed_out[spot, :] = normed
        q, k, v = [dot(normed, weight[part], ((1,), (0,))).astype(BF16) for part in range(3)]
        q_flat[spot, :] = q
        for h in range(n_z):
            cut = slice(h * HEAD_DIM, (h + 1) * HEAD_DIM)
            kv_all[h, spot, :] = jnp.concatenate([k[:, cut], v[:, cut]], axis=1)
    for h in range(n_z):
        cut = slice(h * HEAD_DIM, (h + 1) * HEAD_DIM)
        q_all[h] = jnp.concatenate([q_flat[:half, cut], q_flat[half:, cut]], axis=1)
    pairs = []
    for k in range(n_z):
        head = lax.rem(here[0] + k, n_z)
        pairs += [(kv_all.at[head], kv_out[k]), (q_all.at[head], q_out[k])]
    for c in load_all(pairs, sems):
        c.wait()


def project(n_z, here, x, gain, shift, weight):
    rows, width = x.shape
    half = rows // 2
    outs = pl.pallas_call(
        functools.partial(project_kernel, n_z),
        in_specs=[SM, VM, VM, VM, VM],
        out_specs=[VM] + [ANY] * (2 * n_z),
        out_shape=[shape_of(rows, width)]
        + [shape_of(rows, 128)] * n_z
        + [shape_of(half, 128)] * n_z,
        scratch_shapes=[
            pltpu.VMEM((n_z, rows, 128), BF16),
            pltpu.VMEM((n_z, half, 128), BF16),
            pltpu.VMEM((rows, n_z * HEAD_DIM), BF16),
            pltpu.SemaphoreType.DMA((2 * n_z,)),
        ],
        compiler_params=PARAMS,
        cost_estimate=cost(2 * rows * width * 3 * weight.shape[2], 6 * 2**20),
        name="project",
    )(here, x, gain, shift, weight)
    return outs[0], outs[1 : 1 + n_z], outs[1 + n_z :]


def spread_kernel(n_z, n_t, here, *refs):
    o_in, (o_all, o_own), sends = refs[:n_z], refs[n_z : n_z + 2], refs[n_z + 2 : n_z + 1 + n_t]
    by_head, sems = refs[n_z + 1 + n_t :]
    half = o_in[0].shape[0]
    quarter = o_own.shape[0]
    copies = load_all(
        [(o_in[k], by_head.at[lax.rem(here[0] + k, n_z)]) for k in range(n_z)], sems
    )
    for c in copies:
        c.wait()
    o_all[:half, :] = jnp.concatenate([by_head[h][:, :HEAD_DIM] for h in range(n_z)], axis=1)
    o_all[half:, :] = jnp.concatenate([by_head[h][:, HEAD_DIM:] for h in range(n_z)], axis=1)
    for m, out in enumerate([o_own] + list(sends)):
        first = pl.multiple_of((here[1] ^ m) * quarter, 16)
        out[...] = o_all[pl.ds(first, quarter), :]


def spread(n_z, n_t, here, o_slots):
    half = o_slots[0].shape[0]
    rows, width = 2 * half, n_z * HEAD_DIM
    outs = pl.pallas_call(
        functools.partial(spread_kernel, n_z, n_t),
        in_specs=[SM] + [ANY] * n_z,
        out_specs=[VM] * (1 + n_t),
        out_shape=[shape_of(rows, width)] + [shape_of(rows // n_t, width)] * n_t,
        scratch_shapes=[pltpu.VMEM((n_z, half, 128), BF16), pltpu.SemaphoreType.DMA((n_z,))],
        compiler_params=PARAMS,
        cost_estimate=cost(0, 2**20),
        name="spread",
    )(here, *o_slots)
    return outs[0], outs[1:]


def mix_kernel(n_t, here, x, gain, shift, *refs):
    parts, weights, (after_out, normed_out) = refs[:n_t], refs[n_t : 2 * n_t], refs[2 * n_t :]
    quarter = parts[0].shape[0]
    mixed = sum(dot(parts[m][...], weights[m][...], ((1,), (0,))) for m in range(n_t))
    first = pl.multiple_of(here[1] * quarter, 16)
    after = x[pl.ds(first, quarter), :].astype(F32) + mixed
    after_out[...] = after
    centered, rate = stats(after)
    normed_out[...] = (centered * rate * gain[...] + shift[...]).astype(BF16)


def mix(n_t, here, x, gain, shift, parts, weights):
    quarter, width = parts[0].shape[0], x.shape[1]
    return pl.pallas_call(
        functools.partial(mix_kernel, n_t),
        in_specs=[SM] + [VM] * (3 + 2 * n_t),
        out_specs=[VM] * 2,
        out_shape=[shape_of(quarter, width, dtype=F32), shape_of(quarter, width)],
        compiler_params=PARAMS,
        cost_estimate=cost(2 * quarter * width * width, 6 * 2**20),
        name="mix",
    )(here, x, gain, shift, *parts, *weights)


def gelu_pair(u):
    c = math.sqrt(2.0 / math.pi)
    square = u * u
    t = jnp.tanh(c * (u + 0.044715 * square * u))
    slope = 0.5 * (1.0 + t) + 0.5 * u * (1.0 - t * t) * c * (1.0 + 3 * 0.044715 * square)
    return 0.5 * u * (1.0 + t), slope


def hidden_kernel(n_t, here, cot, up, down, *refs):
    normed, refs = refs[:n_t], refs[n_t:]
    act_out, pre_out, normed_out, cot_out, own = refs[:5]
    sends = refs[5 : 4 + n_t]
    quarter = normed[0].shape[0]
    for m in range(n_t):
        spot = slice(m * quarter, (m + 1) * quarter)
        normed_out[spot, :] = normed[m][...]
        first = pl.multiple_of((here[1] ^ m) * quarter, 16)
        cot_out[spot, :] = cot[pl.ds(first, quarter), :]
    tile = 256

    def one(j, _):
        cut = pl.ds(pl.multiple_of(j * tile, tile), tile)
        act, slope = gelu_pair(dot(normed_out[...], up[:, cut], ((1,), (0,))))
        act_out[:, cut] = act.astype(BF16)
        grad = dot(cot_out[...], down[cut, :], ((1,), (1,)))
        pre_out[:, cut] = (grad * slope).astype(BF16)
        return 0

    lax.fori_loop(0, up.shape[1] // tile, one, 0)
    for m, out in enumerate([own] + list(sends)):
        spot = slice(m * quarter, (m + 1) * quarter)
        out[...] = dot(pre_out[spot, :], up[...], ((1,), (1,))).astype(out.dtype)


def hidden_layer(n_t, here, cot, up, down, normed):
    quarter, width = normed[0].shape
    rows, units = n_t * quarter, up.shape[1]
    outs = pl.pallas_call(
        functools.partial(hidden_kernel, n_t),
        in_specs=[SM] + [VM] * (3 + n_t),
        out_specs=[VM] * (4 + n_t),
        out_shape=[
            shape_of(rows, units),
            shape_of(rows, units),
            shape_of(rows, width),
            shape_of(rows, width),
            shape_of(quarter, width, dtype=F32),
        ]
        + [shape_of(quarter, width)] * (n_t - 1),
        compiler_params=PARAMS,
        cost_estimate=cost(6 * rows * width * units, 16 * 2**20),
        name="hidden_layer",
    )(here, cot, up, down, *normed)
    return outs[0], outs[1], outs[2], outs[3], outs[4:]


def branch_kernel(n_t, act, down, own, *sends):
    quarter = own.shape[0]
    for m, out in enumerate([own] + list(sends)):
        spot = slice(m * quarter, (m + 1) * quarter)
        out[...] = dot(act[spot, :], down[...], ((1,), (0,))).astype(out.dtype)


def branch_parts(n_t, act, down):
    rows, width = act.shape[0], down.shape[1]
    return pl.pallas_call(
        functools.partial(branch_kernel, n_t),
        in_specs=[VM] * 2,
        out_specs=[VM] * n_t,
        out_shape=[shape_of(rows // n_t, width, dtype=F32)]
        + [shape_of(rows // n_t, width)] * (n_t - 1),
        compiler_params=PARAMS,
        cost_estimate=cost(2 * rows * width * act.shape[1], 6 * 2**20),
        name="branch",
    )(act, down)


def middle_kernel(n_t, here, after, cot, gain, *refs):
    parts, weights, refs = refs[:n_t], refs[n_t : 2 * n_t], refs[2 * n_t :]
    middle_out, mixed_out, sums_out = refs[:3]
    grads = refs[3:]
    quarter = after.shape[0]
    grad = sum(parts[m][...].astype(F32) for m in range(n_t))
    centered, rate = stats(after[...])
    xhat = centered * rate
    sums_out[...] = column_sums(grad, xhat)
    first = pl.multiple_of(here[1] * quarter, 16)
    upstream = cot[pl.ds(first, quarter), :].astype(F32)
    middle = upstream + norm_back(grad, xhat, rate, gain[...])
    middle_out[...] = middle
    mixed = middle.astype(BF16)
    mixed_out[...] = mixed
    for m in range(n_t):
        grads[m][...] = dot(mixed, weights[m][...], ((1,), (1,))).astype(BF16)


def middle_back(n_t, here, after, cot, gain, parts, weights):
    quarter, width = after.shape
    share = weights[0].shape[0]
    outs = pl.pallas_call(
        functools.partial(middle_kernel, n_t),
        in_specs=[SM] + [VM] * (3 + 2 * n_t),
        out_specs=[VM] * (3 + n_t),
        out_shape=[
            shape_of(quarter, width, dtype=F32),
            shape_of(quarter, width),
            shape_of(2, width, dtype=F32),
        ]
        + [shape_of(quarter, share)] * n_t,
        compiler_params=PARAMS,
        cost_estimate=cost(2 * quarter * width * width, 8 * 2**20),
        name="middle_back",
    )(here, after, cot, gain, *parts, *weights)
    return outs[0], outs[1], outs[2], outs[3:]


def gather_kernel(n_z, n_t, here, *refs):
    g_in, g_out, (flat, packed, sems) = refs[:n_t], refs[n_t : n_t + n_z], refs[n_t + n_z :]
    quarter = g_in[0].shape[0]
    half = flat.shape[0] // 2
    for m in range(n_t):
        first = pl.multiple_of((here[1] ^ m) * quarter, 16)
        flat[pl.ds(first, quarter), :] = g_in[m][...]
    for h in range(n_z):
        cut = slice(h * HEAD_DIM, (h + 1) * HEAD_DIM)
        packed[h] = jnp.concatenate([flat[:half, cut], flat[half:, cut]], axis=1)
    copies = load_all(
        [(packed.at[lax.rem(here[0] + k, n_z)], g_out[k]) for k in range(n_z)], sems
    )
    for c in copies:
        c.wait()


def gather_grads(n_z, n_t, here, parts):
    quarter, width = parts[0].shape
    rows = n_t * quarter
    return pl.pallas_call(
        functools.partial(gather_kernel, n_z, n_t),
        in_specs=[SM] + [VM] * n_t,
        out_specs=[ANY] * n_z,
        out_shape=[shape_of(rows // 2, 128)] * n_z,
        scratch_shapes=[
            pltpu.VMEM((rows, width), BF16),
            pltpu.VMEM((n_z, rows // 2, 128), BF16),
            pltpu.SemaphoreType.DMA((n_z,)),
        ],
        compiler_params=PARAMS,
        cost_estimate=cost(0, 2**20),
        name="gather_grads",
    )(here, *parts)


def join_kernel(n_z, theirs, *refs):
    mine, outs = refs[:n_z], refs[n_z:]
    rows = mine[0].shape[0]
    lane = lax.broadcasted_iota(jnp.int32, (rows, 128), 1)
    factor = jnp.where(lane < HEAD_DIM, SCORE, 1.0)
    for k in range(n_z):
        total = mine[k][...] + theirs[k * rows : (k + 1) * rows, :].astype(F32)
        outs[k][...] = (total * factor).astype(BF16)


def join(n_z, mine, theirs):
    rows = mine[0].shape[0]
    return pl.pallas_call(
        functools.partial(join_kernel, n_z),
        in_specs=[VM] * (1 + n_z),
        out_specs=[VM] * n_z,
        out_shape=[shape_of(rows, 128)] * n_z,
        compiler_params=PARAMS,
        cost_estimate=cost(0, 3 * 2**20),
        name="join",
    )(theirs, *mine)


def unproject_kernel(n_z, n_t, here, weight, *refs):
    kv_in, q_in, (flat, own), refs = (
        refs[:n_z],
        refs[n_z : 2 * n_z],
        refs[2 * n_z : 2 * n_z + 2],
        refs[2 * n_z + 2 :],
    )
    sends, (kv_all, q_all, sems) = refs[: n_t - 1], refs[n_t - 1 :]
    half = q_all.shape[1]
    width = n_z * HEAD_DIM
    quarter = own.shape[0]
    pairs = []
    for k in range(n_z):
        head = lax.rem(here[0] + k, n_z)
        pairs += [(kv_in[k], kv_all.at[head]), (q_in[k], q_all.at[head])]
    for c in load_all(pairs, sems):
        c.wait()
    heads = range(n_z)
    flat[:half, :width] = jnp.concatenate([q_all[h][:, :HEAD_DIM] for h in heads], axis=1)
    flat[half:, :width] = jnp.concatenate([q_all[h][:, HEAD_DIM:] for h in heads], axis=1)
    flat[:, width : 2 * width] = jnp.concatenate([kv_all[h][:, :HEAD_DIM] for h in heads], axis=1)
    flat[:, 2 * width :] = jnp.concatenate([kv_all[h][:, HEAD_DIM:] for h in heads], axis=1)
    for m, out in enumerate([own] + list(sends)):
        first = pl.multiple_of((here[1] ^ m) * quarter, 16)
        grad = flat[pl.ds(first, quarter), :]
        total = sum(
            dot(grad[:, c * width : (c + 1) * width], weight[c], ((1,), (1,))) for c in range(3)
        )
        out[...] = total.astype(out.dtype)


def unproject(n_z, n_t, here, weight, kv_slots, q_slots):
    rows, half = kv_slots[0].shape[0], q_slots[0].shape[0]
    width = weight.shape[1]
    outs = pl.pallas_call(
        functools.partial(unproject_kernel, n_z, n_t),
        in_specs=[SM, VM] + [ANY] * (2 * n_z),
        out_specs=[VM] * (1 + n_t),
        out_shape=[
            shape_of(rows, 3 * n_z * HEAD_DIM),
            shape_of(rows // n_t, width, dtype=F32),
        ]
        + [shape_of(rows // n_t, width)] * (n_t - 1),
        scratch_shapes=[
            pltpu.VMEM((n_z, rows, 128), BF16),
            pltpu.VMEM((n_z, half, 128), BF16),
            pltpu.SemaphoreType.DMA((2 * n_z,)),
        ],
        compiler_params=PARAMS,
        cost_estimate=cost(2 * rows * width * 3 * n_z * HEAD_DIM, 7 * 2**20),
        name="unproject",
    )(here, weight, *kv_slots, *q_slots)
    return outs[0], outs[1:]


def last_kernel(n_t, here, x, middle, gain, *refs):
    parts, (grad_out, sums_out) = refs[:n_t], refs[n_t:]
    quarter = middle.shape[0]
    grad = sum(parts[m][...].astype(F32) for m in range(n_t))
    first = pl.multiple_of(here[1] * quarter, 16)
    centered, rate = stats(x[pl.ds(first, quarter), :].astype(F32))
    xhat = centered * rate
    sums_out[...] = column_sums(grad, xhat)
    grad_out[...] = (middle[...] + norm_back(grad, xhat, rate, gain[...])).astype(BF16)


def last_back(n_t, here, x, middle, gain, parts):
    quarter, width = middle.shape
    return pl.pallas_call(
        functools.partial(last_kernel, n_t),
        in_specs=[SM] + [VM] * (3 + n_t),
        out_specs=[VM] * 2,
        out_shape=[shape_of(quarter, width), shape_of(2, width, dtype=F32)],
        compiler_params=PARAMS,
        cost_estimate=cost(0, 6 * 2**20),
        name="last_back",
    )(here, x, middle, gain, *parts)


def lay_kernel(n_t, here, *refs):
    parts, out = refs[:n_t], refs[n_t]
    quarter = parts[0].shape[0]
    for m in range(n_t):
        first = pl.multiple_of((here[1] ^ m) * quarter, 16)
        out[pl.ds(first, quarter), :] = parts[m][...].astype(out.dtype)


def lay(n_t, here, parts, dtype):
    quarter, width = parts[0].shape
    return pl.pallas_call(
        functools.partial(lay_kernel, n_t),
        in_specs=[SM] + [VM] * n_t,
        out_specs=VM,
        out_shape=shape_of(n_t * quarter, width, dtype=dtype),
        compiler_params=PARAMS,
        cost_estimate=cost(0, 5 * 2**20),
        name="lay",
    )(here, *parts)


def stack_lanes(block):
    return [block[:, i * 128 : (i + 1) * 128] for i in range(block.shape[1] // 128)]


def early_kernel(n_z, n_t, here, act, pre, normed, cot, attended, *refs):
    mixed, (mine, theirs) = refs[:n_t], refs[n_t:]
    z, i, c = here[0], here[1], here[2]
    units = act.shape[1]
    quarter = mixed[0].shape[0]
    width = normed.shape[1]
    for out, side in ((theirs, 1 - c), (mine, c)):
        for k in range(n_z):
            owner = lax.rem(z + k, n_z) * 2 + side
            cut = pl.ds(pl.multiple_of(owner * 128, 128), 128)
            out[k, :units, :] = dot(act[...], cot[:, cut], ((0,), (0,))).astype(out.dtype)
            up = dot(normed[:, cut], pre[...], ((0,), (0,))).astype(out.dtype)
            for j, block in enumerate(stack_lanes(up)):
                out[k, units + j * 128 : units + (j + 1) * 128, :] = block
            outward = sum(
                dot(
                    attended[pl.ds(pl.multiple_of((i ^ m) * quarter, 16), quarter), :],
                    mixed[m][:, cut],
                    ((0,), (0,)),
                )
                for m in range(n_t)
            )
            out[k, 2 * units :, :] = outward.astype(out.dtype)


def early_grads(n_z, n_t, here, act, pre, normed, cot, attended, mixed):
    units, share = act.shape[1], attended.shape[1]
    depth = 2 * units + share
    return pl.pallas_call(
        functools.partial(early_kernel, n_z, n_t),
        in_specs=[SM] + [VM] * (5 + n_t),
        out_specs=[VM] * 2,
        out_shape=[shape_of(n_z, depth, 128, dtype=F32), shape_of(n_z, depth, 128)],
        compiler_params=PARAMS,
        cost_estimate=cost(2 * act.shape[0] * depth * normed.shape[1], 18 * 2**20),
        name="early_grads",
    )(here, act, pre, normed, cot, attended, *mixed)


def late_kernel(n_z, here, normed, grad, mine, theirs):
    z, c = here[0], here[2]
    for out, side in ((theirs, 1 - c), (mine, c)):
        for k in range(n_z):
            owner = lax.rem(z + k, n_z) * 2 + side
            cut = pl.ds(pl.multiple_of(owner * 128, 128), 128)
            block = dot(normed[:, cut], grad[...], ((0,), (0,))).astype(out.dtype)
            for j, piece in enumerate(stack_lanes(block)):
                out[k, j * 128 : (j + 1) * 128, :] = piece


def late_grads(n_z, here, normed, grad):
    depth = grad.shape[1]
    return pl.pallas_call(
        functools.partial(late_kernel, n_z),
        in_specs=[SM] + [VM] * 2,
        out_specs=[VM] * 2,
        out_shape=[shape_of(n_z, depth, 128, dtype=F32), shape_of(n_z, depth, 128)],
        compiler_params=PARAMS,
        cost_estimate=cost(2 * grad.shape[0] * depth * normed.shape[1], 8 * 2**20),
        name="late_grads",
    )(here, normed, grad)


def fold_kernel(mine, theirs, own, *sends):
    for k, out in enumerate([own] + list(sends)):
        out[...] = (mine[k] + theirs[k].astype(F32)).astype(out.dtype)


def fold(mine, theirs):
    n_z, depth, _ = mine.shape
    return pl.pallas_call(
        fold_kernel,
        in_specs=[VM] * 2,
        out_specs=[VM] * n_z,
        out_shape=[shape_of(depth, 128, dtype=F32)] + [shape_of(depth, 128)] * (n_z - 1),
        compiler_params=PARAMS,
        cost_estimate=cost(0, 8 * 2**20),
        name="fold",
    )(mine, theirs)


def finish_early_kernel(n_z, *refs):
    parts, (down_out, up_out, outward_out) = refs[:n_z], refs[n_z:]
    total = parts[0][...]
    for part in parts[1:]:
        total = total + part[...].astype(F32)
    units = down_out.shape[0]
    down_out[...] = total[:units]
    for j in range(units // 128):
        up_out[:, j * 128 : (j + 1) * 128] = total[units + j * 128 : units + (j + 1) * 128]
    outward_out[...] = total[2 * units :]


def finish_early(n_z, units, share, parts):
    return pl.pallas_call(
        functools.partial(finish_early_kernel, n_z),
        in_specs=[VM] * n_z,
        out_specs=[VM] * 3,
        out_shape=[
            shape_of(units, 128, dtype=F32),
            shape_of(128, units, dtype=F32),
            shape_of(share, 128, dtype=F32),
        ],
        compiler_params=PARAMS,
        cost_estimate=cost(0, 5 * 2**20),
        name="finish_early",
    )(*parts)


def finish_late_kernel(n_z, *refs):
    parts, out = refs[:n_z], refs[n_z]
    total = parts[0][...]
    for part in parts[1:]:
        total = total + part[...].astype(F32)
    per = out.shape[2] // 128
    for c in range(3):
        for j in range(per):
            at = (c * per + j) * 128
            out[c, :, j * 128 : (j + 1) * 128] = total[at : at + 128]


def finish_late(n_z, share, parts):
    return pl.pallas_call(
        functools.partial(finish_late_kernel, n_z),
        in_specs=[VM] * n_z,
        out_specs=VM,
        out_shape=shape_of(3, 128, share, dtype=F32),
        compiler_params=PARAMS,
        cost_estimate=cost(0, 2 * 2**20),
        name="finish_late",
    )(*parts)


def body(
    n_seq,
    n_tp,
    tokens,
    scene_index,
    inward_weight,
    outward_weight,
    up_weight,
    down_weight,
    norm_gains,
    norm_shifts,
    cotangent,
):
    n_z, total = n_seq // 2, scene_index.shape[0]
    seq, tp = lax.axis_index("seq"), lax.axis_index("tp")
    z, c = seq // 2, seq % 2
    here = place_of([z, tp, c])

    def along(x, k):
        return lax.ppermute(
            x, "seq", [(a * 2 + b, (a + k) % n_z * 2 + b) for a in range(n_z) for b in range(2)]
        )

    def across(x):
        return lax.ppermute(x, "seq", [(a, a ^ 1) for a in range(n_seq)])

    def over(x, m):
        return lax.ppermute(x, "tp", [(a, a ^ m) for a in range(n_tp)])

    def ring(slots):
        return [slots[0]] + [along(slots[k], k) for k in range(1, n_z)]

    def square(slots):
        return [slots[0]] + [over(slots[m], m) for m in range(1, n_tp)]

    def square_same(x):
        return [x] + [over(x, m) for m in range(1, n_tp)]

    place = place_of([(z + n_z - k) % n_z * 2 + (c ^ g) for g in range(2) for k in range(n_z)])
    at = lax.iota(jnp.int32, total)
    edge = jnp.concatenate(
        [jnp.ones((1,), jnp.bool_), scene_index[1:] != scene_index[:-1]]
    )
    starts = lax.cummax(jnp.where(edge, at, 0))
    closing = jnp.concatenate([edge[1:], jnp.ones((1,), jnp.bool_)])
    ends = lax.cummin(jnp.where(closing, at + 1, total), reverse=True)

    gains, shifts = norm_gains[0], norm_shifts[0]
    inward, outward, up, down = inward_weight[0], outward_weight[0], up_weight[0], down_weight[0]
    normed, kv_send, q_send = project(n_z, here, tokens, gains[0:1], shifts[0:1], inward)
    kv_mine = ring(kv_send)
    q_slots = ring(q_send)
    kv_other = [across(block) for block in kv_mine]
    outward_all = square_same(outward)
    o_send, o_full, lse, kv_full = attn_fwd(kv_mine + kv_other, q_slots, place, starts, ends, 1024)
    attended, parts = spread(n_z, n_tp, here, ring_back(ring, o_send, n_z, along))
    after, normed_two = mix(
        n_tp, here, tokens, gains[1:2], shifts[1:2], square(parts), outward_all
    )
    act, pre, normed_slots, cot_slots, grad_parts = hidden_layer(
        n_tp, here, cotangent, up, down, square_same(normed_two)
    )
    middle, mixed, sums_two, grad_slots = middle_back(
        n_tp, here, after, cotangent, gains[1:2], square(grad_parts), outward_all
    )
    g_send = gather_grads(n_z, n_tp, here, square(grad_slots))
    dq, dkv_mine, dkv_theirs = attn_bwd(
        kv_full, q_slots, ring(g_send), o_full, lse, place, starts, ends, 1024
    )
    dkv = join(n_z, dkv_mine, across(dkv_theirs))

    branch = square(branch_parts(n_tp, act, down))
    out_own = (after + sum(part.astype(F32) for part in branch)).astype(BF16)
    activations = lay(n_tp, here, square_same(out_own), BF16)
    mine, theirs = early_grads(
        n_z, n_tp, here, act, pre, normed_slots, cot_slots, attended, square_same(mixed)
    )
    units, share = up.shape[1], outward.shape[0]
    down_grad, up_grad, outward_grad = finish_early(
        n_z, units, share, ring(fold(mine, across(theirs)))
    )

    flat, back_parts = unproject(
        n_z,
        n_tp,
        here,
        inward,
        ring_back(ring, dkv, n_z, along),
        ring_back(ring, dq, n_z, along),
    )
    token_own, sums_one = last_back(n_tp, here, tokens, middle, gains[0:1], square(back_parts))
    token_grad = lay(n_tp, here, square_same(token_own), F32)
    mine, theirs = late_grads(n_z, here, normed, flat)
    inward_grad = finish_late(n_z, share, ring(fold(mine, across(theirs))))

    sums = jnp.concatenate([sums_one, sums_two], axis=0)
    m = 1
    while m < n_tp:
        sums = sums + over(sums, m)
        m *= 2
    sums = sums + across(sums)
    sums = sums + sum(along(sums, k) for k in range(1, n_z))
    width = tokens.shape[1] // n_seq
    sums = lax.dynamic_slice_in_dim(sums, seq * width, width, axis=1)
    gain_grad = jnp.stack([sums[0], sums[2]])
    shift_grad = jnp.stack([sums[1], sums[3]])
    return (
        activations,
        token_grad,
        inward_grad[None],
        outward_grad[None],
        up_grad[None],
        down_grad[None],
        gain_grad[None],
        shift_grad[None],
    )


def ring_back(ring, slots, n_z, along):
    return [slots[0]] + [along(slots[k], n_z - k) for k in range(1, n_z)]


def layer_norm(hidden, gain_row, shift_row):
    average = jnp.mean(hidden, axis=-1, keepdims=True)
    centered = hidden - average
    variance = jnp.mean(centered * centered, axis=-1, keepdims=True)
    return centered * lax.rsqrt(variance + 1e-05) * gain_row + shift_row


def gelu_tanh(preactivation):
    return jax.nn.gelu(preactivation, approximate=True)


def to_heads(flat_rows):
    return flat_rows.reshape(flat_rows.shape[0], -1, HEAD_DIM)


def scenes_meet(query_scenes, key_scenes):
    return jnp.logical_and(key_scenes[0] <= query_scenes[-1], key_scenes[-1] >= query_scenes[0])


def score_rows(query_heads, key_heads, query_scenes, key_scenes):
    scores = jnp.einsum(
        "qhd,khd->hqk", query_heads, key_heads, preferred_element_type=jnp.float32
    ) * HEAD_DIM ** (-0.5)
    same_scene = (query_scenes[:, None] == key_scenes[None, :])[None]
    return (scores, same_scene)


def probabilities(scores, same_scene, normalizer):
    return jnp.where(same_scene, jnp.exp(scores - normalizer[:, :, None]), 0.0)


def key_tiles(key_all, value_all, scene_index):
    tile_rows = min(1024, key_all.shape[0])
    tile_count = key_all.shape[0] // tile_rows
    return (
        key_all.reshape(tile_count, tile_rows, -1, HEAD_DIM),
        value_all.reshape(tile_count, tile_rows, -1, HEAD_DIM),
        scene_index.reshape(tile_count, tile_rows),
    )


def log_normalizer(query_heads, query_scenes, tiled_keys):

    def log_visit_tile(running_pair, inputs_pair):
        key_heads, key_scenes = inputs_pair

        def log_compute(pair_now):
            running_max, running_sum = pair_now
            scores, same_scene = score_rows(query_heads, key_heads, query_scenes, key_scenes)
            masked = jnp.where(same_scene, scores, NEG_FILL)
            new_max = jnp.maximum(running_max, jnp.max(masked, axis=-1))
            weights = jnp.where(same_scene, jnp.exp(masked - new_max[:, :, None]), 0.0)
            return (
                new_max,
                running_sum * jnp.exp(running_max - new_max) + jnp.sum(weights, axis=-1),
            )

        return (
            lax.cond(
                scenes_meet(query_scenes, key_scenes),
                log_compute,
                lambda pair_now: pair_now,
                running_pair,
            ),
            None,
        )

    stat_shape = (query_heads.shape[1], query_heads.shape[0])
    start_pair = (jnp.full(stat_shape, NEG_FILL, jnp.float32), jnp.zeros(stat_shape, jnp.float32))
    final_pair, _ = lax.scan(log_visit_tile, start_pair, (tiled_keys[0], tiled_keys[2]))
    return final_pair[0] + jnp.log(final_pair[1])


def attend_all(query_heads, query_scenes, tiled_keys, normalizer):

    def attend_visit_tile(running_total, inputs_triple):
        key_heads, value_heads, key_scenes = inputs_triple

        def attend_compute(total_now):
            scores, same_scene = score_rows(query_heads, key_heads, query_scenes, key_scenes)
            weights = probabilities(scores, same_scene, normalizer).astype(jnp.bfloat16)
            return total_now + jnp.einsum(
                "hqk,khd->qhd", weights, value_heads, preferred_element_type=jnp.float32
            )

        return (
            lax.cond(
                scenes_meet(query_scenes, key_scenes),
                attend_compute,
                lambda total_now: total_now,
                running_total,
            ),
            None,
        )

    running_total, _ = lax.scan(
        attend_visit_tile, jnp.zeros(query_heads.shape, jnp.float32), tiled_keys
    )
    return running_total.reshape(running_total.shape[0], -1)


def score_gradients(
    query_heads,
    key_heads,
    value_heads,
    grad_heads,
    query_scenes,
    key_scenes,
    normalizer,
    delta_rows,
):
    scores, same_scene = score_rows(query_heads, key_heads, query_scenes, key_scenes)
    weights = probabilities(scores, same_scene, normalizer)
    weight_grad = jnp.einsum(
        "qhd,khd->hqk", grad_heads, value_heads, preferred_element_type=jnp.float32
    )
    score_grad = (weights * (weight_grad - delta_rows[:, :, None])).astype(jnp.bfloat16)
    return (weights.astype(jnp.bfloat16), score_grad)


def grads_by_reduce(query_heads, grad_heads, query_scenes, tiled_keys, normalizer, delta_rows):
    tile_rows = tiled_keys[0].shape[1]
    joined_width = 2 * query_heads.shape[1] * query_heads.shape[2]

    def grads_visit_tile(query_total, inputs_triple):
        key_heads, value_heads, key_scenes = inputs_triple

        def grads_compute(total_now):
            weights, score_grad = score_gradients(
                query_heads,
                key_heads,
                value_heads,
                grad_heads,
                query_scenes,
                key_scenes,
                normalizer,
                delta_rows,
            )
            total_now = total_now + jnp.einsum(
                "hqk,khd->qhd", score_grad, key_heads, preferred_element_type=jnp.float32
            )
            key_term = jnp.einsum(
                "hqk,qhd->khd", score_grad, query_heads, preferred_element_type=jnp.float32
            )
            value_term = jnp.einsum(
                "hqk,qhd->khd", weights, grad_heads, preferred_element_type=jnp.float32
            )
            joined = jnp.concatenate(
                [key_term.reshape(tile_rows, -1), value_term.reshape(tile_rows, -1)], axis=1
            )
            return (total_now, joined)

        def skipped(total_now):
            return (total_now, jnp.zeros((tile_rows, joined_width), jnp.float32))

        return lax.cond(scenes_meet(query_scenes, key_scenes), grads_compute, skipped, query_total)

    query_total, key_terms_all = lax.scan(
        grads_visit_tile, jnp.zeros(query_heads.shape, jnp.float32), tiled_keys
    )
    key_terms_all = key_terms_all.reshape(-1, key_terms_all.shape[-1])
    summed = lax.psum_scatter(key_terms_all, "seq", scatter_dimension=0, tiled=True)
    half_width = summed.shape[1] // 2
    return (
        query_total.reshape(query_total.shape[0], -1),
        summed[:, :half_width],
        summed[:, half_width:],
    )


def generic_body(
    tokens,
    scene_index,
    inward_weight,
    outward_weight,
    up_weight,
    down_weight,
    norm_gains,
    norm_shifts,
    cotangent,
):
    local_rows = tokens.shape[0]
    score_factor = HEAD_DIM ** (-0.5)
    query_scenes = lax.dynamic_slice_in_dim(
        scene_index, lax.axis_index("seq") * local_rows, local_rows
    )
    hidden = tokens.astype(jnp.float32)
    layer_number = 0
    gain_pair = norm_gains[layer_number]
    shift_pair = norm_shifts[layer_number]
    normed = layer_norm(hidden, gain_pair[0], shift_pair[0]).astype(jnp.bfloat16)
    projected = jnp.einsum(
        "td,cde->tce", normed, inward_weight[layer_number], preferred_element_type=jnp.float32
    ).astype(jnp.bfloat16)
    queries = projected[:, 0]
    key_local = projected[:, 1]
    value_local = projected[:, 2]
    key_all = lax.all_gather(key_local, "seq", axis=0, tiled=True)
    value_all = lax.all_gather(value_local, "seq", axis=0, tiled=True)
    tiled_keys = key_tiles(key_all, value_all, scene_index)
    query_heads = to_heads(queries)
    normalizer = log_normalizer(query_heads, query_scenes, tiled_keys)
    attended = attend_all(query_heads, query_scenes, tiled_keys, normalizer)
    attended_low = attended.astype(jnp.bfloat16)
    mixed_sum = lax.psum(
        jnp.dot(attended_low, outward_weight[layer_number], preferred_element_type=jnp.float32),
        "tp",
    )
    after_attention = hidden + mixed_sum
    normed_two = layer_norm(after_attention, gain_pair[1], shift_pair[1]).astype(jnp.bfloat16)
    preactivation = jnp.dot(normed_two, up_weight[layer_number], preferred_element_type=jnp.float32)
    activated = gelu_tanh(preactivation).astype(jnp.bfloat16)
    branch = lax.psum(
        jnp.dot(activated, down_weight[layer_number], preferred_element_type=jnp.float32), "tp"
    )
    kept_layers = [
        (
            hidden,
            after_attention,
            queries,
            key_local,
            value_local,
            tiled_keys,
            normalizer,
            attended,
            attended_low,
            preactivation,
            activated,
        )
    ]
    hidden = after_attention + branch
    upstream = cotangent.astype(jnp.float32)
    layer_grads = [None] * LAYERS
    for layer_number in reversed(range(LAYERS)):
        (
            hidden_in,
            after_attention,
            queries,
            key_local,
            value_local,
            tiled_keys,
            normalizer,
            attended,
            attended_low,
            preactivation,
            activated,
        ) = kept_layers[layer_number]
        gain_pair = norm_gains[layer_number]
        shift_pair = norm_shifts[layer_number]
        branch_grad = upstream.astype(jnp.bfloat16)
        down_grad = jnp.einsum(
            "tf,td->fd", activated, branch_grad, preferred_element_type=jnp.float32
        )
        act_grad = jnp.einsum(
            "td,fd->tf", branch_grad, down_weight[layer_number], preferred_element_type=jnp.float32
        )
        _, gelu_pull = jax.vjp(gelu_tanh, preactivation)
        preactivation_grad = gelu_pull(act_grad)[0].astype(jnp.bfloat16)
        normed_two_f, norm_pull_two = jax.vjp(
            layer_norm, after_attention, gain_pair[1], shift_pair[1]
        )
        normed_two = normed_two_f.astype(jnp.bfloat16)
        up_grad = jnp.einsum(
            "td,tf->df", normed_two, preactivation_grad, preferred_element_type=jnp.float32
        )
        normed_two_grad = lax.psum(
            jnp.einsum(
                "tf,df->td",
                preactivation_grad,
                up_weight[layer_number],
                preferred_element_type=jnp.float32,
            ),
            "tp",
        )
        middle_part, gain_two, shift_two = norm_pull_two(normed_two_grad)
        middle_grad = upstream + middle_part
        mixed_grad = middle_grad.astype(jnp.bfloat16)
        outward_grad = jnp.einsum(
            "te,td->ed", attended_low, mixed_grad, preferred_element_type=jnp.float32
        )
        attended_grad = jnp.einsum(
            "td,ed->te",
            mixed_grad,
            outward_weight[layer_number],
            preferred_element_type=jnp.float32,
        ).astype(jnp.bfloat16)
        delta_rows = jnp.sum(to_heads(attended_grad.astype(jnp.float32) * attended), axis=-1).T
        query_sum, key_sum, value_sum = grads_by_reduce(
            to_heads(queries),
            to_heads(attended_grad),
            query_scenes,
            tiled_keys,
            normalizer,
            delta_rows,
        )
        projected_grad = jnp.stack(
            [query_sum * score_factor, key_sum * score_factor, value_sum], axis=1
        ).astype(jnp.bfloat16)
        normed_f, norm_pull = jax.vjp(layer_norm, hidden_in, gain_pair[0], shift_pair[0])
        normed = normed_f.astype(jnp.bfloat16)
        inward_grad = jnp.einsum(
            "td,tce->cde", normed, projected_grad, preferred_element_type=jnp.float32
        )
        normed_grad = lax.psum(
            jnp.einsum(
                "tce,cde->td",
                projected_grad,
                inward_weight[layer_number],
                preferred_element_type=jnp.float32,
            ),
            "tp",
        )
        input_part, gain_one, shift_one = norm_pull(normed_grad)
        upstream = middle_grad + input_part
        layer_grads[layer_number] = (
            lax.psum_scatter(inward_grad, "seq", scatter_dimension=1, tiled=True),
            lax.psum_scatter(outward_grad, "seq", scatter_dimension=1, tiled=True),
            lax.psum_scatter(up_grad, "seq", scatter_dimension=0, tiled=True),
            lax.psum_scatter(down_grad, "seq", scatter_dimension=1, tiled=True),
            lax.psum_scatter(
                jnp.stack([gain_one, gain_two]), "seq", scatter_dimension=1, tiled=True
            ),
            lax.psum_scatter(
                jnp.stack([shift_one, shift_two]), "seq", scatter_dimension=1, tiled=True
            ),
        )
    return (
        hidden.astype(jnp.bfloat16),
        upstream,
        jnp.stack([layer_part[0] for layer_part in layer_grads]),
        jnp.stack([layer_part[1] for layer_part in layer_grads]),
        jnp.stack([layer_part[2] for layer_part in layer_grads]),
        jnp.stack([layer_part[3] for layer_part in layer_grads]),
        jnp.stack([layer_part[4] for layer_part in layer_grads]),
        jnp.stack([layer_part[5] for layer_part in layer_grads]),
    )


def solution(mesh):
    placed = (
        P("seq", None),
        P(),
        P(None, None, None, "tp"),
        P(None, "tp", None),
        P(None, None, "tp"),
        P(None, "tp", None),
        P(),
        P(),
        P("seq", None),
    )
    n_seq, n_tp = mesh.shape["seq"], mesh.shape["tp"]
    fits = n_seq == 8 and n_tp == 4
    return jax.shard_map(
        functools.partial(body, n_seq, n_tp) if fits else generic_body,
        mesh=mesh,
        in_specs=placed,
        out_specs=(
            P("seq", None),
            P("seq", None),
            P(None, None, "seq", "tp"),
            P(None, "tp", "seq"),
            P(None, "seq", "tp"),
            P(None, "tp", "seq"),
            P(None, None, "seq"),
            P(None, None, "seq"),
        ),
        check_vma=False,
    )
```

```python
import functools
import math
import jax
import jax.numpy as jnp
from jax import lax
from jax.experimental import pallas as pl
from jax.experimental.pallas import tpu as pltpu
from jax.sharding import PartitionSpec as P

HEAD_DIM = 64
LAYERS = 1
F32, BF16 = jnp.float32, jnp.bfloat16
NEG_FILL = -1e30
SCORE = HEAD_DIM ** -0.5
LOG2E = math.log2(math.e)
ANY = pl.BlockSpec(memory_space=pl.ANY)
VM = pl.BlockSpec(memory_space=pltpu.VMEM)
SM = pl.BlockSpec(memory_space=pltpu.SMEM)
PARAMS = pltpu.CompilerParams(vmem_limit_bytes=60 * 2**20)


def dot(a, b, dims):
    return lax.dot_general(a, b, (dims, ((), ())), preferred_element_type=F32)


def load_all(pairs, sems):
    copies = [pltpu.make_async_copy(s, d, sems.at[i]) for i, (s, d) in enumerate(pairs)]
    for c in copies:
        c.start()
    return copies


def tile_plan(first, last, starts, ends, bk):
    begin, stop = starts[first], ends[last]
    low, high = begin // bk, (stop + bk - 1) // bk
    alone = ends[first] == stop
    clear0 = jnp.where(alone, (begin + bk - 1) // bk, high)
    clear1 = jnp.where(alone, jnp.maximum(clear0, stop // bk), high)
    return low, high, clear0, clear1


def for_tiles(plan, masked, clear):
    low, high, clear0, clear1 = plan
    head = clear0 - low

    def edge(i, _):
        masked(jnp.where(i < head, low + i, clear1 + i - head))
        return 0

    def inner(j, _):
        clear(j)
        return 0

    lax.fori_loop(0, head + high - clear1, edge, 0)
    lax.fori_loop(clear0, clear1, inner, 0)


def low_half(x):
    lane = lax.broadcasted_iota(jnp.int32, x.shape, 1)
    return jnp.where(lane < HEAD_DIM, x, jnp.zeros_like(x))


def high_half(x):
    lane = lax.broadcasted_iota(jnp.int32, x.shape, 1)
    return jnp.where(lane < HEAD_DIM, jnp.zeros_like(x), x)


def swap_halves(x):
    return jnp.concatenate([x[:, HEAD_DIM:], x[:, :HEAD_DIM]], axis=1)


def fwd_kernel(bk, place, starts, ends, begin_rows, stop_rows, mine, other, q_in, *refs):
    o_out, of_out, lse_out, kv, vt, qz, acc, top, ot, sems = refs
    n_q, half = q_in.shape[:2]
    rows = 2 * half
    spots = [pl.ds(pl.multiple_of(place[i] * rows, 128), rows) for i in range(2 * n_q)]
    copies = load_all(
        [(mine.at[k], kv.at[spots[k]]) for k in range(n_q)]
        + [(other.at[k], kv.at[spots[n_q + k]]) for k in range(n_q)],
        sems,
    )
    for k in range(n_q):
        q = q_in[k]
        qz[2 * k] = low_half(q)
        qz[2 * k + 1] = low_half(swap_halves(q))
    for c in copies:
        c.wait()

    def turn(j, _):
        spot = pl.ds(pl.multiple_of(j * 256, 256), 256)
        vt[:, spot] = kv[spot, :].T[HEAD_DIM:]
        return 0

    lax.fori_loop(0, kv.shape[0] // 256, turn, 0)
    factor = SCORE * LOG2E

    def one(i, _):
        first = place[i // 2] * rows + (i % 2) * half
        query = qz[i]
        acc[...] = jnp.zeros_like(acc)
        top[0:1] = jnp.full((1, half), NEG_FILL, F32)
        top[1:2] = jnp.zeros((1, half), F32)
        slab = first // half

        def visit(j, mask):
            spot = pl.ds(pl.multiple_of(j * bk, bk), bk)
            st = dot(kv[spot, :], query, ((1,), (1,)))
            if mask:
                at = j * bk + lax.broadcasted_iota(jnp.int32, st.shape, 0)
                st = jnp.where((at >= begin_rows[slab]) & (at < stop_rows[slab]), st, NEG_FILL)
            old = top[0:1]
            new = jnp.maximum(old, jnp.max(st, axis=0, keepdims=True))
            p = jnp.exp2(st * factor - new * factor)
            shrink = jnp.exp2((old - new) * factor)
            top[0:1] = new
            top[1:2] = top[1:2] * shrink + jnp.sum(p, axis=0, keepdims=True)
            acc[...] = acc[...] * shrink + dot(vt[:, spot], p.astype(BF16), ((1,), (0,)))

        for_tiles(
            tile_plan(first, first + half - 1, starts, ends, bk),
            lambda j: visit(j, True),
            lambda j: visit(j, False),
        )
        ot[i] = acc[...] / top[1:2]
        lse_out[i] = top[0:1] * factor + jnp.log2(top[1:2])
        return 0

    lax.fori_loop(0, 2 * n_q, one, 0)
    for k in range(n_q):
        joined = jnp.concatenate([ot[2 * k], ot[2 * k + 1]], axis=0).T
        of_out[k] = joined
        o_out[k] = joined.astype(BF16)


def attn_fwd(mine, other, q, place, starts, ends, bk):
    n_q, half = q.shape[:2]
    total = starts.shape[0]
    return pl.pallas_call(
        functools.partial(fwd_kernel, bk),
        in_specs=[SM, SM, SM, VM, VM, ANY, ANY, VM],
        out_specs=[VM] * 4,
        out_shape=[
            jax.ShapeDtypeStruct((n_q, half, 128), BF16),
            jax.ShapeDtypeStruct((n_q, half, 128), F32),
            jax.ShapeDtypeStruct((2 * n_q, 1, half), F32),
            jax.ShapeDtypeStruct((total, 128), BF16),
        ],
        scratch_shapes=[
            pltpu.VMEM((HEAD_DIM, total), BF16),
            pltpu.VMEM((2 * n_q, half, 128), BF16),
            pltpu.VMEM((HEAD_DIM, half), F32),
            pltpu.VMEM((8, half), F32),
            pltpu.VMEM((2 * n_q, HEAD_DIM, half), F32),
            pltpu.SemaphoreType.DMA((2 * n_q,)),
        ],
        compiler_params=PARAMS,
        cost_estimate=pl.CostEstimate(flops=3 * 10**10, bytes_accessed=2**22, transcendentals=0),
        name="attend",
    )(place, starts, ends, starts.reshape(-1, 1, half), ends.reshape(-1, 1, half), mine, other, q)


def bwd_kernel(bk, place, starts, ends, begin_rows, stop_rows, kv_hbm, lse, of, q_in, g_in, *refs):
    dq_out, dkv_out, theirs, kv, kt, qz, gz, delta, dkv, dqt_all, acc, sems = refs
    n_q, half = q_in.shape[:2]
    rows = 2 * half
    copies = load_all([(kv_hbm, kv)], sems)
    for k in range(n_q):
        q, g = q_in[k], g_in[k]
        qz[2 * k] = low_half(q)
        qz[2 * k + 1] = low_half(swap_halves(q))
        gz[2 * k] = high_half(swap_halves(g))
        gz[2 * k + 1] = high_half(g)
        prod = (g.astype(F32) * of[k]).T
        delta[2 * k] = jnp.sum(prod[:HEAD_DIM], axis=0, keepdims=True)
        delta[2 * k + 1] = jnp.sum(prod[HEAD_DIM:], axis=0, keepdims=True)
    copies[0].wait()

    def turn(j, _):
        spot = pl.ds(pl.multiple_of(j * 256, 256), 256)
        kt[:, spot] = kv[spot, :].T[:HEAD_DIM]
        dkv[spot, :] = jnp.zeros((256, 128), F32)
        return 0

    lax.fori_loop(0, kv.shape[0] // 256, turn, 0)
    factor = SCORE * LOG2E

    def one(i, _):
        first = place[i // 2] * rows + (i % 2) * half
        query, grad, lse_row, delta_row = qz[i], gz[i], lse[i], delta[i]
        acc[...] = jnp.zeros_like(acc)
        slab = first // half

        def visit(j, mask):
            spot = pl.ds(pl.multiple_of(j * bk, bk), bk)
            block = kv[spot, :]
            st = dot(block, query, ((1,), (1,)))
            p = jnp.exp2(st * factor - lse_row)
            if mask:
                at = j * bk + lax.broadcasted_iota(jnp.int32, st.shape, 0)
                p = jnp.where((at >= begin_rows[slab]) & (at < stop_rows[slab]), p, 0.0)
            dp = dot(block, grad, ((1,), (1,)))
            ds = (p * (dp - delta_row)).astype(BF16)
            dkv[spot, :] += dot(ds, query, ((1,), (0,))) + dot(p.astype(BF16), grad, ((1,), (0,)))
            acc[...] += dot(kt[:, spot], ds, ((1,), (0,)))

        for_tiles(
            tile_plan(first, first + half - 1, starts, ends, bk),
            lambda j: visit(j, True),
            lambda j: visit(j, False),
        )
        dqt_all[i] = acc[...] * SCORE
        return 0

    lax.fori_loop(0, 2 * n_q, one, 0)
    for k in range(n_q):
        joined = jnp.concatenate([dqt_all[2 * k], dqt_all[2 * k + 1]], axis=0).T
        dq_out[k] = joined.astype(BF16)
    for k in range(n_q):
        dkv_out[k] = dkv[pl.ds(pl.multiple_of(place[k] * rows, 128), rows), :]
        other = pl.ds(pl.multiple_of(place[n_q + k] * rows, 128), rows)
        theirs[k] = dkv[other, :].astype(BF16)


def attn_bwd(kv, q, g, of, lse, place, starts, ends, bk):
    n_q, half = q.shape[:2]
    total = starts.shape[0]
    return pl.pallas_call(
        functools.partial(bwd_kernel, bk),
        in_specs=[SM, SM, SM, VM, VM, ANY] + [VM] * 4,
        out_specs=[VM] * 3,
        out_shape=[
            jax.ShapeDtypeStruct((n_q, half, 128), BF16),
            jax.ShapeDtypeStruct((n_q, 2 * half, 128), F32),
            jax.ShapeDtypeStruct((n_q, 2 * half, 128), BF16),
        ],
        scratch_shapes=[
            pltpu.VMEM((total, 128), BF16),
            pltpu.VMEM((HEAD_DIM, total), BF16),
            pltpu.VMEM((2 * n_q, half, 128), BF16),
            pltpu.VMEM((2 * n_q, half, 128), BF16),
            pltpu.VMEM((2 * n_q, 1, half), F32),
            pltpu.VMEM((total, 128), F32),
            pltpu.VMEM((2 * n_q, HEAD_DIM, half), F32),
            pltpu.VMEM((HEAD_DIM, half), F32),
            pltpu.SemaphoreType.DMA((1,)),
        ],
        compiler_params=PARAMS,
        cost_estimate=pl.CostEstimate(flops=4 * 10**10, bytes_accessed=2**22, transcendentals=0),
        name="attend_back",
    )(place, starts, ends, starts.reshape(-1, 1, half), ends.reshape(-1, 1, half), kv, lse, of, q, g)


SHIELD = 3 * 10**10


def stats(x):
    average = jnp.mean(x, axis=-1, keepdims=True)
    centered = x - average
    variance = jnp.mean(centered * centered, axis=-1, keepdims=True)
    return centered, lax.rsqrt(variance + 1e-05)


def norm_back(grad, xhat, rate, gain):
    scaled = grad * gain
    return rate * (
        scaled
        - jnp.mean(scaled, axis=-1, keepdims=True)
        - xhat * jnp.mean(scaled * xhat, axis=-1, keepdims=True)
    )


def column_sums(grad, xhat):
    return jnp.concatenate(
        [jnp.sum(grad * xhat, axis=0, keepdims=True), jnp.sum(grad, axis=0, keepdims=True)], axis=0
    )


def shape_of(*dims, dtype=BF16):
    return jax.ShapeDtypeStruct(dims, dtype)


def kernel_call(kernel, name, specs, outs, args, flops=0, scratch=()):
    size = sum(a.size * a.dtype.itemsize for a in list(args) + list(outs))
    return pl.pallas_call(
        kernel,
        in_specs=specs,
        out_specs=[VM] * len(outs),
        out_shape=outs,
        scratch_shapes=list(scratch),
        compiler_params=PARAMS,
        cost_estimate=pl.CostEstimate(flops=flops, bytes_accessed=size, transcendentals=0),
        name=name,
    )(*args)


def block_rows(index, count):
    return pl.ds(pl.multiple_of(index * count, 16), count)


def head_cut(h):
    return slice(h * HEAD_DIM, (h + 1) * HEAD_DIM)


def project_kernel(x, gain, shift, weight, normed_out, kv_out, q_out, q_flat):
    n_z, half, rows = q_out.shape[0], q_out.shape[1], x.shape[0]
    for t in range(2):
        spot = slice(t * half, (t + 1) * half)
        centered, rate = stats(x[spot, :].astype(F32))
        normed = (centered * rate * gain[0, 0:1] + shift[0, 0:1]).astype(BF16)
        normed_out[spot, :] = normed
        q, k, v = [dot(normed, weight[0, c], ((1,), (0,))).astype(BF16) for c in range(3)]
        q_flat[spot, :] = q
        for h in range(n_z):
            kv_out[h, spot, :] = jnp.concatenate([k[:, head_cut(h)], v[:, head_cut(h)]], axis=1)
    for h in range(n_z):
        q_out[h] = jnp.concatenate([q_flat[:half, head_cut(h)], q_flat[half:, head_cut(h)]], axis=1)


def project(n_z, x, gains, shifts, weight):
    rows, width = x.shape
    return kernel_call(
        project_kernel,
        "project",
        [VM] * 4,
        [shape_of(rows, width), shape_of(n_z, rows, 128), shape_of(n_z, rows // 2, 128)],
        (x, gains, shifts, weight),
        2 * rows * weight.size,
        [pltpu.VMEM((rows, n_z * HEAD_DIM), BF16)],
    )


def spread_kernel(o_in, out):
    n_z, half = o_in.shape[:2]
    out[:half, :] = jnp.concatenate([o_in[h, :, :HEAD_DIM] for h in range(n_z)], axis=1)
    out[half:, :] = jnp.concatenate([o_in[h, :, HEAD_DIM:] for h in range(n_z)], axis=1)


def spread(o):
    n_z, half = o.shape[:2]
    return kernel_call(spread_kernel, "spread", [VM], [shape_of(2 * half, n_z * HEAD_DIM)], (o,))[0]


def pack_kernel(x, out):
    n_z, half = out.shape[:2]
    for h in range(n_z):
        out[h] = jnp.concatenate([x[:half, head_cut(h)], x[half:, head_cut(h)]], axis=1)


def pack(n_z, x):
    return kernel_call(pack_kernel, "pack", [VM], [shape_of(n_z, x.shape[0] // 2, 128)], (x,))[0]


def mix_kernel(here, x, gain, shift, parts, *refs):
    weights, (after_out, normed_out) = refs[:-2], refs[-2:]
    quarter = parts.shape[1]
    mixed = sum(dot(parts[here[1] ^ m], w[...], ((1,), (0,))) for m, w in enumerate(weights))
    after = x[block_rows(here[1], quarter), :].astype(F32) + mixed
    after_out[...] = after
    centered, rate = stats(after)
    normed_out[...] = (centered * rate * gain[0, 1:2] + shift[0, 1:2]).astype(BF16)


def mix(here, x, gains, shifts, parts, weights):
    n_t, quarter, width = parts.shape[0], parts.shape[1], x.shape[1]
    return kernel_call(
        mix_kernel,
        "mix",
        [SM] + [VM] * (4 + n_t),
        [shape_of(quarter, width, dtype=F32), shape_of(quarter, width)],
        (here, x, gains, shifts, parts, *weights),
        2 * quarter * width * width,
    )


def gelu_pair(u):
    c = math.sqrt(2.0 / math.pi)
    square = u * u
    t = jnp.tanh(c * (u + 0.044715 * square * u))
    slope = 0.5 * (1.0 + t) + 0.5 * u * (1.0 - t * t) * c * (1.0 + 3 * 0.044715 * square)
    return 0.5 * u * (1.0 + t), slope


def hidden_kernel(n_t, here, cot, up, down, *refs):
    slots, (act_out, pre_out, normed), parts = refs[:n_t], refs[n_t : n_t + 3], refs[n_t + 3 :]
    quarter, tile = slots[0].shape[0], 256
    for m, part in enumerate(slots):
        normed[block_rows(here[1] ^ m, quarter), :] = part[...]

    def one(j, _):
        cut = pl.ds(pl.multiple_of(j * tile, tile), tile)
        act, slope = gelu_pair(dot(normed[...], up[0, :, cut], ((1,), (0,))))
        act_out[:, cut] = act.astype(BF16)
        grad = dot(cot[...], down[0, cut, :], ((1,), (1,)))
        pre_out[:, cut] = (grad * slope).astype(BF16)
        return 0

    lax.fori_loop(0, up.shape[2] // tile, one, 0)
    for m, out in enumerate(parts):
        mine = pre_out[block_rows(here[1] ^ m, quarter), :]
        out[...] = dot(mine, up[0], ((1,), (1,))).astype(BF16)


def hidden_layer(here, slots, cot, up, down):
    quarter, width = slots[0].shape
    n_t, units = len(slots), up.shape[2]
    rows = n_t * quarter
    outs = kernel_call(
        functools.partial(hidden_kernel, n_t),
        "hidden_layer",
        [SM] + [VM] * (3 + n_t),
        [shape_of(rows, units), shape_of(rows, units), shape_of(rows, width)]
        + [shape_of(quarter, width)] * n_t,
        (here, cot, up, down, *slots),
        6 * rows * width * units,
    )
    return outs[0], outs[1], outs[2], outs[3:]


def branch_kernel(here, act, down, own, *sends):
    quarter = own.shape[0]
    for m, out in enumerate([own] + list(sends)):
        part = act[block_rows(here[1] ^ m, quarter), :]
        out[...] = dot(part, down[0], ((1,), (0,))).astype(out.dtype)


def branch_parts(n_t, here, act, down):
    rows, width = act.shape[0], down.shape[2]
    quarter = rows // n_t
    return kernel_call(
        branch_kernel,
        "branch",
        [SM] + [VM] * 2,
        [shape_of(quarter, width, dtype=F32)] + [shape_of(quarter, width)] * (n_t - 1),
        (here, act, down),
        2 * rows * width * act.shape[1],
    )


def middle_kernel(n_t, here, after, cot, gain, *refs):
    parts, weights, refs = refs[:n_t], refs[n_t : 2 * n_t], refs[2 * n_t :]
    middle_out, mixed_out, sums_out, grads = refs
    quarter = after.shape[0]
    grad = sum(part[...].astype(F32) for part in parts)
    centered, rate = stats(after[...])
    xhat = centered * rate
    sums_out[...] = column_sums(grad, xhat)
    upstream = cot[block_rows(here[1], quarter), :].astype(F32)
    middle = upstream + norm_back(grad, xhat, rate, gain[0, 1:2])
    middle_out[...] = middle
    mixed = middle.astype(BF16)
    mixed_out[...] = mixed
    for m in range(n_t):
        grads[here[1] ^ m] = dot(mixed, weights[m][...], ((1,), (1,))).astype(BF16)


def middle_back(here, after, cot, gains, parts, weights):
    n_t, (quarter, width) = len(parts), parts[0].shape
    return kernel_call(
        functools.partial(middle_kernel, n_t),
        "middle_back",
        [SM] + [VM] * (3 + 2 * n_t),
        [
            shape_of(quarter, width, dtype=F32),
            shape_of(quarter, width),
            shape_of(2, width, dtype=F32),
            shape_of(n_t, quarter, weights[0].shape[0]),
        ],
        (here, after, cot, gains, *parts, *weights),
        SHIELD,
    )


def join_kernel(mine, theirs, q, out):
    n_z, rows = mine.shape[:2]
    lane = lax.broadcasted_iota(jnp.int32, mine.shape[1:], 1)
    factor = jnp.where(lane < HEAD_DIM, SCORE, 1.0)
    for k in range(n_z):
        out[k, :rows] = ((mine[k] + theirs[k].astype(F32)) * factor).astype(BF16)
        out[k, rows:] = q[k]


def join(mine, theirs, q):
    n_z, rows = mine.shape[:2]
    return kernel_call(
        join_kernel,
        "join",
        [VM] * 3,
        [shape_of(n_z, rows + q.shape[1], 128)],
        (mine, theirs, q),
    )[0]


def unproject_kernel(weight, grads, flat, part):
    n_z, rows = grads.shape[0], flat.shape[0]
    half = rows // 2
    width = n_z * HEAD_DIM
    heads = range(n_z)
    low, high = slice(0, HEAD_DIM), slice(HEAD_DIM, 2 * HEAD_DIM)
    flat[:half, :width] = jnp.concatenate([grads[h, rows:, low] for h in heads], axis=1)
    flat[half:, :width] = jnp.concatenate([grads[h, rows:, high] for h in heads], axis=1)
    flat[:, width : 2 * width] = jnp.concatenate([grads[h, :rows, low] for h in heads], axis=1)
    flat[:, 2 * width :] = jnp.concatenate([grads[h, :rows, high] for h in heads], axis=1)
    total = sum(
        dot(flat[:, c * width : (c + 1) * width], weight[0, c], ((1,), (1,))) for c in range(3)
    )
    part[...] = total.astype(BF16)


def unproject(weight, grads):
    width = weight.shape[2]
    rows = grads.shape[1] * 2 // 3
    return kernel_call(
        unproject_kernel,
        "unproject",
        [VM] * 2,
        [shape_of(rows, 3 * weight.shape[3]), shape_of(rows, width)],
        (weight, grads),
        2 * rows * weight.size,
    )


def last_kernel(here, x, middle, gain, parts, out):
    quarter = middle.shape[0]
    grad = slot_sum(parts)
    centered, rate = stats(x[block_rows(here[1], quarter), :].astype(F32))
    out[...] = (middle[...] + norm_back(grad, centered * rate, rate, gain[0, 0:1])).astype(BF16)


def last_back(here, x, middle, gains, parts):
    return kernel_call(
        last_kernel,
        "last_back",
        [SM] + [VM] * 4,
        [shape_of(*middle.shape)],
        (here, x, middle, gains, parts),
        SHIELD,
    )[0]


def lay_kernel(here, *refs):
    parts, out = refs[:-1], refs[-1]
    for m, part in enumerate(parts):
        out[block_rows(here[1] ^ m, part.shape[0]), :] = part[...].astype(out.dtype)


def lay(here, parts, dtype):
    quarter, width = parts[0].shape
    return kernel_call(
        lay_kernel,
        "lay",
        [SM] + [VM] * len(parts),
        [shape_of(len(parts) * quarter, width, dtype=dtype)],
        (here, *parts),
    )[0]


def pair_sides(here, mine, theirs):
    for out, side in ((theirs, 1), (mine, 0)):
        for k in range(mine.shape[0]):
            owner = 2 * k + (here[2] ^ side)
            yield out, k, pl.ds(pl.multiple_of(owner * 128, 128), 128)


def sides(n_z, depth):
    return [shape_of(n_z, depth, 128, dtype=F32), shape_of(n_z, depth, 128)]


def put_lanes(out, k, first, block):
    for j in range(block.shape[1] // 128):
        out[k, first + j * 128 : first + (j + 1) * 128, :] = block[:, j * 128 : (j + 1) * 128]


def early_kernel(here, act, pre, normed, cot, mine, theirs):
    units = act.shape[1]
    for out, k, cut in pair_sides(here, mine, theirs):
        out[k, :units, :] = dot(act[...], cot[:, cut], ((0,), (0,))).astype(out.dtype)
        put_lanes(out, k, units, dot(normed[:, cut], pre[...], ((0,), (0,))).astype(out.dtype))


def early_grads(n_z, here, act, pre, normed, cot):
    depth = 2 * act.shape[1]
    return kernel_call(
        early_kernel,
        "early_grads",
        [SM] + [VM] * 4,
        sides(n_z, depth),
        (here, act, pre, normed, cot),
        2 * act.shape[0] * depth * normed.shape[1],
    )


def halves(x):
    high = x.astype(BF16)
    return high, (x - high.astype(F32)).astype(BF16)


def outward_kernel(here, attended, *refs):
    mixed, (mine, theirs) = refs[:-2], refs[-2:]
    quarter = mixed[0].shape[0]
    for out, k, cut in pair_sides(here, mine, theirs):
        outward = sum(
            dot(attended[block_rows(here[1] ^ m, quarter), :], part[:, cut], ((0,), (0,)))
            for m, part in enumerate(mixed)
        )
        out[k] = outward.astype(out.dtype)


def outward_grads(n_z, here, attended, mixed):
    rows, share = attended.shape
    return kernel_call(
        outward_kernel,
        "outward_grads",
        [SM] + [VM] * (1 + len(mixed)),
        sides(n_z, share),
        (here, attended, *mixed),
        2 * rows * share * mixed[0].shape[1],
    )


def fold_slots_kernel(here, mine, theirs, *outs):
    for k, out in enumerate(outs):
        at = lax.rem(here[0] + k, len(outs))
        out[...] = (mine[at] + theirs[at].astype(F32)).astype(out.dtype)


def fold_slots(here, mine, theirs):
    n_z, depth, _ = mine.shape
    return kernel_call(
        fold_slots_kernel,
        "fold_slots",
        [SM] + [VM] * 2,
        [shape_of(depth, 128, dtype=F32)] + [shape_of(depth, 128)] * (n_z - 1),
        (here, mine, theirs),
    )


def late_kernel(here, x, normed, grad, sums, part, mine, theirs, scratch):
    depth, step = grad.shape[1], 256
    total = jnp.zeros((2, x.shape[1]), F32)
    for m in range(x.shape[0] // step):
        spot = slice(m * step, (m + 1) * step)
        centered, rate = stats(x[spot, :].astype(F32))
        total = total + column_sums(part[spot, :].astype(F32), centered * rate)
    scratch[0:2, :] = total
    scratch[2:4, :] = sums[...]
    scratch[4:8, :] = jnp.zeros((4, x.shape[1]), F32)
    for out, k, cut in pair_sides(here, mine, theirs):
        put_lanes(out, k, 0, dot(normed[:, cut], grad[...], ((0,), (0,))).astype(out.dtype))
        block = scratch[:, cut]
        if out.dtype == BF16:
            high, low = halves(block[0:4].astype(F32))
            block = jnp.concatenate([high.astype(F32), low.astype(F32)], axis=0).astype(BF16)
        out[k, depth:, :] = block


def late_grads(n_z, here, x, normed, grad, sums, part):
    depth = grad.shape[1] + 8
    return kernel_call(
        late_kernel,
        "late_grads",
        [SM] + [VM] * 5,
        sides(n_z, depth),
        (here, x, normed, grad, sums, part),
        2 * grad.shape[0] * depth * normed.shape[1],
        [pltpu.VMEM((8, x.shape[1]), F32)],
    )


def fold_kernel(mine, theirs, out):
    for k in range(mine.shape[0]):
        out[k] = (mine[k] + theirs[k].astype(F32)).astype(BF16)


def fold(mine, theirs):
    return kernel_call(fold_kernel, "fold", [VM] * 2, [shape_of(*mine.shape)], (mine, theirs))[0]


def fold_late_kernel(mine, theirs, out):
    depth = mine.shape[1] - 8
    for k in range(mine.shape[0]):
        out[k, :depth] = (mine[k, :depth] + theirs[k, :depth].astype(F32)).astype(BF16)
        tail = mine[k, depth:] + theirs[k, depth:].astype(F32)
        high, low = halves(tail[0:4] + tail[4:8])
        both = jnp.concatenate([high.astype(F32), low.astype(F32)], axis=0)
        out[k, depth:] = both.astype(BF16)


def fold_late(mine, theirs):
    return kernel_call(
        fold_late_kernel, "fold_late", [VM] * 2, [shape_of(*mine.shape)], (mine, theirs)
    )[0]


def slot_sum(parts):
    return sum(parts[k].astype(F32) for k in range(parts.shape[0]))


def finish_early_kernel(parts, down_out, up_out):
    total = slot_sum(parts)
    units = down_out.shape[0]
    down_out[...] = total[:units]
    for j in range(units // 128):
        up_out[:, j * 128 : (j + 1) * 128] = total[units + j * 128 : units + (j + 1) * 128]


def finish_early(units, parts):
    return kernel_call(
        finish_early_kernel,
        "finish_early",
        [VM],
        [shape_of(units, 128, dtype=F32), shape_of(128, units, dtype=F32)],
        (parts,),
    )


def finish_late_kernel(parts, out, sums_out):
    total = slot_sum(parts)
    per = out.shape[2] // 128
    for c in range(3):
        for j in range(per):
            at = (c * per + j) * 128
            out[c, :, j * 128 : (j + 1) * 128] = total[at : at + 128]
    last = total.shape[0] - 8
    sums_out[...] = jnp.concatenate([total[last : last + 4] + total[last + 4 :]] * 2, axis=0)


def finish_late(share, parts):
    return kernel_call(
        finish_late_kernel,
        "finish_late",
        [VM],
        [
            shape_of(3, 128, share, dtype=F32),
            shape_of(8, 128, dtype=F32),
        ],
        (parts,),
    )


def scene_edges(scene_index):
    total = scene_index.shape[0]
    at = lax.iota(jnp.int32, total)
    edge = jnp.concatenate([jnp.ones((1,), jnp.bool_), scene_index[1:] != scene_index[:-1]])
    starts = lax.cummax(jnp.where(edge, at, 0))
    closing = jnp.concatenate([edge[1:], jnp.ones((1,), jnp.bool_)])
    return starts, lax.cummin(jnp.where(closing, at + 1, total), reverse=True)


def body(
    n_seq,
    n_tp,
    tokens,
    scene_index,
    inward_weight,
    outward_weight,
    up_weight,
    down_weight,
    norm_gains,
    norm_shifts,
    cotangent,
):
    n_z, rows, width = n_seq // 2, tokens.shape[0], tokens.shape[1]
    units, share = up_weight.shape[2], outward_weight.shape[1]
    quarter = rows // n_tp
    seq, tp = lax.axis_index("seq"), lax.axis_index("tp")
    z, c = seq // 2, seq % 2
    here = jnp.stack([z, tp, c]).astype(jnp.int32)
    lines = [list(range(b, n_seq, 2)) for b in range(2)]

    def line(x):
        return lax.all_to_all(x, "seq", 0, 0, axis_index_groups=lines, tiled=True)

    def plane(x):
        return lax.all_to_all(x, "tp", 0, 0, tiled=True)

    def across(x):
        return lax.ppermute(x, "seq", [(a, a ^ 1) for a in range(n_seq)])

    def along(x, k):
        return lax.ppermute(
            x, "seq", [(a * 2 + b, (a + k) % n_z * 2 + b) for a in range(n_z) for b in range(2)]
        )

    def over(x, m):
        return lax.ppermute(x, "tp", [(a, a ^ m) for a in range(n_tp)])

    def square(slots):
        return [slots[0]] + [over(slots[m], m) for m in range(1, n_tp)]

    place = jnp.stack([k * 2 + (c ^ g) for g in range(2) for k in range(n_z)]).astype(jnp.int32)
    starts, ends = scene_edges(scene_index)
    normed, kv_send, q_send = project(n_z, tokens, norm_gains, norm_shifts, inward_weight)
    kv_mine = line(kv_send)
    kv_other = across(kv_mine)
    q = line(q_send)
    outward_all = square([outward_weight[0]] * n_tp)
    (q, outward_all) = lax.optimization_barrier((q, outward_all))
    o, o_full, lse, kv_full = attn_fwd(kv_mine, kv_other, q, place, starts, ends, 1024)
    attended = spread(line(o))
    parts = plane(attended.reshape(n_tp, quarter, share))
    after, normed_two = mix(here, tokens, norm_gains, norm_shifts, parts, outward_all)
    act, pre, normed_two, grad_parts = hidden_layer(
        here, square([normed_two] * n_tp), cotangent, up_weight, down_weight
    )
    middle, mixed, sums_two, grads = middle_back(
        here, after, cotangent, norm_gains, square(grad_parts), outward_all
    )
    mine, theirs = early_grads(n_z, here, act, pre, normed_two, cotangent)
    theirs = across(theirs)
    branch = branch_parts(n_tp, here, act, down_weight)
    early = fold(mine, theirs)
    grads = plane(grads)
    (grads, mixed) = lax.optimization_barrier((grads, mixed))
    mixed = square([mixed] * n_tp)
    g = line(pack(n_z, grads.reshape(rows, share)))
    (g, early, branch, mixed) = lax.optimization_barrier((g, early, branch, mixed))
    branch = square(branch)
    early = line(early)
    dq, dkv, dkv_theirs = attn_bwd(kv_full, q, g, o_full, lse, place, starts, ends, 1024)
    (dq, dkv, dkv_theirs, early, branch) = lax.optimization_barrier(
        (dq, dkv, dkv_theirs, early, branch)
    )
    back = line(join(dkv, across(dkv_theirs), dq))
    out_own = (after + sum(part.astype(F32) for part in branch)).astype(BF16)
    out_slots = square([out_own] * n_tp)
    down_grad, up_grad = finish_early(units, early)
    activations = lay(here, out_slots, BF16)
    mine, theirs = outward_grads(n_z, here, attended, mixed)
    side = fold_slots(here, mine, across(theirs))
    (back, activations, down_grad, up_grad, side) = lax.optimization_barrier(
        (back, activations, down_grad, up_grad, side)
    )
    side = [side[0]] + [along(side[k], k) for k in range(1, n_z)]
    flat, back_part = unproject(inward_weight, back)
    mine, theirs = late_grads(n_z, here, tokens, normed, flat, sums_two, back_part)
    late = fold_late(mine, across(theirs))
    back_part = plane(back_part.reshape(n_tp, quarter, width))
    (back_part, late, side) = lax.optimization_barrier((back_part, late, side))
    outward_grad = sum(part.astype(F32) for part in side)
    token_own = last_back(here, tokens, middle, norm_gains, back_part)
    (late, token_own) = lax.optimization_barrier((late, token_own))
    late = line(late)
    token_slots = square([token_own] * n_tp)
    inward_grad, sums = finish_late(share, late)
    (sums, token_slots) = lax.optimization_barrier((sums, token_slots))
    sums = square([sums] * n_tp)
    token_grad = lay(here, token_slots, F32)
    while len(sums) > 1:
        sums = [sums[m] + sums[m + 1] for m in range(0, len(sums), 2)]
    sums = sums[0]
    gain_grad = jnp.stack([sums[0], sums[2]])
    shift_grad = jnp.stack([sums[1], sums[3]])
    return (
        activations,
        token_grad,
        inward_grad[None],
        outward_grad[None],
        up_grad[None],
        down_grad[None],
        gain_grad[None],
        shift_grad[None],
    )


def layer_norm(hidden, gain_row, shift_row):
    average = jnp.mean(hidden, axis=-1, keepdims=True)
    centered = hidden - average
    variance = jnp.mean(centered * centered, axis=-1, keepdims=True)
    return centered * lax.rsqrt(variance + 1e-05) * gain_row + shift_row


def gelu_tanh(preactivation):
    return jax.nn.gelu(preactivation, approximate=True)


def to_heads(flat_rows):
    return flat_rows.reshape(flat_rows.shape[0], -1, HEAD_DIM)


def scenes_meet(query_scenes, key_scenes):
    return jnp.logical_and(key_scenes[0] <= query_scenes[-1], key_scenes[-1] >= query_scenes[0])


def score_rows(query_heads, key_heads, query_scenes, key_scenes):
    scores = jnp.einsum(
        "qhd,khd->hqk", query_heads, key_heads, preferred_element_type=jnp.float32
    ) * HEAD_DIM ** (-0.5)
    same_scene = (query_scenes[:, None] == key_scenes[None, :])[None]
    return (scores, same_scene)


def probabilities(scores, same_scene, normalizer):
    return jnp.where(same_scene, jnp.exp(scores - normalizer[:, :, None]), 0.0)


def key_tiles(key_all, value_all, scene_index):
    tile_rows = min(1024, key_all.shape[0])
    tile_count = key_all.shape[0] // tile_rows
    return (
        key_all.reshape(tile_count, tile_rows, -1, HEAD_DIM),
        value_all.reshape(tile_count, tile_rows, -1, HEAD_DIM),
        scene_index.reshape(tile_count, tile_rows),
    )


def log_normalizer(query_heads, query_scenes, tiled_keys):

    def log_visit_tile(running_pair, inputs_pair):
        key_heads, key_scenes = inputs_pair

        def log_compute(pair_now):
            running_max, running_sum = pair_now
            scores, same_scene = score_rows(query_heads, key_heads, query_scenes, key_scenes)
            masked = jnp.where(same_scene, scores, NEG_FILL)
            new_max = jnp.maximum(running_max, jnp.max(masked, axis=-1))
            weights = jnp.where(same_scene, jnp.exp(masked - new_max[:, :, None]), 0.0)
            return (
                new_max,
                running_sum * jnp.exp(running_max - new_max) + jnp.sum(weights, axis=-1),
            )

        return (
            lax.cond(
                scenes_meet(query_scenes, key_scenes),
                log_compute,
                lambda pair_now: pair_now,
                running_pair,
            ),
            None,
        )

    stat_shape = (query_heads.shape[1], query_heads.shape[0])
    start_pair = (jnp.full(stat_shape, NEG_FILL, jnp.float32), jnp.zeros(stat_shape, jnp.float32))
    final_pair, _ = lax.scan(log_visit_tile, start_pair, (tiled_keys[0], tiled_keys[2]))
    return final_pair[0] + jnp.log(final_pair[1])


def attend_all(query_heads, query_scenes, tiled_keys, normalizer):

    def attend_visit_tile(running_total, inputs_triple):
        key_heads, value_heads, key_scenes = inputs_triple

        def attend_compute(total_now):
            scores, same_scene = score_rows(query_heads, key_heads, query_scenes, key_scenes)
            weights = probabilities(scores, same_scene, normalizer).astype(jnp.bfloat16)
            return total_now + jnp.einsum(
                "hqk,khd->qhd", weights, value_heads, preferred_element_type=jnp.float32
            )

        return (
            lax.cond(
                scenes_meet(query_scenes, key_scenes),
                attend_compute,
                lambda total_now: total_now,
                running_total,
            ),
            None,
        )

    running_total, _ = lax.scan(
        attend_visit_tile, jnp.zeros(query_heads.shape, jnp.float32), tiled_keys
    )
    return running_total.reshape(running_total.shape[0], -1)


def score_gradients(
    query_heads,
    key_heads,
    value_heads,
    grad_heads,
    query_scenes,
    key_scenes,
    normalizer,
    delta_rows,
):
    scores, same_scene = score_rows(query_heads, key_heads, query_scenes, key_scenes)
    weights = probabilities(scores, same_scene, normalizer)
    weight_grad = jnp.einsum(
        "qhd,khd->hqk", grad_heads, value_heads, preferred_element_type=jnp.float32
    )
    score_grad = (weights * (weight_grad - delta_rows[:, :, None])).astype(jnp.bfloat16)
    return (weights.astype(jnp.bfloat16), score_grad)


def grads_by_reduce(query_heads, grad_heads, query_scenes, tiled_keys, normalizer, delta_rows):
    tile_rows = tiled_keys[0].shape[1]
    joined_width = 2 * query_heads.shape[1] * query_heads.shape[2]

    def grads_visit_tile(query_total, inputs_triple):
        key_heads, value_heads, key_scenes = inputs_triple

        def grads_compute(total_now):
            weights, score_grad = score_gradients(
                query_heads,
                key_heads,
                value_heads,
                grad_heads,
                query_scenes,
                key_scenes,
                normalizer,
                delta_rows,
            )
            total_now = total_now + jnp.einsum(
                "hqk,khd->qhd", score_grad, key_heads, preferred_element_type=jnp.float32
            )
            key_term = jnp.einsum(
                "hqk,qhd->khd", score_grad, query_heads, preferred_element_type=jnp.float32
            )
            value_term = jnp.einsum(
                "hqk,qhd->khd", weights, grad_heads, preferred_element_type=jnp.float32
            )
            joined = jnp.concatenate(
                [key_term.reshape(tile_rows, -1), value_term.reshape(tile_rows, -1)], axis=1
            )
            return (total_now, joined)

        def skipped(total_now):
            return (total_now, jnp.zeros((tile_rows, joined_width), jnp.float32))

        return lax.cond(scenes_meet(query_scenes, key_scenes), grads_compute, skipped, query_total)

    query_total, key_terms_all = lax.scan(
        grads_visit_tile, jnp.zeros(query_heads.shape, jnp.float32), tiled_keys
    )
    key_terms_all = key_terms_all.reshape(-1, key_terms_all.shape[-1])
    summed = lax.psum_scatter(key_terms_all, "seq", scatter_dimension=0, tiled=True)
    half_width = summed.shape[1] // 2
    return (
        query_total.reshape(query_total.shape[0], -1),
        summed[:, :half_width],
        summed[:, half_width:],
    )


def generic_body(
    tokens,
    scene_index,
    inward_weight,
    outward_weight,
    up_weight,
    down_weight,
    norm_gains,
    norm_shifts,
    cotangent,
):
    local_rows = tokens.shape[0]
    score_factor = HEAD_DIM ** (-0.5)
    query_scenes = lax.dynamic_slice_in_dim(
        scene_index, lax.axis_index("seq") * local_rows, local_rows
    )
    hidden = tokens.astype(jnp.float32)
    layer_number = 0
    gain_pair = norm_gains[layer_number]
    shift_pair = norm_shifts[layer_number]
    normed = layer_norm(hidden, gain_pair[0], shift_pair[0]).astype(jnp.bfloat16)
    projected = jnp.einsum(
        "td,cde->tce", normed, inward_weight[layer_number], preferred_element_type=jnp.float32
    ).astype(jnp.bfloat16)
    queries = projected[:, 0]
    key_local = projected[:, 1]
    value_local = projected[:, 2]
    key_all = lax.all_gather(key_local, "seq", axis=0, tiled=True)
    value_all = lax.all_gather(value_local, "seq", axis=0, tiled=True)
    tiled_keys = key_tiles(key_all, value_all, scene_index)
    query_heads = to_heads(queries)
    normalizer = log_normalizer(query_heads, query_scenes, tiled_keys)
    attended = attend_all(query_heads, query_scenes, tiled_keys, normalizer)
    attended_low = attended.astype(jnp.bfloat16)
    mixed_sum = lax.psum(
        jnp.dot(attended_low, outward_weight[layer_number], preferred_element_type=jnp.float32),
        "tp",
    )
    after_attention = hidden + mixed_sum
    normed_two = layer_norm(after_attention, gain_pair[1], shift_pair[1]).astype(jnp.bfloat16)
    preactivation = jnp.dot(normed_two, up_weight[layer_number], preferred_element_type=jnp.float32)
    activated = gelu_tanh(preactivation).astype(jnp.bfloat16)
    branch = lax.psum(
        jnp.dot(activated, down_weight[layer_number], preferred_element_type=jnp.float32), "tp"
    )
    kept_layers = [
        (
            hidden,
            after_attention,
            queries,
            key_local,
            value_local,
            tiled_keys,
            normalizer,
            attended,
            attended_low,
            preactivation,
            activated,
        )
    ]
    hidden = after_attention + branch
    upstream = cotangent.astype(jnp.float32)
    layer_grads = [None] * LAYERS
    for layer_number in reversed(range(LAYERS)):
        (
            hidden_in,
            after_attention,
            queries,
            key_local,
            value_local,
            tiled_keys,
            normalizer,
            attended,
            attended_low,
            preactivation,
            activated,
        ) = kept_layers[layer_number]
        gain_pair = norm_gains[layer_number]
        shift_pair = norm_shifts[layer_number]
        branch_grad = upstream.astype(jnp.bfloat16)
        down_grad = jnp.einsum(
            "tf,td->fd", activated, branch_grad, preferred_element_type=jnp.float32
        )
        act_grad = jnp.einsum(
            "td,fd->tf", branch_grad, down_weight[layer_number], preferred_element_type=jnp.float32
        )
        _, gelu_pull = jax.vjp(gelu_tanh, preactivation)
        preactivation_grad = gelu_pull(act_grad)[0].astype(jnp.bfloat16)
        normed_two_f, norm_pull_two = jax.vjp(
            layer_norm, after_attention, gain_pair[1], shift_pair[1]
        )
        normed_two = normed_two_f.astype(jnp.bfloat16)
        up_grad = jnp.einsum(
            "td,tf->df", normed_two, preactivation_grad, preferred_element_type=jnp.float32
        )
        normed_two_grad = lax.psum(
            jnp.einsum(
                "tf,df->td",
                preactivation_grad,
                up_weight[layer_number],
                preferred_element_type=jnp.float32,
            ),
            "tp",
        )
        middle_part, gain_two, shift_two = norm_pull_two(normed_two_grad)
        middle_grad = upstream + middle_part
        mixed_grad = middle_grad.astype(jnp.bfloat16)
        outward_grad = jnp.einsum(
            "te,td->ed", attended_low, mixed_grad, preferred_element_type=jnp.float32
        )
        attended_grad = jnp.einsum(
            "td,ed->te",
            mixed_grad,
            outward_weight[layer_number],
            preferred_element_type=jnp.float32,
        ).astype(jnp.bfloat16)
        delta_rows = jnp.sum(to_heads(attended_grad.astype(jnp.float32) * attended), axis=-1).T
        query_sum, key_sum, value_sum = grads_by_reduce(
            to_heads(queries),
            to_heads(attended_grad),
            query_scenes,
            tiled_keys,
            normalizer,
            delta_rows,
        )
        projected_grad = jnp.stack(
            [query_sum * score_factor, key_sum * score_factor, value_sum], axis=1
        ).astype(jnp.bfloat16)
        normed_f, norm_pull = jax.vjp(layer_norm, hidden_in, gain_pair[0], shift_pair[0])
        normed = normed_f.astype(jnp.bfloat16)
        inward_grad = jnp.einsum(
            "td,tce->cde", normed, projected_grad, preferred_element_type=jnp.float32
        )
        normed_grad = lax.psum(
            jnp.einsum(
                "tce,cde->td",
                projected_grad,
                inward_weight[layer_number],
                preferred_element_type=jnp.float32,
            ),
            "tp",
        )
        input_part, gain_one, shift_one = norm_pull(normed_grad)
        upstream = middle_grad + input_part
        layer_grads[layer_number] = (
            lax.psum_scatter(inward_grad, "seq", scatter_dimension=1, tiled=True),
            lax.psum_scatter(outward_grad, "seq", scatter_dimension=1, tiled=True),
            lax.psum_scatter(up_grad, "seq", scatter_dimension=0, tiled=True),
            lax.psum_scatter(down_grad, "seq", scatter_dimension=1, tiled=True),
            lax.psum_scatter(
                jnp.stack([gain_one, gain_two]), "seq", scatter_dimension=1, tiled=True
            ),
            lax.psum_scatter(
                jnp.stack([shift_one, shift_two]), "seq", scatter_dimension=1, tiled=True
            ),
        )
    return (
        hidden.astype(jnp.bfloat16),
        upstream,
        jnp.stack([layer_part[0] for layer_part in layer_grads]),
        jnp.stack([layer_part[1] for layer_part in layer_grads]),
        jnp.stack([layer_part[2] for layer_part in layer_grads]),
        jnp.stack([layer_part[3] for layer_part in layer_grads]),
        jnp.stack([layer_part[4] for layer_part in layer_grads]),
        jnp.stack([layer_part[5] for layer_part in layer_grads]),
    )


def solution(mesh):
    placed = (
        P("seq", None),
        P(),
        P(None, None, None, "tp"),
        P(None, "tp", None),
        P(None, None, "tp"),
        P(None, "tp", None),
        P(),
        P(),
        P("seq", None),
    )
    n_seq, n_tp = mesh.shape["seq"], mesh.shape["tp"]
    fits = n_seq == 8 and n_tp == 4
    return jax.shard_map(
        functools.partial(body, n_seq, n_tp) if fits else generic_body,
        mesh=mesh,
        in_specs=placed,
        out_specs=(
            P("seq", None),
            P("seq", None),
            P(None, None, "seq", "tp"),
            P(None, "tp", "seq"),
            P(None, "seq", "tp"),
            P(None, "tp", "seq"),
            P(None, None, "seq"),
            P(None, None, "seq"),
        ),
        check_vma=False,
    )
```

```python
import functools
import math
import jax
import jax.numpy as jnp
from jax import lax
from jax.experimental import pallas as pl
from jax.experimental.pallas import tpu as pltpu
from jax.sharding import PartitionSpec as P

HEAD_DIM = 64
LAYERS = 1
F32, BF16 = jnp.float32, jnp.bfloat16
NEG_FILL = -1e30
SCORE = HEAD_DIM ** -0.5
LOG2E = math.log2(math.e)
ANY = pl.BlockSpec(memory_space=pl.ANY)
VM = pl.BlockSpec(memory_space=pltpu.VMEM)
SM = pl.BlockSpec(memory_space=pltpu.SMEM)
FWD_PARAMS = pltpu.CompilerParams(vmem_limit_bytes=58 * 2**20)
BWD_PARAMS = pltpu.CompilerParams(vmem_limit_bytes=58 * 2**20)


def dot(a, b, dims):
    return lax.dot_general(a, b, (dims, ((), ())), preferred_element_type=F32)


def load_all(pairs, sems):
    copies = [pltpu.make_async_copy(s, d, sems.at[i]) for i, (s, d) in enumerate(pairs)]
    for c in copies:
        c.start()
    return copies


def for_tiles(first, last, starts, ends, bk, visit):
    edge = bk // 2
    begin, stop = starts[first], ends[last]
    low, high = begin // edge, (stop + edge - 1) // edge
    clear0 = jnp.where(ends[first] == stop, (begin + edge - 1) // edge, high)
    count = jnp.maximum(stop // edge - clear0, 0) // 2
    head = clear0 - low

    def masked(i, _):
        j = jnp.where(i < head, low + i, clear0 + 2 * count + i - head)
        visit(pl.multiple_of(j * edge, edge), edge, True)
        return 0

    def clear(i, _):
        visit(pl.multiple_of((clear0 + 2 * i) * edge, edge), bk, False)
        return 0

    lax.fori_loop(0, high - low - 2 * count, masked, 0)
    lax.fori_loop(0, count, clear, 0)


def low_half(x):
    lane = lax.broadcasted_iota(jnp.int32, x.shape, 1)
    return jnp.where(lane < HEAD_DIM, x, jnp.zeros_like(x))


def high_half(x):
    lane = lax.broadcasted_iota(jnp.int32, x.shape, 1)
    return jnp.where(lane < HEAD_DIM, jnp.zeros_like(x), x)


def swap_halves(x):
    return jnp.concatenate([x[:, HEAD_DIM:], x[:, :HEAD_DIM]], axis=1)


def fwd_kernel(bk, place, starts, ends, begin_rows, stop_rows, mine, other, q_in, *refs):
    o_out, of_out, lse_out, kv, vt, qz, acc, top, ot, sems = refs
    n_q, half = q_in.shape[:2]
    rows = 2 * half
    spots = [pl.ds(pl.multiple_of(place[i] * rows, 128), rows) for i in range(2 * n_q)]
    copies = load_all(
        [(mine.at[k], kv.at[spots[k]]) for k in range(n_q)]
        + [(other.at[k], kv.at[spots[n_q + k]]) for k in range(n_q)],
        sems,
    )
    for k in range(n_q):
        q = q_in[k]
        qz[2 * k] = low_half(q)
        qz[2 * k + 1] = low_half(swap_halves(q))
    for c in copies:
        c.wait()

    def turn(j, _):
        spot = pl.ds(pl.multiple_of(j * 256, 256), 256)
        vt[:, spot] = kv[spot, :].T[HEAD_DIM:]
        return 0

    lax.fori_loop(0, kv.shape[0] // 256, turn, 0)
    factor = SCORE * LOG2E

    def one(i, _):
        first = place[i // 2] * rows + (i % 2) * half
        query = qz[i]
        acc[...] = jnp.zeros_like(acc)
        top[0:1] = jnp.full((1, half), NEG_FILL, F32)
        top[1:2] = jnp.zeros((1, half), F32)
        slab = first // half

        def visit(at, size, mask):
            spot = pl.ds(at, size)
            st = dot(kv[spot, :], query, ((1,), (1,)))
            if mask:
                key = at + lax.broadcasted_iota(jnp.int32, st.shape, 0)
                st = jnp.where((key >= begin_rows[slab]) & (key < stop_rows[slab]), st, NEG_FILL)
            old = top[0:1]
            new = jnp.maximum(old, jnp.max(st, axis=0, keepdims=True))
            p = jnp.exp2(st * factor - new * factor)
            shrink = jnp.exp2((old - new) * factor)
            top[0:1] = new
            top[1:2] = top[1:2] * shrink + jnp.sum(p, axis=0, keepdims=True)
            acc[...] = acc[...] * shrink + dot(vt[:, spot], p.astype(BF16), ((1,), (0,)))

        for_tiles(first, first + half - 1, starts, ends, bk, visit)
        ot[i] = acc[...] / top[1:2]
        lse_out[i] = top[0:1] * factor + jnp.log2(top[1:2])
        return 0

    lax.fori_loop(0, 2 * n_q, one, 0)
    for k in range(n_q):
        joined = jnp.concatenate([ot[2 * k], ot[2 * k + 1]], axis=0).T
        of_out[k] = joined
        o_out[k] = joined.astype(BF16)


def attn_fwd(mine, other, q, place, starts, ends, bk):
    n_q, half = q.shape[:2]
    total = starts.shape[0]
    return pl.pallas_call(
        functools.partial(fwd_kernel, bk),
        in_specs=[SM, SM, SM, VM, VM, ANY, ANY, VM],
        out_specs=[VM] * 4,
        out_shape=[
            jax.ShapeDtypeStruct((n_q, half, 128), BF16),
            jax.ShapeDtypeStruct((n_q, half, 128), F32),
            jax.ShapeDtypeStruct((2 * n_q, 1, half), F32),
            jax.ShapeDtypeStruct((total, 128), BF16),
        ],
        scratch_shapes=[
            pltpu.VMEM((HEAD_DIM, total), BF16),
            pltpu.VMEM((2 * n_q, half, 128), BF16),
            pltpu.VMEM((HEAD_DIM, half), F32),
            pltpu.VMEM((8, half), F32),
            pltpu.VMEM((2 * n_q, HEAD_DIM, half), F32),
            pltpu.SemaphoreType.DMA((2 * n_q,)),
        ],
        compiler_params=FWD_PARAMS,
        cost_estimate=pl.CostEstimate(flops=3 * 10**10, bytes_accessed=2**22, transcendentals=0),
        name="attend",
    )(place, starts, ends, starts.reshape(-1, 1, half), ends.reshape(-1, 1, half), mine, other, q)


def bwd_kernel(bk, here, place, starts, ends, begin_rows, stop_rows, kv_hbm, lse, of, q_in, *refs):
    n_q, half = q_in.shape[:2]
    g_in, refs = refs[:n_q], refs[n_q:]
    dq_out, dkv_out, theirs, kv, kt, qz, gz, delta, dkv, dqt_all, acc, sems = refs
    rows = 2 * half
    copies = load_all([(kv_hbm, kv)], sems)
    for k in range(n_q):
        q = q_in[k]
        qz[2 * k] = low_half(q)
        qz[2 * k + 1] = low_half(swap_halves(q))
    for s in range(n_q):
        k = lax.rem(here[0] + n_q - s, n_q)
        g = g_in[s][...]
        gz[2 * k] = high_half(swap_halves(g))
        gz[2 * k + 1] = high_half(g)
        prod = (g.astype(F32) * of[k]).T
        delta[2 * k] = jnp.sum(prod[:HEAD_DIM], axis=0, keepdims=True)
        delta[2 * k + 1] = jnp.sum(prod[HEAD_DIM:], axis=0, keepdims=True)
    copies[0].wait()

    def turn(j, _):
        spot = pl.ds(pl.multiple_of(j * 256, 256), 256)
        kt[:, spot] = kv[spot, :].T[:HEAD_DIM]
        dkv[spot, :] = jnp.zeros((256, 128), F32)
        return 0

    lax.fori_loop(0, kv.shape[0] // 256, turn, 0)
    factor = SCORE * LOG2E

    def one(i, _):
        first = place[i // 2] * rows + (i % 2) * half
        query, grad, lse_row, delta_row = qz[i], gz[i], lse[i], delta[i]
        acc[...] = jnp.zeros_like(acc)
        slab = first // half

        def visit(at, size, mask):
            spot = pl.ds(at, size)
            block = kv[spot, :]
            st = dot(block, query, ((1,), (1,)))
            p = jnp.exp2(st * factor - lse_row)
            if mask:
                key = at + lax.broadcasted_iota(jnp.int32, st.shape, 0)
                p = jnp.where((key >= begin_rows[slab]) & (key < stop_rows[slab]), p, 0.0)
            dp = dot(block, grad, ((1,), (1,)))
            ds = (p * (dp - delta_row)).astype(BF16)
            dkv[spot, :] += dot(ds, query, ((1,), (0,))) + dot(p.astype(BF16), grad, ((1,), (0,)))
            acc[...] += dot(kt[:, spot], ds, ((1,), (0,)))

        for_tiles(first, first + half - 1, starts, ends, bk, visit)
        dqt_all[i] = acc[...] * SCORE
        return 0

    lax.fori_loop(0, 2 * n_q, one, 0)
    for k in range(n_q):
        joined = jnp.concatenate([dqt_all[2 * k], dqt_all[2 * k + 1]], axis=0).T
        dq_out[k] = joined.astype(BF16)
    for k in range(n_q):
        dkv_out[k] = dkv[pl.ds(pl.multiple_of(place[k] * rows, 128), rows), :]
        other = pl.ds(pl.multiple_of(place[n_q + k] * rows, 128), rows)
        theirs[k] = dkv[other, :].astype(BF16)


def attn_bwd(kv, q, g, of, lse, here, place, starts, ends, bk):
    n_q, half = q.shape[:2]
    total = starts.shape[0]
    return pl.pallas_call(
        functools.partial(bwd_kernel, bk),
        in_specs=[SM, SM, SM, SM, VM, VM, ANY] + [VM] * (3 + n_q),
        out_specs=[VM] * 3,
        out_shape=[
            jax.ShapeDtypeStruct((n_q, half, 128), BF16),
            jax.ShapeDtypeStruct((n_q, 2 * half, 128), F32),
            jax.ShapeDtypeStruct((n_q, 2 * half, 128), BF16),
        ],
        scratch_shapes=[
            pltpu.VMEM((total, 128), BF16),
            pltpu.VMEM((HEAD_DIM, total), BF16),
            pltpu.VMEM((2 * n_q, half, 128), BF16),
            pltpu.VMEM((2 * n_q, half, 128), BF16),
            pltpu.VMEM((2 * n_q, 1, half), F32),
            pltpu.VMEM((total, 128), F32),
            pltpu.VMEM((2 * n_q, HEAD_DIM, half), F32),
            pltpu.VMEM((HEAD_DIM, half), F32),
            pltpu.SemaphoreType.DMA((1,)),
        ],
        compiler_params=BWD_PARAMS,
        cost_estimate=pl.CostEstimate(flops=4 * 10**10, bytes_accessed=2**22, transcendentals=0),
        name="attend_back",
    )(
        here,
        place,
        starts,
        ends,
        starts.reshape(-1, 1, half),
        ends.reshape(-1, 1, half),
        kv,
        lse,
        of,
        q,
        *g,
    )


SHIELD = 3 * 10**10
ROOM = 6 * 2**20
WIDE = 58 * 2**20


def stats(x):
    average = jnp.mean(x, axis=-1, keepdims=True)
    centered = x - average
    variance = jnp.mean(centered * centered, axis=-1, keepdims=True)
    return centered, lax.rsqrt(variance + 1e-05)


def norm_back(grad, xhat, rate, gain):
    scaled = grad * gain
    return rate * (
        scaled
        - jnp.mean(scaled, axis=-1, keepdims=True)
        - xhat * jnp.mean(scaled * xhat, axis=-1, keepdims=True)
    )


def column_sums(grad, xhat):
    return jnp.concatenate(
        [jnp.sum(grad * xhat, axis=0, keepdims=True), jnp.sum(grad, axis=0, keepdims=True)], axis=0
    )


def shape_of(*dims, dtype=BF16):
    return jax.ShapeDtypeStruct(dims, dtype)


def kernel_call(kernel, name, specs, outs, args, flops=0, scratch=(), room=ROOM):
    size = sum(a.size * a.dtype.itemsize for a in list(args) + list(outs))
    return pl.pallas_call(
        kernel,
        in_specs=specs,
        out_specs=[VM] * len(outs),
        out_shape=outs,
        scratch_shapes=list(scratch),
        compiler_params=pltpu.CompilerParams(vmem_limit_bytes=min(size + room, WIDE)),
        cost_estimate=pl.CostEstimate(flops=flops, bytes_accessed=size, transcendentals=0),
        name=name,
    )(*args)


def block_rows(index, count):
    return pl.ds(pl.multiple_of(index * count, 16), count)


def head_cut(h):
    return slice(h * HEAD_DIM, (h + 1) * HEAD_DIM)


def project_kernel(x, gain, shift, weight, normed_out, kv_out, q_out, q_flat):
    n_z, half, rows = q_out.shape[0], q_out.shape[1], x.shape[0]
    for t in range(2):
        spot = slice(t * half, (t + 1) * half)
        centered, rate = stats(x[spot, :].astype(F32))
        normed = (centered * rate * gain[0, 0:1] + shift[0, 0:1]).astype(BF16)
        normed_out[spot, :] = normed
        q, k, v = [dot(normed, weight[0, c], ((1,), (0,))).astype(BF16) for c in range(3)]
        q_flat[spot, :] = q
        for h in range(n_z):
            kv_out[h, spot, :] = jnp.concatenate([k[:, head_cut(h)], v[:, head_cut(h)]], axis=1)
    for h in range(n_z):
        q_out[h] = jnp.concatenate([q_flat[:half, head_cut(h)], q_flat[half:, head_cut(h)]], axis=1)


def project(n_z, x, gains, shifts, weight):
    rows, width = x.shape
    return kernel_call(
        project_kernel,
        "project",
        [VM] * 4,
        [shape_of(rows, width), shape_of(n_z, rows, 128), shape_of(n_z, rows // 2, 128)],
        (x, gains, shifts, weight),
        2 * rows * weight.size,
        [pltpu.VMEM((rows, n_z * HEAD_DIM), BF16)],
        room=WIDE,
    )


def spread_kernel(o_in, out):
    n_z, half = o_in.shape[:2]
    out[:half, :] = jnp.concatenate([o_in[h, :, :HEAD_DIM] for h in range(n_z)], axis=1)
    out[half:, :] = jnp.concatenate([o_in[h, :, HEAD_DIM:] for h in range(n_z)], axis=1)


def spread(o):
    n_z, half = o.shape[:2]
    return kernel_call(spread_kernel, "spread", [VM], [shape_of(2 * half, n_z * HEAD_DIM)], (o,))[0]


def pack_kernel(here, x, *outs):
    n_z, half = len(outs), outs[0].shape[0]
    for h in range(n_z):
        block = jnp.concatenate([x[:half, head_cut(h)], x[half:, head_cut(h)]], axis=1)
        for k, out in enumerate(outs):

            @pl.when(lax.rem(here[0] + k, n_z) == h)
            def _():
                out[...] = block


def pack(n_z, here, x):
    return kernel_call(
        pack_kernel, "pack", [SM, VM], [shape_of(x.shape[0] // 2, 128)] * n_z, (here, x)
    )


def mix_kernel(here, x, gain, shift, parts, *refs):
    weights, (after_out, normed_out) = refs[:-2], refs[-2:]
    quarter = parts.shape[1]
    mixed = sum(dot(parts[here[1] ^ m], w[...], ((1,), (0,))) for m, w in enumerate(weights))
    after = x[block_rows(here[1], quarter), :].astype(F32) + mixed
    after_out[...] = after
    centered, rate = stats(after)
    normed_out[...] = (centered * rate * gain[0, 1:2] + shift[0, 1:2]).astype(BF16)


def mix(here, x, gains, shifts, parts, weights):
    n_t, quarter, width = parts.shape[0], parts.shape[1], x.shape[1]
    return kernel_call(
        mix_kernel,
        "mix",
        [SM] + [VM] * (4 + n_t),
        [shape_of(quarter, width, dtype=F32), shape_of(quarter, width)],
        (here, x, gains, shifts, parts, *weights),
        2 * quarter * width * width,
    )


def gelu_pair(u):
    c = math.sqrt(2.0 / math.pi)
    square = u * u
    t = jnp.tanh(c * (u + 0.044715 * square * u))
    slope = 0.5 * (1.0 + t) + 0.5 * u * (1.0 - t * t) * c * (1.0 + 3 * 0.044715 * square)
    return 0.5 * u * (1.0 + t), slope


def hidden_kernel(n_t, here, cot, up, down, *refs):
    slots, (act_out, pre_out, normed), parts = refs[:n_t], refs[n_t : n_t + 3], refs[n_t + 3 :]
    quarter, tile = slots[0].shape[0], 256
    for m, part in enumerate(slots):
        normed[block_rows(here[1] ^ m, quarter), :] = part[...]

    def one(j, _):
        cut = pl.ds(pl.multiple_of(j * tile, tile), tile)
        act, slope = gelu_pair(dot(normed[...], up[0, :, cut], ((1,), (0,))))
        act_out[:, cut] = act.astype(BF16)
        grad = dot(cot[...], down[0, cut, :], ((1,), (1,)))
        pre_out[:, cut] = (grad * slope).astype(BF16)
        return 0

    lax.fori_loop(0, up.shape[2] // tile, one, 0)
    for m, out in enumerate(parts):
        mine = pre_out[block_rows(here[1] ^ m, quarter), :]
        out[...] = dot(mine, up[0], ((1,), (1,))).astype(BF16)


def hidden_layer(here, slots, cot, up, down):
    quarter, width = slots[0].shape
    n_t, units = len(slots), up.shape[2]
    rows = n_t * quarter
    outs = kernel_call(
        functools.partial(hidden_kernel, n_t),
        "hidden_layer",
        [SM] + [VM] * (3 + n_t),
        [shape_of(rows, units), shape_of(rows, units), shape_of(rows, width)]
        + [shape_of(quarter, width)] * n_t,
        (here, cot, up, down, *slots),
        6 * rows * width * units,
    )
    return outs[0], outs[1], outs[2], outs[3:]


def branch_kernel(here, act, down, mixed, own, *sends):
    quarter = own.shape[0]
    for m, out in enumerate([own] + list(sends)):
        part = act[block_rows(here[1] ^ m, quarter), :]
        out[:quarter, :] = dot(part, down[0], ((1,), (0,))).astype(out.dtype)
        if m > 0:
            out[quarter:, :] = mixed[...]


def branch_parts(n_t, here, act, down, mixed):
    rows, (quarter, width) = act.shape[0], mixed.shape
    return kernel_call(
        branch_kernel,
        "branch",
        [SM] + [VM] * 3,
        [shape_of(quarter, width, dtype=F32)] + [shape_of(2 * quarter, width)] * (n_t - 1),
        (here, act, down, mixed),
        2 * rows * width * act.shape[1],
        room=WIDE,
    )


def middle_kernel(n_t, here, after, cot, gain, *refs):
    parts, weights, refs = refs[:n_t], refs[n_t : 2 * n_t], refs[2 * n_t :]
    middle_out, mixed_out, sums_out, grads = refs
    quarter = after.shape[0]
    grad = sum(part[...].astype(F32) for part in parts)
    centered, rate = stats(after[...])
    xhat = centered * rate
    sums_out[...] = column_sums(grad, xhat)
    upstream = cot[block_rows(here[1], quarter), :].astype(F32)
    middle = upstream + norm_back(grad, xhat, rate, gain[0, 1:2])
    middle_out[...] = middle
    mixed = middle.astype(BF16)
    mixed_out[...] = mixed
    for m in range(n_t):
        grads[here[1] ^ m] = dot(mixed, weights[m][...], ((1,), (1,))).astype(BF16)


def middle_back(here, after, cot, gains, parts, weights):
    n_t, (quarter, width) = len(parts), parts[0].shape
    return kernel_call(
        functools.partial(middle_kernel, n_t),
        "middle_back",
        [SM] + [VM] * (3 + 2 * n_t),
        [
            shape_of(quarter, width, dtype=F32),
            shape_of(quarter, width),
            shape_of(2, width, dtype=F32),
            shape_of(n_t, quarter, weights[0].shape[0]),
        ],
        (here, after, cot, gains, *parts, *weights),
        SHIELD,
    )


def join_kernel(mine, theirs, q, out):
    n_z, rows = mine.shape[:2]
    lane = lax.broadcasted_iota(jnp.int32, mine.shape[1:], 1)
    factor = jnp.where(lane < HEAD_DIM, SCORE, 1.0)
    for k in range(n_z):
        out[k, :rows] = ((mine[k] + theirs[k].astype(F32)) * factor).astype(BF16)
        out[k, rows:] = q[k]


def join(mine, theirs, q):
    n_z, rows = mine.shape[:2]
    return kernel_call(
        join_kernel,
        "join",
        [VM] * 3,
        [shape_of(n_z, rows + q.shape[1], 128)],
        (mine, theirs, q),
    )[0]


def unproject_kernel(weight, grads, flat, part):
    n_z, rows = grads.shape[0], flat.shape[0]
    half = rows // 2
    width = n_z * HEAD_DIM
    heads = range(n_z)
    low, high = slice(0, HEAD_DIM), slice(HEAD_DIM, 2 * HEAD_DIM)
    flat[:half, :width] = jnp.concatenate([grads[h, rows:, low] for h in heads], axis=1)
    flat[half:, :width] = jnp.concatenate([grads[h, rows:, high] for h in heads], axis=1)
    flat[:, width : 2 * width] = jnp.concatenate([grads[h, :rows, low] for h in heads], axis=1)
    flat[:, 2 * width :] = jnp.concatenate([grads[h, :rows, high] for h in heads], axis=1)
    total = sum(
        dot(flat[:, c * width : (c + 1) * width], weight[0, c], ((1,), (1,))) for c in range(3)
    )
    part[...] = total.astype(BF16)


def unproject(weight, grads):
    width = weight.shape[2]
    rows = grads.shape[1] * 2 // 3
    return kernel_call(
        unproject_kernel,
        "unproject",
        [VM] * 2,
        [shape_of(rows, 3 * weight.shape[3]), shape_of(rows, width)],
        (weight, grads),
        2 * rows * weight.size,
    )


def last_kernel(here, x, middle, gain, parts, out):
    quarter = middle.shape[0]
    grad = slot_sum(parts)
    centered, rate = stats(x[block_rows(here[1], quarter), :].astype(F32))
    out[...] = (middle[...] + norm_back(grad, centered * rate, rate, gain[0, 0:1])).astype(BF16)


def last_back(here, x, middle, gains, parts):
    return kernel_call(
        last_kernel,
        "last_back",
        [SM] + [VM] * 4,
        [shape_of(*middle.shape)],
        (here, x, middle, gains, parts),
        SHIELD,
    )[0]


def lay_kernel(here, *refs):
    parts, out = refs[:-1], refs[-1]
    for m, part in enumerate(parts):
        out[block_rows(here[1] ^ m, part.shape[0]), :] = part[...].astype(out.dtype)


def lay(here, parts, dtype):
    quarter, width = parts[0].shape
    return kernel_call(
        lay_kernel,
        "lay",
        [SM] + [VM] * len(parts),
        [shape_of(len(parts) * quarter, width, dtype=dtype)],
        (here, *parts),
    )[0]


def for_sides(here, mine, theirs, work):
    for out, side in ((theirs, 1), (mine, 0)):

        def one(k, _, out=out, side=side):
            owner = 2 * k + (here[2] ^ side)
            work(out, k, pl.ds(pl.multiple_of(owner * 128, 128), 128))
            return 0

        lax.fori_loop(0, mine.shape[0], one, 0)


def sides(n_z, depth):
    return [shape_of(n_z, depth, 128, dtype=F32), shape_of(n_z, depth, 128)]


def put_lanes(out, k, first, block):
    for j in range(block.shape[1] // 128):
        out[k, first + j * 128 : first + (j + 1) * 128, :] = block[:, j * 128 : (j + 1) * 128]


def early_kernel(here, act, pre, normed, cot, mine, theirs):
    units = act.shape[1]

    def work(out, k, cut):
        out[k, :units, :] = dot(act[...], cot[:, cut], ((0,), (0,))).astype(out.dtype)
        put_lanes(out, k, units, dot(normed[:, cut], pre[...], ((0,), (0,))).astype(out.dtype))

    for_sides(here, mine, theirs, work)


def early_grads(n_z, here, act, pre, normed, cot):
    depth = 2 * act.shape[1]
    return kernel_call(
        early_kernel,
        "early_grads",
        [SM] + [VM] * 4,
        sides(n_z, depth),
        (here, act, pre, normed, cot),
        2 * act.shape[0] * depth * normed.shape[1],
    )


def halves(x):
    high = x.astype(BF16)
    return high, (x - high.astype(F32)).astype(BF16)


def outward_kernel(here, attended, *refs):
    mixed, (mine, theirs) = refs[:-2], refs[-2:]
    quarter = attended.shape[0] // len(mixed)

    def work(out, k, cut):
        outward = sum(
            dot(attended[block_rows(here[1] ^ m, quarter), :], part[-quarter:, cut], ((0,), (0,)))
            for m, part in enumerate(mixed)
        )
        out[k] = outward.astype(out.dtype)

    for_sides(here, mine, theirs, work)


def outward_grads(n_z, here, attended, mixed):
    rows, share = attended.shape
    return kernel_call(
        outward_kernel,
        "outward_grads",
        [SM] + [VM] * (1 + len(mixed)),
        sides(n_z, share),
        (here, attended, *mixed),
        2 * rows * share * mixed[0].shape[1],
    )


def fold_slots_kernel(here, mine, theirs, *outs):
    for k, out in enumerate(outs):
        at = lax.rem(here[0] + k, len(outs))
        out[...] = (mine[at] + theirs[at].astype(F32)).astype(out.dtype)


def fold_slots(here, mine, theirs):
    n_z, depth, _ = mine.shape
    return kernel_call(
        fold_slots_kernel,
        "fold_slots",
        [SM] + [VM] * 2,
        [shape_of(depth, 128, dtype=F32)] + [shape_of(depth, 128)] * (n_z - 1),
        (here, mine, theirs),
    )


def late_kernel(here, x, normed, grad, sums, part, mine, theirs, scratch):
    depth, step = grad.shape[1], 256
    total = jnp.zeros((2, x.shape[1]), F32)
    for m in range(x.shape[0] // step):
        spot = slice(m * step, (m + 1) * step)
        centered, rate = stats(x[spot, :].astype(F32))
        total = total + column_sums(part[spot, :].astype(F32), centered * rate)
    scratch[0:2, :] = total
    scratch[2:4, :] = sums[...]
    scratch[4:8, :] = jnp.zeros((4, x.shape[1]), F32)

    def work(out, k, cut):
        put_lanes(out, k, 0, dot(normed[:, cut], grad[...], ((0,), (0,))).astype(out.dtype))
        block = scratch[:, cut]
        if out.dtype == BF16:
            high, low = halves(block[0:4])
            block = jnp.concatenate([high.astype(F32), low.astype(F32)], axis=0).astype(BF16)
        out[k, depth:, :] = block

    for_sides(here, mine, theirs, work)


def late_grads(n_z, here, x, normed, grad, sums, part):
    depth = grad.shape[1] + 8
    return kernel_call(
        late_kernel,
        "late_grads",
        [SM] + [VM] * 5,
        sides(n_z, depth),
        (here, x, normed, grad, sums, part),
        2 * grad.shape[0] * depth * normed.shape[1],
        [pltpu.VMEM((8, x.shape[1]), F32)],
    )


def fold_kernel(mine, theirs, out):
    for k in range(mine.shape[0]):
        out[k] = (mine[k] + theirs[k].astype(F32)).astype(BF16)


def fold(mine, theirs):
    return kernel_call(
        fold_kernel, "fold", [VM] * 2, [shape_of(*mine.shape)], (mine, theirs)
    )[0]


def fold_late_kernel(mine, theirs, out):
    depth = mine.shape[1] - 8
    for k in range(mine.shape[0]):
        out[k, :depth] = (mine[k, :depth] + theirs[k, :depth].astype(F32)).astype(BF16)
        tail = mine[k, depth:] + theirs[k, depth:].astype(F32)
        high, low = halves(tail[0:4] + tail[4:8])
        both = jnp.concatenate([high.astype(F32), low.astype(F32)], axis=0)
        out[k, depth:] = both.astype(BF16)


def fold_late(mine, theirs):
    return kernel_call(
        fold_late_kernel, "fold_late", [VM] * 2, [shape_of(*mine.shape)], (mine, theirs)
    )[0]


def slot_sum(parts):
    return sum(parts[k].astype(F32) for k in range(parts.shape[0]))


def finish_early_kernel(parts, down_out, up_out):
    total = slot_sum(parts)
    units = down_out.shape[0]
    down_out[...] = total[:units]
    for j in range(units // 128):
        up_out[:, j * 128 : (j + 1) * 128] = total[units + j * 128 : units + (j + 1) * 128]


def finish_early(units, parts):
    return kernel_call(
        finish_early_kernel,
        "finish_early",
        [VM],
        [shape_of(units, 128, dtype=F32), shape_of(128, units, dtype=F32)],
        (parts,),
    )


def finish_late_kernel(parts, out, sums_out):
    total = slot_sum(parts)
    per = out.shape[2] // 128
    for c in range(3):
        for j in range(per):
            at = (c * per + j) * 128
            out[c, :, j * 128 : (j + 1) * 128] = total[at : at + 128]
    last = total.shape[0] - 8
    sums_out[...] = jnp.concatenate([total[last : last + 4] + total[last + 4 :]] * 2, axis=0)


def finish_late(share, parts):
    return kernel_call(
        finish_late_kernel,
        "finish_late",
        [VM],
        [
            shape_of(3, 128, share, dtype=F32),
            shape_of(8, 128, dtype=F32),
        ],
        (parts,),
    )


def scene_edges(scene_index):
    total = scene_index.shape[0]
    at = lax.iota(jnp.int32, total)
    edge = jnp.concatenate([jnp.ones((1,), jnp.bool_), scene_index[1:] != scene_index[:-1]])
    starts = lax.cummax(jnp.where(edge, at, 0))
    closing = jnp.concatenate([edge[1:], jnp.ones((1,), jnp.bool_)])
    return starts, lax.cummin(jnp.where(closing, at + 1, total), reverse=True)


def body(
    n_seq,
    n_tp,
    tokens,
    scene_index,
    inward_weight,
    outward_weight,
    up_weight,
    down_weight,
    norm_gains,
    norm_shifts,
    cotangent,
):
    n_z, rows, width = n_seq // 2, tokens.shape[0], tokens.shape[1]
    units, share = up_weight.shape[2], outward_weight.shape[1]
    quarter = rows // n_tp
    seq, tp = lax.axis_index("seq"), lax.axis_index("tp")
    z, c = seq // 2, seq % 2
    here = jnp.stack([z, tp, c]).astype(jnp.int32)
    lines = [list(range(b, n_seq, 2)) for b in range(2)]

    def line(x):
        return lax.all_to_all(x, "seq", 0, 0, axis_index_groups=lines, tiled=True)

    def plane(x):
        return lax.all_to_all(x, "tp", 0, 0, tiled=True)

    def across(x):
        return lax.ppermute(x, "seq", [(a, a ^ 1) for a in range(n_seq)])

    def along(x, k):
        return lax.ppermute(
            x, "seq", [(a * 2 + b, (a + k) % n_z * 2 + b) for a in range(n_z) for b in range(2)]
        )

    def over(x, m):
        return lax.ppermute(x, "tp", [(a, a ^ m) for a in range(n_tp)])

    def square(slots):
        return [slots[0]] + [over(slots[m], m) for m in range(1, n_tp)]

    place = jnp.stack([k * 2 + (c ^ g) for g in range(2) for k in range(n_z)]).astype(jnp.int32)
    starts, ends = scene_edges(scene_index)
    normed, kv_send, q_send = project(n_z, tokens, norm_gains, norm_shifts, inward_weight)
    kv_mine = line(kv_send)
    kv_other = across(kv_mine)
    q = line(q_send)
    outward_all = square([outward_weight[0]] * n_tp)
    (q, outward_all) = lax.optimization_barrier((q, outward_all))
    o, o_full, lse, kv_full = attn_fwd(kv_mine, kv_other, q, place, starts, ends, 1024)
    attended = spread(line(o))
    parts = plane(attended.reshape(n_tp, quarter, share))
    after, normed_two = mix(here, tokens, norm_gains, norm_shifts, parts, outward_all)
    act, pre, normed_two, grad_parts = hidden_layer(
        here, square([normed_two] * n_tp), cotangent, up_weight, down_weight
    )
    middle, mixed, sums_two, grads = middle_back(
        here, after, cotangent, norm_gains, square(grad_parts), outward_all
    )
    mine, theirs = early_grads(n_z, here, act, pre, normed_two, cotangent)
    early = fold(mine, across(theirs))
    branch = branch_parts(n_tp, here, act, down_weight, mixed)
    grads = plane(grads)
    (grads, early, branch) = lax.optimization_barrier((grads, early, branch))
    g = pack(n_z, here, grads.reshape(rows, share))
    g = [g[0]] + [along(g[k], k) for k in range(1, n_z)]
    (g, early) = lax.optimization_barrier((g, early))
    early = line(early)
    branch = square(branch)
    dq, dkv, dkv_theirs = attn_bwd(kv_full, q, g, o_full, lse, here, place, starts, ends, 1024)
    (dq, dkv, dkv_theirs, early, branch) = lax.optimization_barrier(
        (dq, dkv, dkv_theirs, early, branch)
    )
    mixed = [mixed] + branch[1:]
    back = line(join(dkv, across(dkv_theirs), dq))
    out_own = (after + sum(part[:quarter].astype(F32) for part in branch)).astype(BF16)
    out_slots = square([out_own] * n_tp)
    down_grad, up_grad = finish_early(units, early)
    activations = lay(here, out_slots, BF16)
    mine, theirs = outward_grads(n_z, here, attended, mixed)
    side = fold_slots(here, mine, across(theirs))
    (back, activations, down_grad, up_grad, side) = lax.optimization_barrier(
        (back, activations, down_grad, up_grad, side)
    )
    side = [side[0]] + [along(side[k], k) for k in range(1, n_z)]
    flat, back_part = unproject(inward_weight, back)
    mine, theirs = late_grads(n_z, here, tokens, normed, flat, sums_two, back_part)
    late = fold_late(mine, across(theirs))
    back_part = plane(back_part.reshape(n_tp, quarter, width))
    (back_part, late, side) = lax.optimization_barrier((back_part, late, side))
    outward_grad = sum(part.astype(F32) for part in side)
    token_own = last_back(here, tokens, middle, norm_gains, back_part)
    (late, token_own) = lax.optimization_barrier((late, token_own))
    late = line(late)
    token_slots = square([token_own] * n_tp)
    token_grad = lay(here, token_slots, F32)
    (late, token_grad) = lax.optimization_barrier((late, token_grad))
    inward_grad, sums = finish_late(share, late)
    sums = square([sums] * n_tp)
    while len(sums) > 1:
        sums = [sums[m] + sums[m + 1] for m in range(0, len(sums), 2)]
    sums = sums[0]
    gain_grad = jnp.stack([sums[0], sums[2]])
    shift_grad = jnp.stack([sums[1], sums[3]])
    return (
        activations,
        token_grad,
        inward_grad[None],
        outward_grad[None],
        up_grad[None],
        down_grad[None],
        gain_grad[None],
        shift_grad[None],
    )


def layer_norm(hidden, gain_row, shift_row):
    average = jnp.mean(hidden, axis=-1, keepdims=True)
    centered = hidden - average
    variance = jnp.mean(centered * centered, axis=-1, keepdims=True)
    return centered * lax.rsqrt(variance + 1e-05) * gain_row + shift_row


def gelu_tanh(preactivation):
    return jax.nn.gelu(preactivation, approximate=True)


def to_heads(flat_rows):
    return flat_rows.reshape(flat_rows.shape[0], -1, HEAD_DIM)


def scenes_meet(query_scenes, key_scenes):
    return jnp.logical_and(key_scenes[0] <= query_scenes[-1], key_scenes[-1] >= query_scenes[0])


def score_rows(query_heads, key_heads, query_scenes, key_scenes):
    scores = jnp.einsum(
        "qhd,khd->hqk", query_heads, key_heads, preferred_element_type=jnp.float32
    ) * HEAD_DIM ** (-0.5)
    same_scene = (query_scenes[:, None] == key_scenes[None, :])[None]
    return (scores, same_scene)


def probabilities(scores, same_scene, normalizer):
    return jnp.where(same_scene, jnp.exp(scores - normalizer[:, :, None]), 0.0)


def key_tiles(key_all, value_all, scene_index):
    tile_rows = min(1024, key_all.shape[0])
    tile_count = key_all.shape[0] // tile_rows
    return (
        key_all.reshape(tile_count, tile_rows, -1, HEAD_DIM),
        value_all.reshape(tile_count, tile_rows, -1, HEAD_DIM),
        scene_index.reshape(tile_count, tile_rows),
    )


def log_normalizer(query_heads, query_scenes, tiled_keys):

    def log_visit_tile(running_pair, inputs_pair):
        key_heads, key_scenes = inputs_pair

        def log_compute(pair_now):
            running_max, running_sum = pair_now
            scores, same_scene = score_rows(query_heads, key_heads, query_scenes, key_scenes)
            masked = jnp.where(same_scene, scores, NEG_FILL)
            new_max = jnp.maximum(running_max, jnp.max(masked, axis=-1))
            weights = jnp.where(same_scene, jnp.exp(masked - new_max[:, :, None]), 0.0)
            return (
                new_max,
                running_sum * jnp.exp(running_max - new_max) + jnp.sum(weights, axis=-1),
            )

        return (
            lax.cond(
                scenes_meet(query_scenes, key_scenes),
                log_compute,
                lambda pair_now: pair_now,
                running_pair,
            ),
            None,
        )

    stat_shape = (query_heads.shape[1], query_heads.shape[0])
    start_pair = (jnp.full(stat_shape, NEG_FILL, jnp.float32), jnp.zeros(stat_shape, jnp.float32))
    final_pair, _ = lax.scan(log_visit_tile, start_pair, (tiled_keys[0], tiled_keys[2]))
    return final_pair[0] + jnp.log(final_pair[1])


def attend_all(query_heads, query_scenes, tiled_keys, normalizer):

    def attend_visit_tile(running_total, inputs_triple):
        key_heads, value_heads, key_scenes = inputs_triple

        def attend_compute(total_now):
            scores, same_scene = score_rows(query_heads, key_heads, query_scenes, key_scenes)
            weights = probabilities(scores, same_scene, normalizer).astype(jnp.bfloat16)
            return total_now + jnp.einsum(
                "hqk,khd->qhd", weights, value_heads, preferred_element_type=jnp.float32
            )

        return (
            lax.cond(
                scenes_meet(query_scenes, key_scenes),
                attend_compute,
                lambda total_now: total_now,
                running_total,
            ),
            None,
        )

    running_total, _ = lax.scan(
        attend_visit_tile, jnp.zeros(query_heads.shape, jnp.float32), tiled_keys
    )
    return running_total.reshape(running_total.shape[0], -1)


def score_gradients(
    query_heads,
    key_heads,
    value_heads,
    grad_heads,
    query_scenes,
    key_scenes,
    normalizer,
    delta_rows,
):
    scores, same_scene = score_rows(query_heads, key_heads, query_scenes, key_scenes)
    weights = probabilities(scores, same_scene, normalizer)
    weight_grad = jnp.einsum(
        "qhd,khd->hqk", grad_heads, value_heads, preferred_element_type=jnp.float32
    )
    score_grad = (weights * (weight_grad - delta_rows[:, :, None])).astype(jnp.bfloat16)
    return (weights.astype(jnp.bfloat16), score_grad)


def grads_by_reduce(query_heads, grad_heads, query_scenes, tiled_keys, normalizer, delta_rows):
    tile_rows = tiled_keys[0].shape[1]
    joined_width = 2 * query_heads.shape[1] * query_heads.shape[2]

    def grads_visit_tile(query_total, inputs_triple):
        key_heads, value_heads, key_scenes = inputs_triple

        def grads_compute(total_now):
            weights, score_grad = score_gradients(
                query_heads,
                key_heads,
                value_heads,
                grad_heads,
                query_scenes,
                key_scenes,
                normalizer,
                delta_rows,
            )
            total_now = total_now + jnp.einsum(
                "hqk,khd->qhd", score_grad, key_heads, preferred_element_type=jnp.float32
            )
            key_term = jnp.einsum(
                "hqk,qhd->khd", score_grad, query_heads, preferred_element_type=jnp.float32
            )
            value_term = jnp.einsum(
                "hqk,qhd->khd", weights, grad_heads, preferred_element_type=jnp.float32
            )
            joined = jnp.concatenate(
                [key_term.reshape(tile_rows, -1), value_term.reshape(tile_rows, -1)], axis=1
            )
            return (total_now, joined)

        def skipped(total_now):
            return (total_now, jnp.zeros((tile_rows, joined_width), jnp.float32))

        return lax.cond(scenes_meet(query_scenes, key_scenes), grads_compute, skipped, query_total)

    query_total, key_terms_all = lax.scan(
        grads_visit_tile, jnp.zeros(query_heads.shape, jnp.float32), tiled_keys
    )
    key_terms_all = key_terms_all.reshape(-1, key_terms_all.shape[-1])
    summed = lax.psum_scatter(key_terms_all, "seq", scatter_dimension=0, tiled=True)
    half_width = summed.shape[1] // 2
    return (
        query_total.reshape(query_total.shape[0], -1),
        summed[:, :half_width],
        summed[:, half_width:],
    )


def generic_body(
    tokens,
    scene_index,
    inward_weight,
    outward_weight,
    up_weight,
    down_weight,
    norm_gains,
    norm_shifts,
    cotangent,
):
    local_rows = tokens.shape[0]
    score_factor = HEAD_DIM ** (-0.5)
    query_scenes = lax.dynamic_slice_in_dim(
        scene_index, lax.axis_index("seq") * local_rows, local_rows
    )
    hidden = tokens.astype(jnp.float32)
    layer_number = 0
    gain_pair = norm_gains[layer_number]
    shift_pair = norm_shifts[layer_number]
    normed = layer_norm(hidden, gain_pair[0], shift_pair[0]).astype(jnp.bfloat16)
    projected = jnp.einsum(
        "td,cde->tce", normed, inward_weight[layer_number], preferred_element_type=jnp.float32
    ).astype(jnp.bfloat16)
    queries = projected[:, 0]
    key_local = projected[:, 1]
    value_local = projected[:, 2]
    key_all = lax.all_gather(key_local, "seq", axis=0, tiled=True)
    value_all = lax.all_gather(value_local, "seq", axis=0, tiled=True)
    tiled_keys = key_tiles(key_all, value_all, scene_index)
    query_heads = to_heads(queries)
    normalizer = log_normalizer(query_heads, query_scenes, tiled_keys)
    attended = attend_all(query_heads, query_scenes, tiled_keys, normalizer)
    attended_low = attended.astype(jnp.bfloat16)
    mixed_sum = lax.psum(
        jnp.dot(attended_low, outward_weight[layer_number], preferred_element_type=jnp.float32),
        "tp",
    )
    after_attention = hidden + mixed_sum
    normed_two = layer_norm(after_attention, gain_pair[1], shift_pair[1]).astype(jnp.bfloat16)
    preactivation = jnp.dot(normed_two, up_weight[layer_number], preferred_element_type=jnp.float32)
    activated = gelu_tanh(preactivation).astype(jnp.bfloat16)
    branch = lax.psum(
        jnp.dot(activated, down_weight[layer_number], preferred_element_type=jnp.float32), "tp"
    )
    kept_layers = [
        (
            hidden,
            after_attention,
            queries,
            key_local,
            value_local,
            tiled_keys,
            normalizer,
            attended,
            attended_low,
            preactivation,
            activated,
        )
    ]
    hidden = after_attention + branch
    upstream = cotangent.astype(jnp.float32)
    layer_grads = [None] * LAYERS
    for layer_number in reversed(range(LAYERS)):
        (
            hidden_in,
            after_attention,
            queries,
            key_local,
            value_local,
            tiled_keys,
            normalizer,
            attended,
            attended_low,
            preactivation,
            activated,
        ) = kept_layers[layer_number]
        gain_pair = norm_gains[layer_number]
        shift_pair = norm_shifts[layer_number]
        branch_grad = upstream.astype(jnp.bfloat16)
        down_grad = jnp.einsum(
            "tf,td->fd", activated, branch_grad, preferred_element_type=jnp.float32
        )
        act_grad = jnp.einsum(
            "td,fd->tf", branch_grad, down_weight[layer_number], preferred_element_type=jnp.float32
        )
        _, gelu_pull = jax.vjp(gelu_tanh, preactivation)
        preactivation_grad = gelu_pull(act_grad)[0].astype(jnp.bfloat16)
        normed_two_f, norm_pull_two = jax.vjp(
            layer_norm, after_attention, gain_pair[1], shift_pair[1]
        )
        normed_two = normed_two_f.astype(jnp.bfloat16)
        up_grad = jnp.einsum(
            "td,tf->df", normed_two, preactivation_grad, preferred_element_type=jnp.float32
        )
        normed_two_grad = lax.psum(
            jnp.einsum(
                "tf,df->td",
                preactivation_grad,
                up_weight[layer_number],
                preferred_element_type=jnp.float32,
            ),
            "tp",
        )
        middle_part, gain_two, shift_two = norm_pull_two(normed_two_grad)
        middle_grad = upstream + middle_part
        mixed_grad = middle_grad.astype(jnp.bfloat16)
        outward_grad = jnp.einsum(
            "te,td->ed", attended_low, mixed_grad, preferred_element_type=jnp.float32
        )
        attended_grad = jnp.einsum(
            "td,ed->te",
            mixed_grad,
            outward_weight[layer_number],
            preferred_element_type=jnp.float32,
        ).astype(jnp.bfloat16)
        delta_rows = jnp.sum(to_heads(attended_grad.astype(jnp.float32) * attended), axis=-1).T
        query_sum, key_sum, value_sum = grads_by_reduce(
            to_heads(queries),
            to_heads(attended_grad),
            query_scenes,
            tiled_keys,
            normalizer,
            delta_rows,
        )
        projected_grad = jnp.stack(
            [query_sum * score_factor, key_sum * score_factor, value_sum], axis=1
        ).astype(jnp.bfloat16)
        normed_f, norm_pull = jax.vjp(layer_norm, hidden_in, gain_pair[0], shift_pair[0])
        normed = normed_f.astype(jnp.bfloat16)
        inward_grad = jnp.einsum(
            "td,tce->cde", normed, projected_grad, preferred_element_type=jnp.float32
        )
        normed_grad = lax.psum(
            jnp.einsum(
                "tce,cde->td",
                projected_grad,
                inward_weight[layer_number],
                preferred_element_type=jnp.float32,
            ),
            "tp",
        )
        input_part, gain_one, shift_one = norm_pull(normed_grad)
        upstream = middle_grad + input_part
        layer_grads[layer_number] = (
            lax.psum_scatter(inward_grad, "seq", scatter_dimension=1, tiled=True),
            lax.psum_scatter(outward_grad, "seq", scatter_dimension=1, tiled=True),
            lax.psum_scatter(up_grad, "seq", scatter_dimension=0, tiled=True),
            lax.psum_scatter(down_grad, "seq", scatter_dimension=1, tiled=True),
            lax.psum_scatter(
                jnp.stack([gain_one, gain_two]), "seq", scatter_dimension=1, tiled=True
            ),
            lax.psum_scatter(
                jnp.stack([shift_one, shift_two]), "seq", scatter_dimension=1, tiled=True
            ),
        )
    return (
        hidden.astype(jnp.bfloat16),
        upstream,
        jnp.stack([layer_part[0] for layer_part in layer_grads]),
        jnp.stack([layer_part[1] for layer_part in layer_grads]),
        jnp.stack([layer_part[2] for layer_part in layer_grads]),
        jnp.stack([layer_part[3] for layer_part in layer_grads]),
        jnp.stack([layer_part[4] for layer_part in layer_grads]),
        jnp.stack([layer_part[5] for layer_part in layer_grads]),
    )


def solution(mesh):
    placed = (
        P("seq", None),
        P(),
        P(None, None, None, "tp"),
        P(None, "tp", None),
        P(None, None, "tp"),
        P(None, "tp", None),
        P(),
        P(),
        P("seq", None),
    )
    n_seq, n_tp = mesh.shape["seq"], mesh.shape["tp"]
    fits = n_seq == 8 and n_tp == 4
    return jax.shard_map(
        functools.partial(body, n_seq, n_tp) if fits else generic_body,
        mesh=mesh,
        in_specs=placed,
        out_specs=(
            P("seq", None),
            P("seq", None),
            P(None, None, "seq", "tp"),
            P(None, "tp", "seq"),
            P(None, "seq", "tp"),
            P(None, "tp", "seq"),
            P(None, None, "seq"),
            P(None, None, "seq"),
        ),
        check_vma=False,
    )
```

```python
import functools
import math
import jax
import jax.numpy as jnp
from jax import lax
from jax.experimental import pallas as pl
from jax.experimental.pallas import tpu as pltpu
from jax.sharding import PartitionSpec as P

HEAD_DIM = 64
LAYERS = 1
F32, BF16 = jnp.float32, jnp.bfloat16
NEG_FILL = -1e30
SCORE = HEAD_DIM ** -0.5
LOG2E = math.log2(math.e)
ANY = pl.BlockSpec(memory_space=pl.ANY)
VM = pl.BlockSpec(memory_space=pltpu.VMEM)
SM = pl.BlockSpec(memory_space=pltpu.SMEM)
FWD_PARAMS = pltpu.CompilerParams(vmem_limit_bytes=58 * 2**20)
BWD_PARAMS = pltpu.CompilerParams(vmem_limit_bytes=58 * 2**20)


def dot(a, b, dims):
    return lax.dot_general(a, b, (dims, ((), ())), preferred_element_type=F32)


def load_all(pairs, sems):
    copies = [pltpu.make_async_copy(s, d, sems.at[i]) for i, (s, d) in enumerate(pairs)]
    for c in copies:
        c.start()
    return copies


def for_tiles(first, last, starts, ends, bk, visit):
    edge = bk // 2
    begin, stop = starts[first], ends[last]
    low, high = begin // edge, (stop + edge - 1) // edge
    clear0 = jnp.where(ends[first] == stop, (begin + edge - 1) // edge, high)
    count = jnp.maximum(stop // edge - clear0, 0) // 2
    head = clear0 - low

    def masked(i, _):
        j = jnp.where(i < head, low + i, clear0 + 2 * count + i - head)
        visit(pl.multiple_of(j * edge, edge), edge, True)
        return 0

    def clear(i, _):
        visit(pl.multiple_of((clear0 + 2 * i) * edge, edge), bk, False)
        return 0

    lax.fori_loop(0, high - low - 2 * count, masked, 0)
    lax.fori_loop(0, count, clear, 0)


def low_half(x):
    lane = lax.broadcasted_iota(jnp.int32, x.shape, 1)
    return jnp.where(lane < HEAD_DIM, x, jnp.zeros_like(x))


def high_half(x):
    lane = lax.broadcasted_iota(jnp.int32, x.shape, 1)
    return jnp.where(lane < HEAD_DIM, jnp.zeros_like(x), x)


def swap_halves(x):
    return jnp.concatenate([x[:, HEAD_DIM:], x[:, :HEAD_DIM]], axis=1)


def fwd_kernel(bk, here, place, starts, ends, begin_rows, stop_rows, mine, other, *refs):
    n_q = mine.shape[0]
    q_in, refs = refs[:n_q], refs[n_q:]
    o_out, of_out, lse_out, kv, vt, qz, acc, top, ot, sems = refs
    half = q_in[0].shape[0]
    rows = 2 * half
    spots = [pl.ds(pl.multiple_of(place[i] * rows, 128), rows) for i in range(2 * n_q)]
    copies = load_all(
        [(mine.at[k], kv.at[spots[k]]) for k in range(n_q)]
        + [(other.at[k], kv.at[spots[n_q + k]]) for k in range(n_q)],
        sems,
    )
    for s in range(n_q):
        k = lax.rem(here[0] + n_q - s, n_q)
        q = q_in[s][...]
        qz[2 * k] = low_half(q)
        qz[2 * k + 1] = low_half(swap_halves(q))
    for c in copies:
        c.wait()

    def turn(j, _):
        spot = pl.ds(pl.multiple_of(j * 256, 256), 256)
        vt[:HEAD_DIM, spot] = kv[spot, :].T[HEAD_DIM:]
        vt[HEAD_DIM:, spot] = jnp.ones((16, 256), BF16)
        return 0

    lax.fori_loop(0, kv.shape[0] // 256, turn, 0)
    factor = SCORE * LOG2E

    def one(i, _):
        first = place[i // 2] * rows + (i % 2) * half
        query = qz[i]
        acc[...] = jnp.zeros_like(acc)
        top[0:1] = jnp.full((1, half), NEG_FILL, F32)
        slab = first // half

        def visit(at, size, mask):
            step = bk // 2
            spots = [pl.ds(pl.multiple_of(at + s * step, step), step) for s in range(size // step)]
            best, total = top[0:1], acc[...]
            ahead = dot(kv[spots[0], :], query, ((1,), (1,)))
            for s, spot in enumerate(spots):
                st = ahead
                if s + 1 < len(spots):
                    ahead = dot(kv[spots[s + 1], :], query, ((1,), (1,)))
                if mask:
                    key = at + s * step + lax.broadcasted_iota(jnp.int32, st.shape, 0)
                    inside = (key >= begin_rows[slab]) & (key < stop_rows[slab])
                    st = jnp.where(inside, st, NEG_FILL)
                new = jnp.maximum(best, jnp.max(st, axis=0, keepdims=True))
                p = jnp.exp2(st * factor - new * factor)
                shrink = jnp.exp2((best - new) * factor)
                best = new
                total = total * shrink + dot(vt[:, spot], p.astype(BF16), ((1,), (0,)))
            top[0:1] = best
            acc[...] = total

        for_tiles(first, first + half - 1, starts, ends, bk, visit)
        weight = acc[HEAD_DIM : HEAD_DIM + 1]
        ot[i] = acc[:HEAD_DIM] / weight
        lse_out[i] = top[0:1] * factor + jnp.log2(weight)
        return 0

    lax.fori_loop(0, 2 * n_q, one, 0)
    for k in range(n_q):
        joined = jnp.concatenate([ot[2 * k], ot[2 * k + 1]], axis=0).T
        of_out[k] = joined
        o_out[k] = joined.astype(BF16)


def attn_fwd(mine, other, q, here, place, starts, ends, bk):
    n_q, half = len(q), q[0].shape[0]
    total = starts.shape[0]
    return pl.pallas_call(
        functools.partial(fwd_kernel, bk),
        in_specs=[SM, SM, SM, SM, VM, VM, ANY, ANY] + [VM] * n_q,
        out_specs=[VM] * 4,
        out_shape=[
            jax.ShapeDtypeStruct((n_q, half, 128), BF16),
            jax.ShapeDtypeStruct((n_q, half, 128), F32),
            jax.ShapeDtypeStruct((2 * n_q, 1, half), F32),
            jax.ShapeDtypeStruct((total, 128), BF16),
        ],
        scratch_shapes=[
            pltpu.VMEM((HEAD_DIM + 16, total), BF16),
            pltpu.VMEM((2 * n_q, half, 128), BF16),
            pltpu.VMEM((HEAD_DIM + 16, half), F32),
            pltpu.VMEM((8, half), F32),
            pltpu.VMEM((2 * n_q, HEAD_DIM, half), F32),
            pltpu.SemaphoreType.DMA((2 * n_q,)),
        ],
        compiler_params=FWD_PARAMS,
        cost_estimate=pl.CostEstimate(flops=3 * 10**10, bytes_accessed=2**22, transcendentals=0),
        name="attend",
    )(
        here,
        place,
        starts,
        ends,
        starts.reshape(-1, 1, half),
        ends.reshape(-1, 1, half),
        mine,
        other,
        *q,
    )


def bwd_kernel(bk, here, place, starts, ends, begin_rows, stop_rows, kv_hbm, lse, of, *refs):
    n_q, half = of.shape[:2]
    q_in, g_in, refs = refs[:n_q], refs[n_q : 2 * n_q], refs[2 * n_q :]
    dq_out, dkv_out, theirs, kv, kt, qz, gz, delta, dkv, dqt_all, acc, sems = refs
    rows = 2 * half
    copies = load_all([(kv_hbm, kv)], sems)
    for s in range(n_q):
        k = lax.rem(here[0] + n_q - s, n_q)
        q, g = q_in[s][...], g_in[s][...]
        qz[2 * k] = low_half(q)
        qz[2 * k + 1] = low_half(swap_halves(q))
        gz[2 * k] = high_half(swap_halves(g))
        gz[2 * k + 1] = high_half(g)
        prod = (g.astype(F32) * of[k]).T
        delta[2 * k] = jnp.sum(prod[:HEAD_DIM], axis=0, keepdims=True)
        delta[2 * k + 1] = jnp.sum(prod[HEAD_DIM:], axis=0, keepdims=True)
    copies[0].wait()

    def turn(j, _):
        spot = pl.ds(pl.multiple_of(j * 256, 256), 256)
        kt[:, spot] = kv[spot, :].T[:HEAD_DIM]
        dkv[spot, :] = jnp.zeros((256, 128), F32)
        return 0

    lax.fori_loop(0, kv.shape[0] // 256, turn, 0)
    factor = SCORE * LOG2E

    def one(i, _):
        first = place[i // 2] * rows + (i % 2) * half
        query, grad, lse_row, delta_row = qz[i], gz[i], lse[i], delta[i]
        acc[...] = jnp.zeros_like(acc)
        slab = first // half

        def visit(at, size, mask):
            spot = pl.ds(at, size)
            block = kv[spot, :]
            st = dot(block, query, ((1,), (1,)))
            p = jnp.exp2(st * factor - lse_row)
            if mask:
                key = at + lax.broadcasted_iota(jnp.int32, st.shape, 0)
                p = jnp.where((key >= begin_rows[slab]) & (key < stop_rows[slab]), p, 0.0)
            dp = dot(block, grad, ((1,), (1,)))
            ds = (p * (dp - delta_row)).astype(BF16)
            dkv[spot, :] += dot(ds, query, ((1,), (0,))) + dot(p.astype(BF16), grad, ((1,), (0,)))
            acc[...] += dot(kt[:, spot], ds, ((1,), (0,)))

        for_tiles(first, first + half - 1, starts, ends, bk, visit)
        dqt_all[i] = acc[...] * SCORE
        return 0

    lax.fori_loop(0, 2 * n_q, one, 0)
    for k in range(n_q):
        joined = jnp.concatenate([dqt_all[2 * k], dqt_all[2 * k + 1]], axis=0).T
        dq_out[k] = joined.astype(BF16)
    for k in range(n_q):
        dkv_out[k] = dkv[pl.ds(pl.multiple_of(place[k] * rows, 128), rows), :]
        other = pl.ds(pl.multiple_of(place[n_q + k] * rows, 128), rows)
        theirs[k] = dkv[other, :].astype(BF16)


def attn_bwd(kv, q, g, of, lse, here, place, starts, ends, bk):
    n_q, half = len(q), q[0].shape[0]
    total = starts.shape[0]
    return pl.pallas_call(
        functools.partial(bwd_kernel, bk),
        in_specs=[SM, SM, SM, SM, VM, VM, ANY] + [VM] * (2 + 2 * n_q),
        out_specs=[VM] * 3,
        out_shape=[
            jax.ShapeDtypeStruct((n_q, half, 128), BF16),
            jax.ShapeDtypeStruct((n_q, 2 * half, 128), F32),
            jax.ShapeDtypeStruct((n_q, 2 * half, 128), BF16),
        ],
        scratch_shapes=[
            pltpu.VMEM((total, 128), BF16),
            pltpu.VMEM((HEAD_DIM, total), BF16),
            pltpu.VMEM((2 * n_q, half, 128), BF16),
            pltpu.VMEM((2 * n_q, half, 128), BF16),
            pltpu.VMEM((2 * n_q, 1, half), F32),
            pltpu.VMEM((total, 128), F32),
            pltpu.VMEM((2 * n_q, HEAD_DIM, half), F32),
            pltpu.VMEM((HEAD_DIM, half), F32),
            pltpu.SemaphoreType.DMA((1,)),
        ],
        compiler_params=BWD_PARAMS,
        cost_estimate=pl.CostEstimate(flops=4 * 10**10, bytes_accessed=2**22, transcendentals=0),
        name="attend_back",
    )(
        here,
        place,
        starts,
        ends,
        starts.reshape(-1, 1, half),
        ends.reshape(-1, 1, half),
        kv,
        lse,
        of,
        *q,
        *g,
    )


SHIELD = 3 * 10**10
ROOM = 6 * 2**20
WIDE = 58 * 2**20


def stats(x):
    average = jnp.mean(x, axis=-1, keepdims=True)
    centered = x - average
    variance = jnp.mean(centered * centered, axis=-1, keepdims=True)
    return centered, lax.rsqrt(variance + 1e-05)


def norm_back(grad, xhat, rate, gain):
    scaled = grad * gain
    return rate * (
        scaled
        - jnp.mean(scaled, axis=-1, keepdims=True)
        - xhat * jnp.mean(scaled * xhat, axis=-1, keepdims=True)
    )


def column_sums(grad, xhat):
    return jnp.concatenate(
        [jnp.sum(grad * xhat, axis=0, keepdims=True), jnp.sum(grad, axis=0, keepdims=True)], axis=0
    )


def shape_of(*dims, dtype=BF16):
    return jax.ShapeDtypeStruct(dims, dtype)


def kernel_call(kernel, name, specs, outs, args, flops=0, scratch=(), room=ROOM):
    size = sum(a.size * a.dtype.itemsize for a in list(args) + list(outs))
    return pl.pallas_call(
        kernel,
        in_specs=specs,
        out_specs=[VM] * len(outs),
        out_shape=outs,
        scratch_shapes=list(scratch),
        compiler_params=pltpu.CompilerParams(vmem_limit_bytes=min(size + room, WIDE)),
        cost_estimate=pl.CostEstimate(flops=flops, bytes_accessed=size, transcendentals=0),
        name=name,
    )(*args)


def block_rows(index, count):
    return pl.ds(pl.multiple_of(index * count, 16), count)


def head_cut(h):
    return slice(h * HEAD_DIM, (h + 1) * HEAD_DIM)


def project_kernel(here, x, gain, shift, weight, normed_out, kv_out, *refs):
    q_out, q_flat = refs[:-1], refs[-1]
    n_z, half = len(q_out), x.shape[0] // 2
    for t in range(2):
        spot = slice(t * half, (t + 1) * half)
        centered, rate = stats(x[spot, :].astype(F32))
        normed = (centered * rate * gain[0, 0:1] + shift[0, 0:1]).astype(BF16)
        normed_out[spot, :] = normed
        q, k, v = [dot(normed, weight[0, c], ((1,), (0,))).astype(BF16) for c in range(3)]
        q_flat[spot, :] = q
        for h in range(n_z):
            kv_out[h, spot, :] = jnp.concatenate([k[:, head_cut(h)], v[:, head_cut(h)]], axis=1)
    put_slots(here, q_out, q_flat)


def put_slots(here, outs, flat):
    n_z, half = len(outs), outs[0].shape[0]
    for h in range(n_z):
        block = jnp.concatenate([flat[:half, head_cut(h)], flat[half:, head_cut(h)]], axis=1)
        for k, out in enumerate(outs):

            @pl.when(lax.rem(here[0] + k, n_z) == h)
            def _(out=out, block=block):
                out[...] = block


def project(n_z, here, x, gains, shifts, weight):
    rows, width = x.shape
    outs = kernel_call(
        project_kernel,
        "project",
        [SM] + [VM] * 4,
        [shape_of(rows, width), shape_of(n_z, rows, 128)] + [shape_of(rows // 2, 128)] * n_z,
        (here, x, gains, shifts, weight),
        2 * rows * weight.size,
        [pltpu.VMEM((rows, n_z * HEAD_DIM), BF16)],
        room=WIDE,
    )
    return outs[0], outs[1], outs[2:]


def spread_kernel(o_in, out):
    n_z, half = o_in.shape[:2]
    out[:half, :] = jnp.concatenate([o_in[h, :, :HEAD_DIM] for h in range(n_z)], axis=1)
    out[half:, :] = jnp.concatenate([o_in[h, :, HEAD_DIM:] for h in range(n_z)], axis=1)


def spread(o):
    n_z, half = o.shape[:2]
    return kernel_call(spread_kernel, "spread", [VM], [shape_of(2 * half, n_z * HEAD_DIM)], (o,))[0]


def pack_kernel(here, x, *outs):
    put_slots(here, outs, x)


def pack(n_z, here, x):
    return kernel_call(
        pack_kernel, "pack", [SM, VM], [shape_of(x.shape[0] // 2, 128)] * n_z, (here, x)
    )


def mix_kernel(here, x, gain, shift, parts, *refs):
    weights, (after_out, normed_out) = refs[:-2], refs[-2:]
    quarter = parts.shape[1]
    mixed = sum(dot(parts[here[1] ^ m], w[...], ((1,), (0,))) for m, w in enumerate(weights))
    after = x[block_rows(here[1], quarter), :].astype(F32) + mixed
    after_out[...] = after
    centered, rate = stats(after)
    normed_out[...] = (centered * rate * gain[0, 1:2] + shift[0, 1:2]).astype(BF16)


def mix(here, x, gains, shifts, parts, weights):
    n_t, quarter, width = parts.shape[0], parts.shape[1], x.shape[1]
    return kernel_call(
        mix_kernel,
        "mix",
        [SM] + [VM] * (4 + n_t),
        [shape_of(quarter, width, dtype=F32), shape_of(quarter, width)],
        (here, x, gains, shifts, parts, *weights),
        2 * quarter * width * width,
    )


def gelu_pair(u):
    c = math.sqrt(2.0 / math.pi)
    square = u * u
    t = jnp.tanh(c * (u + 0.044715 * square * u))
    slope = 0.5 * (1.0 + t) + 0.5 * u * (1.0 - t * t) * c * (1.0 + 3 * 0.044715 * square)
    return 0.5 * u * (1.0 + t), slope


def hidden_kernel(n_t, here, cot, up, down, *refs):
    slots, (act_out, pre_out, normed), parts = refs[:n_t], refs[n_t : n_t + 3], refs[n_t + 3 :]
    quarter, tile = slots[0].shape[0], 256
    for m, part in enumerate(slots):
        normed[block_rows(here[1] ^ m, quarter), :] = part[...]

    def one(j, _):
        cut = pl.ds(pl.multiple_of(j * tile, tile), tile)
        act, slope = gelu_pair(dot(normed[...], up[0, :, cut], ((1,), (0,))))
        act_out[:, cut] = act.astype(BF16)
        grad = dot(cot[...], down[0, cut, :], ((1,), (1,)))
        pre_out[:, cut] = (grad * slope).astype(BF16)
        return 0

    lax.fori_loop(0, up.shape[2] // tile, one, 0)
    for m, out in enumerate(parts):
        mine = pre_out[block_rows(here[1] ^ m, quarter), :]
        out[...] = dot(mine, up[0], ((1,), (1,))).astype(BF16)


def hidden_layer(here, slots, cot, up, down):
    quarter, width = slots[0].shape
    n_t, units = len(slots), up.shape[2]
    rows = n_t * quarter
    outs = kernel_call(
        functools.partial(hidden_kernel, n_t),
        "hidden_layer",
        [SM] + [VM] * (3 + n_t),
        [shape_of(rows, units), shape_of(rows, units), shape_of(rows, width)]
        + [shape_of(quarter, width)] * n_t,
        (here, cot, up, down, *slots),
        6 * rows * width * units,
    )
    return outs[0], outs[1], outs[2], outs[3:]


def branch_kernel(here, act, down, mixed, own, *sends):
    quarter = own.shape[0]
    for m, out in enumerate([own] + list(sends)):
        part = act[block_rows(here[1] ^ m, quarter), :]
        out[:quarter, :] = dot(part, down[0], ((1,), (0,))).astype(out.dtype)
        if m > 0:
            out[quarter:, :] = mixed[...]


def branch_parts(n_t, here, act, down, mixed):
    rows, (quarter, width) = act.shape[0], mixed.shape
    return kernel_call(
        branch_kernel,
        "branch",
        [SM] + [VM] * 3,
        [shape_of(quarter, width, dtype=F32)] + [shape_of(2 * quarter, width)] * (n_t - 1),
        (here, act, down, mixed),
        2 * rows * width * act.shape[1],
        room=WIDE,
    )


def middle_kernel(n_t, here, after, cot, gain, *refs):
    parts, weights, refs = refs[:n_t], refs[n_t : 2 * n_t], refs[2 * n_t :]
    middle_out, mixed_out, sums_out, grads = refs
    quarter = after.shape[0]
    grad = sum(part[...].astype(F32) for part in parts)
    centered, rate = stats(after[...])
    xhat = centered * rate
    sums_out[...] = column_sums(grad, xhat)
    upstream = cot[block_rows(here[1], quarter), :].astype(F32)
    middle = upstream + norm_back(grad, xhat, rate, gain[0, 1:2])
    middle_out[...] = middle
    mixed = middle.astype(BF16)
    mixed_out[...] = mixed
    for m in range(n_t):
        grads[here[1] ^ m] = dot(mixed, weights[m][...], ((1,), (1,))).astype(BF16)


def middle_back(here, after, cot, gains, parts, weights):
    n_t, (quarter, width) = len(parts), parts[0].shape
    return kernel_call(
        functools.partial(middle_kernel, n_t),
        "middle_back",
        [SM] + [VM] * (3 + 2 * n_t),
        [
            shape_of(quarter, width, dtype=F32),
            shape_of(quarter, width),
            shape_of(2, width, dtype=F32),
            shape_of(n_t, quarter, weights[0].shape[0]),
        ],
        (here, after, cot, gains, *parts, *weights),
        SHIELD,
    )


def join_kernel(mine, theirs, q, out):
    n_z, rows = mine.shape[:2]
    lane = lax.broadcasted_iota(jnp.int32, mine.shape[1:], 1)
    factor = jnp.where(lane < HEAD_DIM, SCORE, 1.0)
    for k in range(n_z):
        out[k, :rows] = ((mine[k] + theirs[k].astype(F32)) * factor).astype(BF16)
        out[k, rows:] = q[k]


def join(mine, theirs, q):
    n_z, rows = mine.shape[:2]
    return kernel_call(
        join_kernel,
        "join",
        [VM] * 3,
        [shape_of(n_z, rows + q.shape[1], 128)],
        (mine, theirs, q),
    )[0]


def unproject_kernel(weight, grads, flat, part):
    n_z, rows = grads.shape[0], flat.shape[0]
    half = rows // 2
    width = n_z * HEAD_DIM
    heads = range(n_z)
    low, high = slice(0, HEAD_DIM), slice(HEAD_DIM, 2 * HEAD_DIM)
    flat[:half, :width] = jnp.concatenate([grads[h, rows:, low] for h in heads], axis=1)
    flat[half:, :width] = jnp.concatenate([grads[h, rows:, high] for h in heads], axis=1)
    flat[:, width : 2 * width] = jnp.concatenate([grads[h, :rows, low] for h in heads], axis=1)
    flat[:, 2 * width :] = jnp.concatenate([grads[h, :rows, high] for h in heads], axis=1)
    total = sum(
        dot(flat[:, c * width : (c + 1) * width], weight[0, c], ((1,), (1,))) for c in range(3)
    )
    part[...] = total.astype(BF16)


def unproject(weight, grads):
    width = weight.shape[2]
    rows = grads.shape[1] * 2 // 3
    return kernel_call(
        unproject_kernel,
        "unproject",
        [VM] * 2,
        [shape_of(rows, 3 * weight.shape[3]), shape_of(rows, width)],
        (weight, grads),
        2 * rows * weight.size,
    )


def last_kernel(here, x, middle, gain, parts, out):
    quarter = middle.shape[0]
    grad = slot_sum(parts)
    centered, rate = stats(x[block_rows(here[1], quarter), :].astype(F32))
    out[...] = (middle[...] + norm_back(grad, centered * rate, rate, gain[0, 0:1])).astype(BF16)


def last_back(here, x, middle, gains, parts):
    return kernel_call(
        last_kernel,
        "last_back",
        [SM] + [VM] * 4,
        [shape_of(*middle.shape)],
        (here, x, middle, gains, parts),
        SHIELD,
    )[0]


def lay_kernel(here, *refs):
    parts, out = refs[:-1], refs[-1]
    for m, part in enumerate(parts):
        out[block_rows(here[1] ^ m, part.shape[0]), :] = part[...].astype(out.dtype)


def lay(here, parts, dtype):
    quarter, width = parts[0].shape
    return kernel_call(
        lay_kernel,
        "lay",
        [SM] + [VM] * len(parts),
        [shape_of(len(parts) * quarter, width, dtype=dtype)],
        (here, *parts),
    )[0]


def for_sides(here, mine, theirs, work):
    for out, side in ((theirs, 1), (mine, 0)):

        def one(k, _, out=out, side=side):
            owner = 2 * k + (here[2] ^ side)
            work(out, k, pl.ds(pl.multiple_of(owner * 128, 128), 128))
            return 0

        lax.fori_loop(0, mine.shape[0], one, 0)


def sides(n_z, depth):
    return [shape_of(n_z, depth, 128, dtype=F32), shape_of(n_z, depth, 128)]


def put_lanes(out, k, first, block):
    for j in range(block.shape[1] // 128):
        out[k, first + j * 128 : first + (j + 1) * 128, :] = block[:, j * 128 : (j + 1) * 128]


def early_kernel(here, act, pre, normed, cot, mine, theirs):
    units = act.shape[1]

    def work(out, k, cut):
        out[k, :units, :] = dot(act[...], cot[:, cut], ((0,), (0,))).astype(out.dtype)
        put_lanes(out, k, units, dot(normed[:, cut], pre[...], ((0,), (0,))).astype(out.dtype))

    for_sides(here, mine, theirs, work)


def early_grads(n_z, here, act, pre, normed, cot):
    depth = 2 * act.shape[1]
    return kernel_call(
        early_kernel,
        "early_grads",
        [SM] + [VM] * 4,
        sides(n_z, depth),
        (here, act, pre, normed, cot),
        2 * act.shape[0] * depth * normed.shape[1],
    )


def halves(x):
    high = x.astype(BF16)
    return high, (x - high.astype(F32)).astype(BF16)


def outward_kernel(here, attended, *refs):
    mixed, (mine, theirs) = refs[:-2], refs[-2:]
    quarter = attended.shape[0] // len(mixed)

    def work(out, k, cut):
        outward = sum(
            dot(attended[block_rows(here[1] ^ m, quarter), :], part[-quarter:, cut], ((0,), (0,)))
            for m, part in enumerate(mixed)
        )
        out[k] = outward.astype(out.dtype)

    for_sides(here, mine, theirs, work)


def outward_grads(n_z, here, attended, mixed):
    rows, share = attended.shape
    return kernel_call(
        outward_kernel,
        "outward_grads",
        [SM] + [VM] * (1 + len(mixed)),
        sides(n_z, share),
        (here, attended, *mixed),
        2 * rows * share * mixed[0].shape[1],
    )


def fold_slots_kernel(here, mine, theirs, *outs):
    for k, out in enumerate(outs):
        at = lax.rem(here[0] + k, len(outs))
        out[...] = (mine[at] + theirs[at].astype(F32)).astype(out.dtype)


def fold_slots(here, mine, theirs):
    n_z, depth, _ = mine.shape
    return kernel_call(
        fold_slots_kernel,
        "fold_slots",
        [SM] + [VM] * 2,
        [shape_of(depth, 128, dtype=F32)] + [shape_of(depth, 128)] * (n_z - 1),
        (here, mine, theirs),
    )


def late_kernel(here, x, normed, grad, sums, part, mine, theirs, scratch):
    depth, step = grad.shape[1], 256
    total = jnp.zeros((2, x.shape[1]), F32)
    for m in range(x.shape[0] // step):
        spot = slice(m * step, (m + 1) * step)
        centered, rate = stats(x[spot, :].astype(F32))
        total = total + column_sums(part[spot, :].astype(F32), centered * rate)
    scratch[0:2, :] = total
    scratch[2:4, :] = sums[...]
    scratch[4:8, :] = jnp.zeros((4, x.shape[1]), F32)

    def work(out, k, cut):
        put_lanes(out, k, 0, dot(normed[:, cut], grad[...], ((0,), (0,))).astype(out.dtype))
        block = scratch[:, cut]
        if out.dtype == BF16:
            high, low = halves(block[0:4])
            block = jnp.concatenate([high.astype(F32), low.astype(F32)], axis=0).astype(BF16)
        out[k, depth:, :] = block

    for_sides(here, mine, theirs, work)


def late_grads(n_z, here, x, normed, grad, sums, part):
    depth = grad.shape[1] + 8
    return kernel_call(
        late_kernel,
        "late_grads",
        [SM] + [VM] * 5,
        sides(n_z, depth),
        (here, x, normed, grad, sums, part),
        2 * grad.shape[0] * depth * normed.shape[1],
        [pltpu.VMEM((8, x.shape[1]), F32)],
    )


def fold_kernel(mine, theirs, out):
    for k in range(mine.shape[0]):
        out[k] = (mine[k] + theirs[k].astype(F32)).astype(BF16)


def fold(mine, theirs):
    return kernel_call(
        fold_kernel, "fold", [VM] * 2, [shape_of(*mine.shape)], (mine, theirs)
    )[0]


def fold_late_kernel(mine, theirs, out):
    depth = mine.shape[1] - 8
    for k in range(mine.shape[0]):
        out[k, :depth] = (mine[k, :depth] + theirs[k, :depth].astype(F32)).astype(BF16)
        tail = mine[k, depth:] + theirs[k, depth:].astype(F32)
        high, low = halves(tail[0:4] + tail[4:8])
        both = jnp.concatenate([high.astype(F32), low.astype(F32)], axis=0)
        out[k, depth:] = both.astype(BF16)


def fold_late(mine, theirs):
    return kernel_call(
        fold_late_kernel, "fold_late", [VM] * 2, [shape_of(*mine.shape)], (mine, theirs)
    )[0]


def slot_sum(parts):
    return sum(parts[k].astype(F32) for k in range(parts.shape[0]))


def finish_early_kernel(parts, down_out, up_out):
    total = slot_sum(parts)
    units = down_out.shape[0]
    down_out[...] = total[:units]
    for j in range(units // 128):
        up_out[:, j * 128 : (j + 1) * 128] = total[units + j * 128 : units + (j + 1) * 128]


def finish_early(units, parts):
    return kernel_call(
        finish_early_kernel,
        "finish_early",
        [VM],
        [shape_of(units, 128, dtype=F32), shape_of(128, units, dtype=F32)],
        (parts,),
    )


def finish_late_kernel(parts, out, sums_out):
    total = slot_sum(parts)
    per = out.shape[2] // 128
    for c in range(3):
        for j in range(per):
            at = (c * per + j) * 128
            out[c, :, j * 128 : (j + 1) * 128] = total[at : at + 128]
    last = total.shape[0] - 8
    sums_out[...] = jnp.concatenate([total[last : last + 4] + total[last + 4 :]] * 2, axis=0)


def finish_late(share, parts):
    return kernel_call(
        finish_late_kernel,
        "finish_late",
        [VM],
        [
            shape_of(3, 128, share, dtype=F32),
            shape_of(8, 128, dtype=F32),
        ],
        (parts,),
    )


def scene_edges(scene_index):
    total = scene_index.shape[0]
    at = lax.iota(jnp.int32, total)
    edge = jnp.concatenate([jnp.ones((1,), jnp.bool_), scene_index[1:] != scene_index[:-1]])
    starts = lax.cummax(jnp.where(edge, at, 0))
    closing = jnp.concatenate([edge[1:], jnp.ones((1,), jnp.bool_)])
    return starts, lax.cummin(jnp.where(closing, at + 1, total), reverse=True)


def body(
    n_seq,
    n_tp,
    tokens,
    scene_index,
    inward_weight,
    outward_weight,
    up_weight,
    down_weight,
    norm_gains,
    norm_shifts,
    cotangent,
):
    n_z, rows, width = n_seq // 2, tokens.shape[0], tokens.shape[1]
    units, share = up_weight.shape[2], outward_weight.shape[1]
    quarter = rows // n_tp
    seq, tp = lax.axis_index("seq"), lax.axis_index("tp")
    z, c = seq // 2, seq % 2
    here = jnp.stack([z, tp, c]).astype(jnp.int32)
    lines = [list(range(b, n_seq, 2)) for b in range(2)]

    def line(x):
        return lax.all_to_all(x, "seq", 0, 0, axis_index_groups=lines, tiled=True)

    def plane(x):
        return lax.all_to_all(x, "tp", 0, 0, tiled=True)

    def across(x):
        return lax.ppermute(x, "seq", [(a, a ^ 1) for a in range(n_seq)])

    def along(x, k):
        return lax.ppermute(
            x, "seq", [(a * 2 + b, (a + k) % n_z * 2 + b) for a in range(n_z) for b in range(2)]
        )

    def over(x, m):
        return lax.ppermute(x, "tp", [(a, a ^ m) for a in range(n_tp)])

    def square(slots):
        return [slots[0]] + [over(slots[m], m) for m in range(1, n_tp)]

    place = jnp.stack([k * 2 + (c ^ g) for g in range(2) for k in range(n_z)]).astype(jnp.int32)
    starts, ends = scene_edges(scene_index)
    normed, kv_send, q_send = project(n_z, here, tokens, norm_gains, norm_shifts, inward_weight)
    kv_mine = line(kv_send)
    q = [q_send[0]] + [along(q_send[k], k) for k in range(1, n_z)]
    (kv_mine, starts, ends, place, q) = lax.optimization_barrier((kv_mine, starts, ends, place, q))
    kv_other = across(kv_mine)
    outward_all = square([outward_weight[0]] * n_tp)
    o, o_full, lse, kv_full = attn_fwd(kv_mine, kv_other, q, here, place, starts, ends, 1024)
    (o, outward_all) = lax.optimization_barrier((o, outward_all))
    attended = spread(line(o))
    parts = plane(attended.reshape(n_tp, quarter, share))
    after, normed_two = mix(here, tokens, norm_gains, norm_shifts, parts, outward_all)
    act, pre, normed_two, grad_parts = hidden_layer(
        here, square([normed_two] * n_tp), cotangent, up_weight, down_weight
    )
    middle, mixed, sums_two, grads = middle_back(
        here, after, cotangent, norm_gains, square(grad_parts), outward_all
    )
    mine, theirs = early_grads(n_z, here, act, pre, normed_two, cotangent)
    early = fold(mine, across(theirs))
    branch = branch_parts(n_tp, here, act, down_weight, mixed)
    grads = plane(grads)
    (grads, early, branch) = lax.optimization_barrier((grads, early, branch))
    g = pack(n_z, here, grads.reshape(rows, share))
    g = [g[0]] + [along(g[k], k) for k in range(1, n_z)]
    (g, early) = lax.optimization_barrier((g, early))
    early = line(early)
    branch = square(branch)
    dq, dkv, dkv_theirs = attn_bwd(kv_full, q, g, o_full, lse, here, place, starts, ends, 1024)
    (dq, dkv, dkv_theirs, early, branch) = lax.optimization_barrier(
        (dq, dkv, dkv_theirs, early, branch)
    )
    mixed = [mixed] + branch[1:]
    back = line(join(dkv, across(dkv_theirs), dq))
    out_own = (after + sum(part[:quarter].astype(F32) for part in branch)).astype(BF16)
    out_slots = square([out_own] * n_tp)
    down_grad, up_grad = finish_early(units, early)
    activations = lay(here, out_slots, BF16)
    mine, theirs = outward_grads(n_z, here, attended, mixed)
    side = fold_slots(here, mine, across(theirs))
    (back, activations, down_grad, up_grad, side) = lax.optimization_barrier(
        (back, activations, down_grad, up_grad, side)
    )
    side = [side[0]] + [along(side[k], k) for k in range(1, n_z)]
    flat, back_part = unproject(inward_weight, back)
    mine, theirs = late_grads(n_z, here, tokens, normed, flat, sums_two, back_part)
    late = fold_late(mine, across(theirs))
    back_part = plane(back_part.reshape(n_tp, quarter, width))
    (back_part, late, side) = lax.optimization_barrier((back_part, late, side))
    outward_grad = sum(part.astype(F32) for part in side)
    token_own = last_back(here, tokens, middle, norm_gains, back_part)
    (late, token_own) = lax.optimization_barrier((late, token_own))
    late = line(late)
    token_slots = square([token_own] * n_tp)
    token_grad = lay(here, token_slots, F32)
    (late, token_grad, outward_grad) = lax.optimization_barrier((late, token_grad, outward_grad))
    inward_grad, sums = finish_late(share, late)
    sums = square([sums] * n_tp)
    while len(sums) > 1:
        sums = [sums[m] + sums[m + 1] for m in range(0, len(sums), 2)]
    sums = sums[0]
    gain_grad = jnp.stack([sums[0], sums[2]])
    shift_grad = jnp.stack([sums[1], sums[3]])
    return (
        activations,
        token_grad,
        inward_grad[None],
        outward_grad[None],
        up_grad[None],
        down_grad[None],
        gain_grad[None],
        shift_grad[None],
    )


def layer_norm(hidden, gain_row, shift_row):
    average = jnp.mean(hidden, axis=-1, keepdims=True)
    centered = hidden - average
    variance = jnp.mean(centered * centered, axis=-1, keepdims=True)
    return centered * lax.rsqrt(variance + 1e-05) * gain_row + shift_row


def gelu_tanh(preactivation):
    return jax.nn.gelu(preactivation, approximate=True)


def to_heads(flat_rows):
    return flat_rows.reshape(flat_rows.shape[0], -1, HEAD_DIM)


def scenes_meet(query_scenes, key_scenes):
    return jnp.logical_and(key_scenes[0] <= query_scenes[-1], key_scenes[-1] >= query_scenes[0])


def score_rows(query_heads, key_heads, query_scenes, key_scenes):
    scores = jnp.einsum(
        "qhd,khd->hqk", query_heads, key_heads, preferred_element_type=jnp.float32
    ) * HEAD_DIM ** (-0.5)
    same_scene = (query_scenes[:, None] == key_scenes[None, :])[None]
    return (scores, same_scene)


def probabilities(scores, same_scene, normalizer):
    return jnp.where(same_scene, jnp.exp(scores - normalizer[:, :, None]), 0.0)


def key_tiles(key_all, value_all, scene_index):
    tile_rows = min(1024, key_all.shape[0])
    tile_count = key_all.shape[0] // tile_rows
    return (
        key_all.reshape(tile_count, tile_rows, -1, HEAD_DIM),
        value_all.reshape(tile_count, tile_rows, -1, HEAD_DIM),
        scene_index.reshape(tile_count, tile_rows),
    )


def log_normalizer(query_heads, query_scenes, tiled_keys):

    def log_visit_tile(running_pair, inputs_pair):
        key_heads, key_scenes = inputs_pair

        def log_compute(pair_now):
            running_max, running_sum = pair_now
            scores, same_scene = score_rows(query_heads, key_heads, query_scenes, key_scenes)
            masked = jnp.where(same_scene, scores, NEG_FILL)
            new_max = jnp.maximum(running_max, jnp.max(masked, axis=-1))
            weights = jnp.where(same_scene, jnp.exp(masked - new_max[:, :, None]), 0.0)
            return (
                new_max,
                running_sum * jnp.exp(running_max - new_max) + jnp.sum(weights, axis=-1),
            )

        return (
            lax.cond(
                scenes_meet(query_scenes, key_scenes),
                log_compute,
                lambda pair_now: pair_now,
                running_pair,
            ),
            None,
        )

    stat_shape = (query_heads.shape[1], query_heads.shape[0])
    start_pair = (jnp.full(stat_shape, NEG_FILL, jnp.float32), jnp.zeros(stat_shape, jnp.float32))
    final_pair, _ = lax.scan(log_visit_tile, start_pair, (tiled_keys[0], tiled_keys[2]))
    return final_pair[0] + jnp.log(final_pair[1])


def attend_all(query_heads, query_scenes, tiled_keys, normalizer):

    def attend_visit_tile(running_total, inputs_triple):
        key_heads, value_heads, key_scenes = inputs_triple

        def attend_compute(total_now):
            scores, same_scene = score_rows(query_heads, key_heads, query_scenes, key_scenes)
            weights = probabilities(scores, same_scene, normalizer).astype(jnp.bfloat16)
            return total_now + jnp.einsum(
                "hqk,khd->qhd", weights, value_heads, preferred_element_type=jnp.float32
            )

        return (
            lax.cond(
                scenes_meet(query_scenes, key_scenes),
                attend_compute,
                lambda total_now: total_now,
                running_total,
            ),
            None,
        )

    running_total, _ = lax.scan(
        attend_visit_tile, jnp.zeros(query_heads.shape, jnp.float32), tiled_keys
    )
    return running_total.reshape(running_total.shape[0], -1)


def score_gradients(
    query_heads,
    key_heads,
    value_heads,
    grad_heads,
    query_scenes,
    key_scenes,
    normalizer,
    delta_rows,
):
    scores, same_scene = score_rows(query_heads, key_heads, query_scenes, key_scenes)
    weights = probabilities(scores, same_scene, normalizer)
    weight_grad = jnp.einsum(
        "qhd,khd->hqk", grad_heads, value_heads, preferred_element_type=jnp.float32
    )
    score_grad = (weights * (weight_grad - delta_rows[:, :, None])).astype(jnp.bfloat16)
    return (weights.astype(jnp.bfloat16), score_grad)


def grads_by_reduce(query_heads, grad_heads, query_scenes, tiled_keys, normalizer, delta_rows):
    tile_rows = tiled_keys[0].shape[1]
    joined_width = 2 * query_heads.shape[1] * query_heads.shape[2]

    def grads_visit_tile(query_total, inputs_triple):
        key_heads, value_heads, key_scenes = inputs_triple

        def grads_compute(total_now):
            weights, score_grad = score_gradients(
                query_heads,
                key_heads,
                value_heads,
                grad_heads,
                query_scenes,
                key_scenes,
                normalizer,
                delta_rows,
            )
            total_now = total_now + jnp.einsum(
                "hqk,khd->qhd", score_grad, key_heads, preferred_element_type=jnp.float32
            )
            key_term = jnp.einsum(
                "hqk,qhd->khd", score_grad, query_heads, preferred_element_type=jnp.float32
            )
            value_term = jnp.einsum(
                "hqk,qhd->khd", weights, grad_heads, preferred_element_type=jnp.float32
            )
            joined = jnp.concatenate(
                [key_term.reshape(tile_rows, -1), value_term.reshape(tile_rows, -1)], axis=1
            )
            return (total_now, joined)

        def skipped(total_now):
            return (total_now, jnp.zeros((tile_rows, joined_width), jnp.float32))

        return lax.cond(scenes_meet(query_scenes, key_scenes), grads_compute, skipped, query_total)

    query_total, key_terms_all = lax.scan(
        grads_visit_tile, jnp.zeros(query_heads.shape, jnp.float32), tiled_keys
    )
    key_terms_all = key_terms_all.reshape(-1, key_terms_all.shape[-1])
    summed = lax.psum_scatter(key_terms_all, "seq", scatter_dimension=0, tiled=True)
    half_width = summed.shape[1] // 2
    return (
        query_total.reshape(query_total.shape[0], -1),
        summed[:, :half_width],
        summed[:, half_width:],
    )


def generic_body(
    tokens,
    scene_index,
    inward_weight,
    outward_weight,
    up_weight,
    down_weight,
    norm_gains,
    norm_shifts,
    cotangent,
):
    local_rows = tokens.shape[0]
    score_factor = HEAD_DIM ** (-0.5)
    query_scenes = lax.dynamic_slice_in_dim(
        scene_index, lax.axis_index("seq") * local_rows, local_rows
    )
    hidden = tokens.astype(jnp.float32)
    layer_number = 0
    gain_pair = norm_gains[layer_number]
    shift_pair = norm_shifts[layer_number]
    normed = layer_norm(hidden, gain_pair[0], shift_pair[0]).astype(jnp.bfloat16)
    projected = jnp.einsum(
        "td,cde->tce", normed, inward_weight[layer_number], preferred_element_type=jnp.float32
    ).astype(jnp.bfloat16)
    queries = projected[:, 0]
    key_local = projected[:, 1]
    value_local = projected[:, 2]
    key_all = lax.all_gather(key_local, "seq", axis=0, tiled=True)
    value_all = lax.all_gather(value_local, "seq", axis=0, tiled=True)
    tiled_keys = key_tiles(key_all, value_all, scene_index)
    query_heads = to_heads(queries)
    normalizer = log_normalizer(query_heads, query_scenes, tiled_keys)
    attended = attend_all(query_heads, query_scenes, tiled_keys, normalizer)
    attended_low = attended.astype(jnp.bfloat16)
    mixed_sum = lax.psum(
        jnp.dot(attended_low, outward_weight[layer_number], preferred_element_type=jnp.float32),
        "tp",
    )
    after_attention = hidden + mixed_sum
    normed_two = layer_norm(after_attention, gain_pair[1], shift_pair[1]).astype(jnp.bfloat16)
    preactivation = jnp.dot(normed_two, up_weight[layer_number], preferred_element_type=jnp.float32)
    activated = gelu_tanh(preactivation).astype(jnp.bfloat16)
    branch = lax.psum(
        jnp.dot(activated, down_weight[layer_number], preferred_element_type=jnp.float32), "tp"
    )
    kept_layers = [
        (
            hidden,
            after_attention,
            queries,
            key_local,
            value_local,
            tiled_keys,
            normalizer,
            attended,
            attended_low,
            preactivation,
            activated,
        )
    ]
    hidden = after_attention + branch
    upstream = cotangent.astype(jnp.float32)
    layer_grads = [None] * LAYERS
    for layer_number in reversed(range(LAYERS)):
        (
            hidden_in,
            after_attention,
            queries,
            key_local,
            value_local,
            tiled_keys,
            normalizer,
            attended,
            attended_low,
            preactivation,
            activated,
        ) = kept_layers[layer_number]
        gain_pair = norm_gains[layer_number]
        shift_pair = norm_shifts[layer_number]
        branch_grad = upstream.astype(jnp.bfloat16)
        down_grad = jnp.einsum(
            "tf,td->fd", activated, branch_grad, preferred_element_type=jnp.float32
        )
        act_grad = jnp.einsum(
            "td,fd->tf", branch_grad, down_weight[layer_number], preferred_element_type=jnp.float32
        )
        _, gelu_pull = jax.vjp(gelu_tanh, preactivation)
        preactivation_grad = gelu_pull(act_grad)[0].astype(jnp.bfloat16)
        normed_two_f, norm_pull_two = jax.vjp(
            layer_norm, after_attention, gain_pair[1], shift_pair[1]
        )
        normed_two = normed_two_f.astype(jnp.bfloat16)
        up_grad = jnp.einsum(
            "td,tf->df", normed_two, preactivation_grad, preferred_element_type=jnp.float32
        )
        normed_two_grad = lax.psum(
            jnp.einsum(
                "tf,df->td",
                preactivation_grad,
                up_weight[layer_number],
                preferred_element_type=jnp.float32,
            ),
            "tp",
        )
        middle_part, gain_two, shift_two = norm_pull_two(normed_two_grad)
        middle_grad = upstream + middle_part
        mixed_grad = middle_grad.astype(jnp.bfloat16)
        outward_grad = jnp.einsum(
            "te,td->ed", attended_low, mixed_grad, preferred_element_type=jnp.float32
        )
        attended_grad = jnp.einsum(
            "td,ed->te",
            mixed_grad,
            outward_weight[layer_number],
            preferred_element_type=jnp.float32,
        ).astype(jnp.bfloat16)
        delta_rows = jnp.sum(to_heads(attended_grad.astype(jnp.float32) * attended), axis=-1).T
        query_sum, key_sum, value_sum = grads_by_reduce(
            to_heads(queries),
            to_heads(attended_grad),
            query_scenes,
            tiled_keys,
            normalizer,
            delta_rows,
        )
        projected_grad = jnp.stack(
            [query_sum * score_factor, key_sum * score_factor, value_sum], axis=1
        ).astype(jnp.bfloat16)
        normed_f, norm_pull = jax.vjp(layer_norm, hidden_in, gain_pair[0], shift_pair[0])
        normed = normed_f.astype(jnp.bfloat16)
        inward_grad = jnp.einsum(
            "td,tce->cde", normed, projected_grad, preferred_element_type=jnp.float32
        )
        normed_grad = lax.psum(
            jnp.einsum(
                "tce,cde->td",
                projected_grad,
                inward_weight[layer_number],
                preferred_element_type=jnp.float32,
            ),
            "tp",
        )
        input_part, gain_one, shift_one = norm_pull(normed_grad)
        upstream = middle_grad + input_part
        layer_grads[layer_number] = (
            lax.psum_scatter(inward_grad, "seq", scatter_dimension=1, tiled=True),
            lax.psum_scatter(outward_grad, "seq", scatter_dimension=1, tiled=True),
            lax.psum_scatter(up_grad, "seq", scatter_dimension=0, tiled=True),
            lax.psum_scatter(down_grad, "seq", scatter_dimension=1, tiled=True),
            lax.psum_scatter(
                jnp.stack([gain_one, gain_two]), "seq", scatter_dimension=1, tiled=True
            ),
            lax.psum_scatter(
                jnp.stack([shift_one, shift_two]), "seq", scatter_dimension=1, tiled=True
            ),
        )
    return (
        hidden.astype(jnp.bfloat16),
        upstream,
        jnp.stack([layer_part[0] for layer_part in layer_grads]),
        jnp.stack([layer_part[1] for layer_part in layer_grads]),
        jnp.stack([layer_part[2] for layer_part in layer_grads]),
        jnp.stack([layer_part[3] for layer_part in layer_grads]),
        jnp.stack([layer_part[4] for layer_part in layer_grads]),
        jnp.stack([layer_part[5] for layer_part in layer_grads]),
    )


def solution(mesh):
    placed = (
        P("seq", None),
        P(),
        P(None, None, None, "tp"),
        P(None, "tp", None),
        P(None, None, "tp"),
        P(None, "tp", None),
        P(),
        P(),
        P("seq", None),
    )
    n_seq, n_tp = mesh.shape["seq"], mesh.shape["tp"]
    fits = n_seq == 8 and n_tp == 4
    return jax.shard_map(
        functools.partial(body, n_seq, n_tp) if fits else generic_body,
        mesh=mesh,
        in_specs=placed,
        out_specs=(
            P("seq", None),
            P("seq", None),
            P(None, None, "seq", "tp"),
            P(None, "tp", "seq"),
            P(None, "seq", "tp"),
            P(None, "tp", "seq"),
            P(None, None, "seq"),
            P(None, None, "seq"),
        ),
        check_vma=False,
    )
```

```python
import functools
import math
import jax
import jax.numpy as jnp
from jax import lax
from jax.experimental import pallas as pl
from jax.experimental.pallas import tpu as pltpu
from jax.sharding import PartitionSpec as P

HEAD_DIM = 64
LAYERS = 1
F32, BF16 = jnp.float32, jnp.bfloat16
NEG_FILL = -1e30
SCORE = HEAD_DIM ** -0.5
LOG2E = math.log2(math.e)
ANY = pl.BlockSpec(memory_space=pl.ANY)
VM = pl.BlockSpec(memory_space=pltpu.VMEM)
SM = pl.BlockSpec(memory_space=pltpu.SMEM)
FWD_PARAMS = pltpu.CompilerParams(vmem_limit_bytes=58 * 2**20)
BWD_PARAMS = pltpu.CompilerParams(vmem_limit_bytes=58 * 2**20)


def dot(a, b, dims):
    return lax.dot_general(a, b, (dims, ((), ())), preferred_element_type=F32)


def load_all(pairs, sems):
    copies = [pltpu.make_async_copy(s, d, sems.at[i]) for i, (s, d) in enumerate(pairs)]
    for c in copies:
        c.start()
    return copies


def for_tiles(first, last, starts, ends, bk, visit):
    edge = bk // 2
    begin, stop = starts[first], ends[last]
    low, high = begin // edge, (stop + edge - 1) // edge
    clear0 = jnp.where(ends[first] == stop, (begin + edge - 1) // edge, high)
    count = jnp.maximum(stop // edge - clear0, 0) // 2
    head = clear0 - low

    def masked(i, _):
        j = jnp.where(i < head, low + i, clear0 + 2 * count + i - head)
        visit(pl.multiple_of(j * edge, edge), edge, True)
        return 0

    def clear(i, _):
        visit(pl.multiple_of((clear0 + 2 * i) * edge, edge), bk, False)
        return 0

    lax.fori_loop(0, high - low - 2 * count, masked, 0)
    lax.fori_loop(0, count, clear, 0)


def low_half(x):
    lane = lax.broadcasted_iota(jnp.int32, x.shape, 1)
    return jnp.where(lane < HEAD_DIM, x, jnp.zeros_like(x))


def high_half(x):
    lane = lax.broadcasted_iota(jnp.int32, x.shape, 1)
    return jnp.where(lane < HEAD_DIM, jnp.zeros_like(x), x)


def swap_halves(x):
    return jnp.concatenate([x[:, HEAD_DIM:], x[:, :HEAD_DIM]], axis=1)


def fwd_kernel(bk, here, place, starts, ends, begin_rows, stop_rows, mine, other, *refs):
    n_q = mine.shape[0]
    q_in, refs = refs[:n_q], refs[n_q:]
    o_out, of_out, lse_out, kv, vt, qz, acc, top, ot, sems = refs
    half = q_in[0].shape[0]
    rows = 2 * half
    spots = [pl.ds(pl.multiple_of(place[i] * rows, 128), rows) for i in range(2 * n_q)]
    copies = load_all(
        [(mine.at[k], kv.at[spots[k]]) for k in range(n_q)]
        + [(other.at[k], kv.at[spots[n_q + k]]) for k in range(n_q)],
        sems,
    )
    for s in range(n_q):
        k = lax.rem(here[0] + n_q - s, n_q)
        q = q_in[s][...]
        qz[2 * k] = low_half(q)
        qz[2 * k + 1] = low_half(swap_halves(q))
    for c in copies:
        c.wait()

    def turn(j, _):
        spot = pl.ds(pl.multiple_of(j * 256, 256), 256)
        vt[:HEAD_DIM, spot] = kv[spot, :].T[HEAD_DIM:]
        vt[HEAD_DIM:, spot] = jnp.ones((16, 256), BF16)
        return 0

    lax.fori_loop(0, kv.shape[0] // 256, turn, 0)
    factor = SCORE * LOG2E

    def one(i, _):
        first = place[i // 2] * rows + (i % 2) * half
        query = qz[i]
        acc[...] = jnp.zeros_like(acc)
        top[0:1] = jnp.full((1, half), NEG_FILL, F32)
        slab = first // half

        def visit(at, size, mask):
            step = bk // 2
            spots = [pl.ds(pl.multiple_of(at + s * step, step), step) for s in range(size // step)]
            best, total = top[0:1], acc[...]
            ahead = dot(kv[spots[0], :], query, ((1,), (1,)))
            for s, spot in enumerate(spots):
                st = ahead
                if s + 1 < len(spots):
                    ahead = dot(kv[spots[s + 1], :], query, ((1,), (1,)))
                if mask:
                    key = at + s * step + lax.broadcasted_iota(jnp.int32, st.shape, 0)
                    inside = (key >= begin_rows[slab]) & (key < stop_rows[slab])
                    st = jnp.where(inside, st, NEG_FILL)
                new = jnp.maximum(best, jnp.max(st, axis=0, keepdims=True))
                p = jnp.exp2(st * factor - new * factor)
                shrink = jnp.exp2((best - new) * factor)
                best = new
                total = total * shrink + dot(vt[:, spot], p.astype(BF16), ((1,), (0,)))
            top[0:1] = best
            acc[...] = total

        for_tiles(first, first + half - 1, starts, ends, bk, visit)
        weight = acc[HEAD_DIM : HEAD_DIM + 1]
        ot[i] = acc[:HEAD_DIM] / weight
        lse_out[i] = top[0:1] * factor + jnp.log2(weight)
        return 0

    lax.fori_loop(0, 2 * n_q, one, 0)
    for k in range(n_q):
        joined = jnp.concatenate([ot[2 * k], ot[2 * k + 1]], axis=0).T
        of_out[k] = joined
        o_out[k] = joined.astype(BF16)


def attn_fwd(mine, other, q, here, place, starts, ends, bk):
    n_q, half = len(q), q[0].shape[0]
    total = starts.shape[0]
    return pl.pallas_call(
        functools.partial(fwd_kernel, bk),
        in_specs=[SM, SM, SM, SM, VM, VM, ANY, ANY] + [VM] * n_q,
        out_specs=[VM] * 4,
        out_shape=[
            jax.ShapeDtypeStruct((n_q, half, 128), BF16),
            jax.ShapeDtypeStruct((n_q, half, 128), F32),
            jax.ShapeDtypeStruct((2 * n_q, 1, half), F32),
            jax.ShapeDtypeStruct((total, 128), BF16),
        ],
        scratch_shapes=[
            pltpu.VMEM((HEAD_DIM + 16, total), BF16),
            pltpu.VMEM((2 * n_q, half, 128), BF16),
            pltpu.VMEM((HEAD_DIM + 16, half), F32),
            pltpu.VMEM((8, half), F32),
            pltpu.VMEM((2 * n_q, HEAD_DIM, half), F32),
            pltpu.SemaphoreType.DMA((2 * n_q,)),
        ],
        compiler_params=FWD_PARAMS,
        cost_estimate=pl.CostEstimate(flops=3 * 10**10, bytes_accessed=2**22, transcendentals=0),
        name="attend",
    )(
        here,
        place,
        starts,
        ends,
        starts.reshape(-1, 1, half),
        ends.reshape(-1, 1, half),
        mine,
        other,
        *q,
    )


def bwd_kernel(bk, here, place, starts, ends, begin_rows, stop_rows, kv_hbm, lse, of, *refs):
    n_q, half = of.shape[:2]
    q_in, g_in, refs = refs[:n_q], refs[n_q : 2 * n_q], refs[2 * n_q :]
    dq_out, dkv_out, theirs, kv, kt, qz, gz, delta, dkv, dqt_all, acc, sems = refs
    rows = 2 * half
    copies = load_all([(kv_hbm, kv)], sems)
    for s in range(n_q):
        k = lax.rem(here[0] + n_q - s, n_q)
        q, g = q_in[s][...], g_in[s][...]
        qz[2 * k] = low_half(q)
        qz[2 * k + 1] = low_half(swap_halves(q))
        gz[2 * k] = high_half(swap_halves(g))
        gz[2 * k + 1] = high_half(g)
        prod = (g.astype(F32) * of[k]).T
        delta[2 * k] = jnp.sum(prod[:HEAD_DIM], axis=0, keepdims=True)
        delta[2 * k + 1] = jnp.sum(prod[HEAD_DIM:], axis=0, keepdims=True)
    copies[0].wait()

    def turn(j, _):
        spot = pl.ds(pl.multiple_of(j * 256, 256), 256)
        kt[:, spot] = kv[spot, :].T[:HEAD_DIM]
        dkv[spot, :] = jnp.zeros((256, 128), F32)
        return 0

    lax.fori_loop(0, kv.shape[0] // 256, turn, 0)
    factor = SCORE * LOG2E

    def one(i, _):
        first = place[i // 2] * rows + (i % 2) * half
        query, grad, lse_row, delta_row = qz[i], gz[i], lse[i], delta[i]
        acc[...] = jnp.zeros_like(acc)
        slab = first // half

        def visit(at, size, mask):
            spot = pl.ds(at, size)
            block = kv[spot, :]
            st = dot(block, query, ((1,), (1,)))
            p = jnp.exp2(st * factor - lse_row)
            if mask:
                key = at + lax.broadcasted_iota(jnp.int32, st.shape, 0)
                p = jnp.where((key >= begin_rows[slab]) & (key < stop_rows[slab]), p, 0.0)
            dp = dot(block, grad, ((1,), (1,)))
            ds = (p * (dp - delta_row)).astype(BF16)
            dkv[spot, :] += dot(ds, query, ((1,), (0,))) + dot(p.astype(BF16), grad, ((1,), (0,)))
            acc[...] += dot(kt[:, spot], ds, ((1,), (0,)))

        for_tiles(first, first + half - 1, starts, ends, bk, visit)
        dqt_all[i] = acc[...] * SCORE
        return 0

    lax.fori_loop(0, 2 * n_q, one, 0)
    for k in range(n_q):
        joined = jnp.concatenate([dqt_all[2 * k], dqt_all[2 * k + 1]], axis=0).T
        dq_out[k] = joined.astype(BF16)
    for k in range(n_q):
        dkv_out[k] = dkv[pl.ds(pl.multiple_of(place[k] * rows, 128), rows), :]
        other = pl.ds(pl.multiple_of(place[n_q + k] * rows, 128), rows)
        theirs[k] = dkv[other, :].astype(BF16)


def attn_bwd(kv, q, g, of, lse, here, place, starts, ends, bk):
    n_q, half = len(q), q[0].shape[0]
    total = starts.shape[0]
    return pl.pallas_call(
        functools.partial(bwd_kernel, bk),
        in_specs=[SM, SM, SM, SM, VM, VM, ANY] + [VM] * (2 + 2 * n_q),
        out_specs=[VM] * 3,
        out_shape=[
            jax.ShapeDtypeStruct((n_q, half, 128), BF16),
            jax.ShapeDtypeStruct((n_q, 2 * half, 128), F32),
            jax.ShapeDtypeStruct((n_q, 2 * half, 128), BF16),
        ],
        scratch_shapes=[
            pltpu.VMEM((total, 128), BF16),
            pltpu.VMEM((HEAD_DIM, total), BF16),
            pltpu.VMEM((2 * n_q, half, 128), BF16),
            pltpu.VMEM((2 * n_q, half, 128), BF16),
            pltpu.VMEM((2 * n_q, 1, half), F32),
            pltpu.VMEM((total, 128), F32),
            pltpu.VMEM((2 * n_q, HEAD_DIM, half), F32),
            pltpu.VMEM((HEAD_DIM, half), F32),
            pltpu.SemaphoreType.DMA((1,)),
        ],
        compiler_params=BWD_PARAMS,
        cost_estimate=pl.CostEstimate(flops=4 * 10**10, bytes_accessed=2**22, transcendentals=0),
        name="attend_back",
    )(
        here,
        place,
        starts,
        ends,
        starts.reshape(-1, 1, half),
        ends.reshape(-1, 1, half),
        kv,
        lse,
        of,
        *q,
        *g,
    )


SHIELD = 3 * 10**10
ROOM = 6 * 2**20
WIDE = 58 * 2**20


def stats(x):
    average = jnp.mean(x, axis=-1, keepdims=True)
    centered = x - average
    variance = jnp.mean(centered * centered, axis=-1, keepdims=True)
    return centered, lax.rsqrt(variance + 1e-05)


def norm_back(grad, xhat, rate, gain):
    scaled = grad * gain
    return rate * (
        scaled
        - jnp.mean(scaled, axis=-1, keepdims=True)
        - xhat * jnp.mean(scaled * xhat, axis=-1, keepdims=True)
    )


def column_sums(grad, xhat):
    return jnp.concatenate(
        [jnp.sum(grad * xhat, axis=0, keepdims=True), jnp.sum(grad, axis=0, keepdims=True)], axis=0
    )


def shape_of(*dims, dtype=BF16):
    return jax.ShapeDtypeStruct(dims, dtype)


def kernel_call(kernel, name, specs, outs, args, flops=0, scratch=(), room=ROOM):
    size = sum(a.size * a.dtype.itemsize for a in list(args) + list(outs))
    return pl.pallas_call(
        kernel,
        in_specs=specs,
        out_specs=[VM] * len(outs),
        out_shape=outs,
        scratch_shapes=list(scratch),
        compiler_params=pltpu.CompilerParams(vmem_limit_bytes=min(size + room, WIDE)),
        cost_estimate=pl.CostEstimate(flops=flops, bytes_accessed=size, transcendentals=0),
        name=name,
    )(*args)


def block_rows(index, count):
    return pl.ds(pl.multiple_of(index * count, 16), count)


def head_cut(h):
    return slice(h * HEAD_DIM, (h + 1) * HEAD_DIM)


def project_kernel(here, x, gain, shift, weight, normed_out, kv_out, *refs):
    q_out, q_flat = refs[:-1], refs[-1]
    n_z, half = len(q_out), x.shape[0] // 2
    for t in range(2):
        spot = slice(t * half, (t + 1) * half)
        centered, rate = stats(x[spot, :].astype(F32))
        normed = (centered * rate * gain[0, 0:1] + shift[0, 0:1]).astype(BF16)
        normed_out[spot, :] = normed
        q, k, v = [dot(normed, weight[0, c], ((1,), (0,))).astype(BF16) for c in range(3)]
        q_flat[spot, :] = q
        for h in range(n_z):
            kv_out[h, spot, :] = jnp.concatenate([k[:, head_cut(h)], v[:, head_cut(h)]], axis=1)
    put_slots(here, q_out, q_flat)


def put_slots(here, outs, flat):
    n_z, half = len(outs), outs[0].shape[0]
    for h in range(n_z):
        block = jnp.concatenate([flat[:half, head_cut(h)], flat[half:, head_cut(h)]], axis=1)
        for k, out in enumerate(outs):

            @pl.when(lax.rem(here[0] + k, n_z) == h)
            def _(out=out, block=block):
                out[...] = block


def project(n_z, here, x, gains, shifts, weight):
    rows, width = x.shape
    outs = kernel_call(
        project_kernel,
        "project",
        [SM] + [VM] * 4,
        [shape_of(rows, width), shape_of(n_z, rows, 128)] + [shape_of(rows // 2, 128)] * n_z,
        (here, x, gains, shifts, weight),
        2 * rows * weight.size,
        [pltpu.VMEM((rows, n_z * HEAD_DIM), BF16)],
        room=WIDE,
    )
    return outs[0], outs[1], outs[2:]


def spread_kernel(o_in, out):
    n_z, half = o_in.shape[:2]
    out[:half, :] = jnp.concatenate([o_in[h, :, :HEAD_DIM] for h in range(n_z)], axis=1)
    out[half:, :] = jnp.concatenate([o_in[h, :, HEAD_DIM:] for h in range(n_z)], axis=1)


def spread(o):
    n_z, half = o.shape[:2]
    return kernel_call(spread_kernel, "spread", [VM], [shape_of(2 * half, n_z * HEAD_DIM)], (o,))[0]


def pack_kernel(here, x, *outs):
    put_slots(here, outs, x)


def pack(n_z, here, x):
    return kernel_call(
        pack_kernel, "pack", [SM, VM], [shape_of(x.shape[0] // 2, 128)] * n_z, (here, x)
    )


def mix_kernel(here, x, gain, shift, parts, *refs):
    weights, (after_out, normed_out) = refs[:-2], refs[-2:]
    quarter = parts.shape[1]
    mixed = sum(dot(parts[here[1] ^ m], w[...], ((1,), (0,))) for m, w in enumerate(weights))
    after = x[block_rows(here[1], quarter), :].astype(F32) + mixed
    after_out[...] = after
    centered, rate = stats(after)
    normed_out[...] = (centered * rate * gain[0, 1:2] + shift[0, 1:2]).astype(BF16)


def mix(here, x, gains, shifts, parts, weights):
    n_t, quarter, width = parts.shape[0], parts.shape[1], x.shape[1]
    return kernel_call(
        mix_kernel,
        "mix",
        [SM] + [VM] * (4 + n_t),
        [shape_of(quarter, width, dtype=F32), shape_of(quarter, width)],
        (here, x, gains, shifts, parts, *weights),
        2 * quarter * width * width,
    )


def gelu_pair(u):
    c = math.sqrt(2.0 / math.pi)
    square = u * u
    t = jnp.tanh(c * (u + 0.044715 * square * u))
    slope = 0.5 * (1.0 + t) + 0.5 * u * (1.0 - t * t) * c * (1.0 + 3 * 0.044715 * square)
    return 0.5 * u * (1.0 + t), slope


def hidden_kernel(n_t, here, cot, up, down, *refs):
    slots, (act_out, pre_out, normed), parts = refs[:n_t], refs[n_t : n_t + 3], refs[n_t + 3 :]
    quarter, tile = slots[0].shape[0], 256
    for m, part in enumerate(slots):
        normed[block_rows(here[1] ^ m, quarter), :] = part[...]

    def one(j, _):
        cut = pl.ds(pl.multiple_of(j * tile, tile), tile)
        act, slope = gelu_pair(dot(normed[...], up[0, :, cut], ((1,), (0,))))
        act_out[:, cut] = act.astype(BF16)
        grad = dot(cot[...], down[0, cut, :], ((1,), (1,)))
        pre_out[:, cut] = (grad * slope).astype(BF16)
        return 0

    lax.fori_loop(0, up.shape[2] // tile, one, 0)
    for m, out in enumerate(parts):
        mine = pre_out[block_rows(here[1] ^ m, quarter), :]
        out[...] = dot(mine, up[0], ((1,), (1,))).astype(BF16)


def hidden_layer(here, slots, cot, up, down):
    quarter, width = slots[0].shape
    n_t, units = len(slots), up.shape[2]
    rows = n_t * quarter
    outs = kernel_call(
        functools.partial(hidden_kernel, n_t),
        "hidden_layer",
        [SM] + [VM] * (3 + n_t),
        [shape_of(rows, units), shape_of(rows, units), shape_of(rows, width)]
        + [shape_of(quarter, width)] * n_t,
        (here, cot, up, down, *slots),
        6 * rows * width * units,
    )
    return outs[0], outs[1], outs[2], outs[3:]


def branch_kernel(here, act, down, mixed, own, *sends):
    quarter = own.shape[0]
    for m, out in enumerate([own] + list(sends)):
        part = act[block_rows(here[1] ^ m, quarter), :]
        out[:quarter, :] = dot(part, down[0], ((1,), (0,))).astype(out.dtype)
        if m > 0:
            out[quarter:, :] = mixed[...]


def branch_parts(n_t, here, act, down, mixed):
    rows, (quarter, width) = act.shape[0], mixed.shape
    return kernel_call(
        branch_kernel,
        "branch",
        [SM] + [VM] * 3,
        [shape_of(quarter, width, dtype=F32)] + [shape_of(2 * quarter, width)] * (n_t - 1),
        (here, act, down, mixed),
        2 * rows * width * act.shape[1],
        room=WIDE,
    )


def middle_kernel(n_t, here, after, cot, gain, *refs):
    parts, weights, refs = refs[:n_t], refs[n_t : 2 * n_t], refs[2 * n_t :]
    middle_out, mixed_out, sums_out, grads = refs
    quarter = after.shape[0]
    grad = sum(part[...].astype(F32) for part in parts)
    centered, rate = stats(after[...])
    xhat = centered * rate
    sums_out[...] = column_sums(grad, xhat)
    upstream = cot[block_rows(here[1], quarter), :].astype(F32)
    middle = upstream + norm_back(grad, xhat, rate, gain[0, 1:2])
    middle_out[...] = middle
    mixed = middle.astype(BF16)
    mixed_out[...] = mixed
    for m in range(n_t):
        grads[here[1] ^ m] = dot(mixed, weights[m][...], ((1,), (1,))).astype(BF16)


def middle_back(here, after, cot, gains, parts, weights):
    n_t, (quarter, width) = len(parts), parts[0].shape
    return kernel_call(
        functools.partial(middle_kernel, n_t),
        "middle_back",
        [SM] + [VM] * (3 + 2 * n_t),
        [
            shape_of(quarter, width, dtype=F32),
            shape_of(quarter, width),
            shape_of(2, width, dtype=F32),
            shape_of(n_t, quarter, weights[0].shape[0]),
        ],
        (here, after, cot, gains, *parts, *weights),
        SHIELD,
    )


def join_kernel(mine, theirs, q, out):
    n_z, rows = mine.shape[:2]
    lane = lax.broadcasted_iota(jnp.int32, mine.shape[1:], 1)
    factor = jnp.where(lane < HEAD_DIM, SCORE, 1.0)
    for k in range(n_z):
        out[k, :rows] = ((mine[k] + theirs[k].astype(F32)) * factor).astype(BF16)
        out[k, rows:] = q[k]


def join(mine, theirs, q):
    n_z, rows = mine.shape[:2]
    return kernel_call(
        join_kernel,
        "join",
        [VM] * 3,
        [shape_of(n_z, rows + q.shape[1], 128)],
        (mine, theirs, q),
    )[0]


def unproject_kernel(weight, grads, flat, part):
    n_z, rows = grads.shape[0], flat.shape[0]
    half = rows // 2
    width = n_z * HEAD_DIM
    heads = range(n_z)
    low, high = slice(0, HEAD_DIM), slice(HEAD_DIM, 2 * HEAD_DIM)
    flat[:half, :width] = jnp.concatenate([grads[h, rows:, low] for h in heads], axis=1)
    flat[half:, :width] = jnp.concatenate([grads[h, rows:, high] for h in heads], axis=1)
    flat[:, width : 2 * width] = jnp.concatenate([grads[h, :rows, low] for h in heads], axis=1)
    flat[:, 2 * width :] = jnp.concatenate([grads[h, :rows, high] for h in heads], axis=1)
    total = sum(
        dot(flat[:, c * width : (c + 1) * width], weight[0, c], ((1,), (1,))) for c in range(3)
    )
    part[...] = total.astype(BF16)


def unproject(weight, grads):
    width = weight.shape[2]
    rows = grads.shape[1] * 2 // 3
    return kernel_call(
        unproject_kernel,
        "unproject",
        [VM] * 2,
        [shape_of(rows, 3 * weight.shape[3]), shape_of(rows, width)],
        (weight, grads),
        2 * rows * weight.size,
    )


def last_kernel(here, x, middle, gain, parts, out):
    quarter = middle.shape[0]
    grad = slot_sum(parts)
    centered, rate = stats(x[block_rows(here[1], quarter), :].astype(F32))
    out[...] = (middle[...] + norm_back(grad, centered * rate, rate, gain[0, 0:1])).astype(BF16)


def last_back(here, x, middle, gains, parts):
    return kernel_call(
        last_kernel,
        "last_back",
        [SM] + [VM] * 4,
        [shape_of(*middle.shape)],
        (here, x, middle, gains, parts),
        SHIELD,
    )[0]


def lay_kernel(here, *refs):
    parts, out = refs[:-1], refs[-1]
    for m, part in enumerate(parts):
        out[block_rows(here[1] ^ m, part.shape[0]), :] = part[...].astype(out.dtype)


def lay_rest_kernel(skip, here, *refs):
    n = (len(refs) - 3) // 2
    parts, out, rows, sems = refs[:n], refs[n + 1], refs[n + 2 : -1], refs[-1]
    spots = [block_rows(here[1] ^ (skip + m), part.shape[0]) for m, part in enumerate(parts)]
    for part, row in zip(parts, rows):
        row[...] = part[...].astype(row.dtype)
    for c in load_all([(row, out.at[spot]) for row, spot in zip(rows, spots)], sems):
        c.wait()


def lay_rest(skip, here, parts, base):
    return pl.pallas_call(
        functools.partial(lay_rest_kernel, skip),
        in_specs=[SM] + [VM] * len(parts) + [ANY],
        out_specs=ANY,
        out_shape=shape_of(*base.shape, dtype=base.dtype),
        scratch_shapes=[pltpu.VMEM(part.shape, base.dtype) for part in parts]
        + [pltpu.SemaphoreType.DMA((len(parts),))],
        input_output_aliases={1 + len(parts): 0},
        compiler_params=pltpu.CompilerParams(vmem_limit_bytes=10 * 2**20),
        name="lay_rest",
    )(here, *parts, base)


def lay(n_t, here, parts, dtype):
    quarter, width = parts[0].shape
    return kernel_call(
        lay_kernel,
        "lay",
        [SM] + [VM] * len(parts),
        [shape_of(n_t * quarter, width, dtype=dtype)],
        (here, *parts),
    )[0]


def for_sides(here, mine, theirs, work):
    for out, side in ((theirs, 1), (mine, 0)):

        def one(k, _, out=out, side=side):
            owner = 2 * k + (here[2] ^ side)
            work(out, k, pl.ds(pl.multiple_of(owner * 128, 128), 128))
            return 0

        lax.fori_loop(0, mine.shape[0], one, 0)


def sides(n_z, depth):
    return [shape_of(n_z, depth, 128, dtype=F32), shape_of(n_z, depth, 128)]


def put_lanes(out, k, first, block):
    for j in range(block.shape[1] // 128):
        out[k, first + j * 128 : first + (j + 1) * 128, :] = block[:, j * 128 : (j + 1) * 128]


def early_kernel(here, act, pre, normed, cot, mine, theirs):
    units = act.shape[1]

    def work(out, k, cut):
        out[k, :units, :] = dot(act[...], cot[:, cut], ((0,), (0,))).astype(out.dtype)
        put_lanes(out, k, units, dot(normed[:, cut], pre[...], ((0,), (0,))).astype(out.dtype))

    for_sides(here, mine, theirs, work)


def early_grads(n_z, here, act, pre, normed, cot):
    depth = 2 * act.shape[1]
    return kernel_call(
        early_kernel,
        "early_grads",
        [SM] + [VM] * 4,
        sides(n_z, depth),
        (here, act, pre, normed, cot),
        2 * act.shape[0] * depth * normed.shape[1],
    )


def halves(x):
    high = x.astype(BF16)
    return high, (x - high.astype(F32)).astype(BF16)


def outward_kernel(here, attended, *refs):
    mixed, (mine, theirs) = refs[:-2], refs[-2:]
    quarter = attended.shape[0] // len(mixed)

    def work(out, k, cut):
        outward = sum(
            dot(attended[block_rows(here[1] ^ m, quarter), :], part[-quarter:, cut], ((0,), (0,)))
            for m, part in enumerate(mixed)
        )
        out[k] = outward.astype(out.dtype)

    for_sides(here, mine, theirs, work)


def outward_grads(n_z, here, attended, mixed):
    rows, share = attended.shape
    return kernel_call(
        outward_kernel,
        "outward_grads",
        [SM] + [VM] * (1 + len(mixed)),
        sides(n_z, share),
        (here, attended, *mixed),
        2 * rows * share * mixed[0].shape[1],
    )


def fold_slots_kernel(here, mine, theirs, *outs):
    for k, out in enumerate(outs):
        at = lax.rem(here[0] + k, len(outs))
        out[...] = (mine[at] + theirs[at].astype(F32)).astype(out.dtype)


def fold_slots(here, mine, theirs):
    n_z, depth, _ = mine.shape
    return kernel_call(
        fold_slots_kernel,
        "fold_slots",
        [SM] + [VM] * 2,
        [shape_of(depth, 128, dtype=F32)] + [shape_of(depth, 128)] * (n_z - 1),
        (here, mine, theirs),
    )


def late_kernel(here, x, normed, grad, sums, part, mine, theirs, scratch):
    depth, step = grad.shape[1], 256
    total = jnp.zeros((2, x.shape[1]), F32)
    for m in range(x.shape[0] // step):
        spot = slice(m * step, (m + 1) * step)
        centered, rate = stats(x[spot, :].astype(F32))
        total = total + column_sums(part[spot, :].astype(F32), centered * rate)
    scratch[0:2, :] = total
    scratch[2:4, :] = sums[...]
    scratch[4:8, :] = jnp.zeros((4, x.shape[1]), F32)

    def work(out, k, cut):
        put_lanes(out, k, 0, dot(normed[:, cut], grad[...], ((0,), (0,))).astype(out.dtype))
        block = scratch[:, cut]
        if out.dtype == BF16:
            high, low = halves(block[0:4])
            block = jnp.concatenate([high.astype(F32), low.astype(F32)], axis=0).astype(BF16)
        out[k, depth:, :] = block

    for_sides(here, mine, theirs, work)


def late_grads(n_z, here, x, normed, grad, sums, part):
    depth = grad.shape[1] + 8
    return kernel_call(
        late_kernel,
        "late_grads",
        [SM] + [VM] * 5,
        sides(n_z, depth),
        (here, x, normed, grad, sums, part),
        2 * grad.shape[0] * depth * normed.shape[1],
        [pltpu.VMEM((8, x.shape[1]), F32)],
    )


def fold_kernel(mine, theirs, out):
    for k in range(mine.shape[0]):
        out[k] = (mine[k] + theirs[k].astype(F32)).astype(BF16)


def fold(mine, theirs):
    return kernel_call(
        fold_kernel, "fold", [VM] * 2, [shape_of(*mine.shape)], (mine, theirs)
    )[0]


def fold_late_kernel(mine, theirs, out):
    depth = mine.shape[1] - 8
    for k in range(mine.shape[0]):
        out[k, :depth] = (mine[k, :depth] + theirs[k, :depth].astype(F32)).astype(BF16)
        tail = mine[k, depth:] + theirs[k, depth:].astype(F32)
        high, low = halves(tail[0:4] + tail[4:8])
        both = jnp.concatenate([high.astype(F32), low.astype(F32)], axis=0)
        out[k, depth:] = both.astype(BF16)


def fold_late(mine, theirs):
    return kernel_call(
        fold_late_kernel, "fold_late", [VM] * 2, [shape_of(*mine.shape)], (mine, theirs)
    )[0]


def slot_sum(parts):
    return sum(parts[k].astype(F32) for k in range(parts.shape[0]))


def finish_early_kernel(parts, down_out, up_out):
    total = slot_sum(parts)
    units = down_out.shape[0]
    down_out[...] = total[:units]
    for j in range(units // 128):
        up_out[:, j * 128 : (j + 1) * 128] = total[units + j * 128 : units + (j + 1) * 128]


def finish_early(units, parts):
    return kernel_call(
        finish_early_kernel,
        "finish_early",
        [VM],
        [shape_of(units, 128, dtype=F32), shape_of(128, units, dtype=F32)],
        (parts,),
    )


def finish_late_kernel(parts, out, sums_out):
    total = slot_sum(parts)
    per = out.shape[2] // 128
    for c in range(3):
        for j in range(per):
            at = (c * per + j) * 128
            out[c, :, j * 128 : (j + 1) * 128] = total[at : at + 128]
    last = total.shape[0] - 8
    sums_out[...] = jnp.concatenate([total[last : last + 4] + total[last + 4 :]] * 2, axis=0)


def finish_late(share, parts):
    return kernel_call(
        finish_late_kernel,
        "finish_late",
        [VM],
        [
            shape_of(3, 128, share, dtype=F32),
            shape_of(8, 128, dtype=F32),
        ],
        (parts,),
    )


def scene_edges(scene_index):
    total = scene_index.shape[0]
    at = lax.iota(jnp.int32, total)
    edge = jnp.concatenate([jnp.ones((1,), jnp.bool_), scene_index[1:] != scene_index[:-1]])
    starts = lax.cummax(jnp.where(edge, at, 0))
    closing = jnp.concatenate([edge[1:], jnp.ones((1,), jnp.bool_)])
    return starts, lax.cummin(jnp.where(closing, at + 1, total), reverse=True)


def body(
    n_seq,
    n_tp,
    tokens,
    scene_index,
    inward_weight,
    outward_weight,
    up_weight,
    down_weight,
    norm_gains,
    norm_shifts,
    cotangent,
):
    n_z, rows, width = n_seq // 2, tokens.shape[0], tokens.shape[1]
    units, share = up_weight.shape[2], outward_weight.shape[1]
    quarter = rows // n_tp
    seq, tp = lax.axis_index("seq"), lax.axis_index("tp")
    z, c = seq // 2, seq % 2
    here = jnp.stack([z, tp, c]).astype(jnp.int32)
    lines = [list(range(b, n_seq, 2)) for b in range(2)]

    def line(x):
        return lax.all_to_all(x, "seq", 0, 0, axis_index_groups=lines, tiled=True)

    def plane(x):
        return lax.all_to_all(x, "tp", 0, 0, tiled=True)

    def across(x):
        return lax.ppermute(x, "seq", [(a, a ^ 1) for a in range(n_seq)])

    def along(x, k):
        return lax.ppermute(
            x, "seq", [(a * 2 + b, (a + k) % n_z * 2 + b) for a in range(n_z) for b in range(2)]
        )

    def over(x, m):
        return lax.ppermute(x, "tp", [(a, a ^ m) for a in range(n_tp)])

    def square(slots):
        return [slots[0]] + [over(slots[m], m) for m in range(1, n_tp)]

    place = jnp.stack([k * 2 + (c ^ g) for g in range(2) for k in range(n_z)]).astype(jnp.int32)
    starts, ends = scene_edges(scene_index)
    normed, kv_send, q_send = project(n_z, here, tokens, norm_gains, norm_shifts, inward_weight)
    kv_mine = line(kv_send)
    q = [q_send[0]] + [along(q_send[k], k) for k in range(1, n_z)]
    (kv_mine, starts, ends, place, q) = lax.optimization_barrier((kv_mine, starts, ends, place, q))
    kv_other = across(kv_mine)
    outward_all = square([outward_weight[0]] * n_tp)
    o, o_full, lse, kv_full = attn_fwd(kv_mine, kv_other, q, here, place, starts, ends, 1024)
    (o, outward_all) = lax.optimization_barrier((o, outward_all))
    attended = spread(line(o))
    parts = plane(attended.reshape(n_tp, quarter, share))
    after, normed_two = mix(here, tokens, norm_gains, norm_shifts, parts, outward_all)
    act, pre, normed_two, grad_parts = hidden_layer(
        here, square([normed_two] * n_tp), cotangent, up_weight, down_weight
    )
    middle, mixed, sums_two, grads = middle_back(
        here, after, cotangent, norm_gains, square(grad_parts), outward_all
    )
    mine, theirs = early_grads(n_z, here, act, pre, normed_two, cotangent)
    early = fold(mine, across(theirs))
    branch = branch_parts(n_tp, here, act, down_weight, mixed)
    grads = plane(grads)
    (grads, early, branch) = lax.optimization_barrier((grads, early, branch))
    g = pack(n_z, here, grads.reshape(rows, share))
    g = [g[0]] + [along(g[k], k) for k in range(1, n_z)]
    (g, early) = lax.optimization_barrier((g, early))
    early = line(early)
    branch = square(branch)
    dq, dkv, dkv_theirs = attn_bwd(kv_full, q, g, o_full, lse, here, place, starts, ends, 1024)
    (dq, dkv, dkv_theirs, branch) = lax.optimization_barrier((dq, dkv, dkv_theirs, branch))
    mixed = [mixed] + branch[1:]
    back = join(dkv, across(dkv_theirs), dq)
    (back, early) = lax.optimization_barrier((back, early))
    back = line(back)
    out_own = (after + sum(part[:quarter].astype(F32) for part in branch)).astype(BF16)
    out_slots = square([out_own] * n_tp)
    down_grad, up_grad = finish_early(units, early)
    activations = lay(n_tp, here, out_slots, BF16)
    mine, theirs = outward_grads(n_z, here, attended, mixed)
    side = fold_slots(here, mine, across(theirs))
    (back, activations, down_grad, up_grad, side) = lax.optimization_barrier(
        (back, activations, down_grad, up_grad, side)
    )
    side = [side[0]] + [along(side[k], k) for k in range(1, n_z)]
    flat, back_part = unproject(inward_weight, back)
    mine, theirs = late_grads(n_z, here, tokens, normed, flat, sums_two, back_part)
    late = fold_late(mine, across(theirs))
    back_part = plane(back_part.reshape(n_tp, quarter, width))
    (back_part, late, side) = lax.optimization_barrier((back_part, late, side))
    outward_grad = sum(part.astype(F32) for part in side)
    token_own = last_back(here, tokens, middle, norm_gains, back_part)
    late = line(late)
    token_slots = square([token_own] * n_tp)
    token_grad = lay(n_tp, here, token_slots[:2], F32)
    (late, token_grad, outward_grad) = lax.optimization_barrier((late, token_grad, outward_grad))
    inward_grad, sums = finish_late(share, late)
    sums = square([sums] * n_tp)
    (sums, token_slots) = lax.optimization_barrier((sums, token_slots))
    token_grad = lay_rest(2, here, token_slots[2:], token_grad)
    while len(sums) > 1:
        sums = [sums[m] + sums[m + 1] for m in range(0, len(sums), 2)]
    sums = sums[0]
    gain_grad = jnp.stack([sums[0], sums[2]])
    shift_grad = jnp.stack([sums[1], sums[3]])
    return (
        activations,
        token_grad,
        inward_grad[None],
        outward_grad[None],
        up_grad[None],
        down_grad[None],
        gain_grad[None],
        shift_grad[None],
    )


def layer_norm(hidden, gain_row, shift_row):
    average = jnp.mean(hidden, axis=-1, keepdims=True)
    centered = hidden - average
    variance = jnp.mean(centered * centered, axis=-1, keepdims=True)
    return centered * lax.rsqrt(variance + 1e-05) * gain_row + shift_row


def gelu_tanh(preactivation):
    return jax.nn.gelu(preactivation, approximate=True)


def to_heads(flat_rows):
    return flat_rows.reshape(flat_rows.shape[0], -1, HEAD_DIM)


def scenes_meet(query_scenes, key_scenes):
    return jnp.logical_and(key_scenes[0] <= query_scenes[-1], key_scenes[-1] >= query_scenes[0])


def score_rows(query_heads, key_heads, query_scenes, key_scenes):
    scores = jnp.einsum(
        "qhd,khd->hqk", query_heads, key_heads, preferred_element_type=jnp.float32
    ) * HEAD_DIM ** (-0.5)
    same_scene = (query_scenes[:, None] == key_scenes[None, :])[None]
    return (scores, same_scene)


def probabilities(scores, same_scene, normalizer):
    return jnp.where(same_scene, jnp.exp(scores - normalizer[:, :, None]), 0.0)


def key_tiles(key_all, value_all, scene_index):
    tile_rows = min(1024, key_all.shape[0])
    tile_count = key_all.shape[0] // tile_rows
    return (
        key_all.reshape(tile_count, tile_rows, -1, HEAD_DIM),
        value_all.reshape(tile_count, tile_rows, -1, HEAD_DIM),
        scene_index.reshape(tile_count, tile_rows),
    )


def log_normalizer(query_heads, query_scenes, tiled_keys):

    def log_visit_tile(running_pair, inputs_pair):
        key_heads, key_scenes = inputs_pair

        def log_compute(pair_now):
            running_max, running_sum = pair_now
            scores, same_scene = score_rows(query_heads, key_heads, query_scenes, key_scenes)
            masked = jnp.where(same_scene, scores, NEG_FILL)
            new_max = jnp.maximum(running_max, jnp.max(masked, axis=-1))
            weights = jnp.where(same_scene, jnp.exp(masked - new_max[:, :, None]), 0.0)
            return (
                new_max,
                running_sum * jnp.exp(running_max - new_max) + jnp.sum(weights, axis=-1),
            )

        return (
            lax.cond(
                scenes_meet(query_scenes, key_scenes),
                log_compute,
                lambda pair_now: pair_now,
                running_pair,
            ),
            None,
        )

    stat_shape = (query_heads.shape[1], query_heads.shape[0])
    start_pair = (jnp.full(stat_shape, NEG_FILL, jnp.float32), jnp.zeros(stat_shape, jnp.float32))
    final_pair, _ = lax.scan(log_visit_tile, start_pair, (tiled_keys[0], tiled_keys[2]))
    return final_pair[0] + jnp.log(final_pair[1])


def attend_all(query_heads, query_scenes, tiled_keys, normalizer):

    def attend_visit_tile(running_total, inputs_triple):
        key_heads, value_heads, key_scenes = inputs_triple

        def attend_compute(total_now):
            scores, same_scene = score_rows(query_heads, key_heads, query_scenes, key_scenes)
            weights = probabilities(scores, same_scene, normalizer).astype(jnp.bfloat16)
            return total_now + jnp.einsum(
                "hqk,khd->qhd", weights, value_heads, preferred_element_type=jnp.float32
            )

        return (
            lax.cond(
                scenes_meet(query_scenes, key_scenes),
                attend_compute,
                lambda total_now: total_now,
                running_total,
            ),
            None,
        )

    running_total, _ = lax.scan(
        attend_visit_tile, jnp.zeros(query_heads.shape, jnp.float32), tiled_keys
    )
    return running_total.reshape(running_total.shape[0], -1)


def score_gradients(
    query_heads,
    key_heads,
    value_heads,
    grad_heads,
    query_scenes,
    key_scenes,
    normalizer,
    delta_rows,
):
    scores, same_scene = score_rows(query_heads, key_heads, query_scenes, key_scenes)
    weights = probabilities(scores, same_scene, normalizer)
    weight_grad = jnp.einsum(
        "qhd,khd->hqk", grad_heads, value_heads, preferred_element_type=jnp.float32
    )
    score_grad = (weights * (weight_grad - delta_rows[:, :, None])).astype(jnp.bfloat16)
    return (weights.astype(jnp.bfloat16), score_grad)


def grads_by_reduce(query_heads, grad_heads, query_scenes, tiled_keys, normalizer, delta_rows):
    tile_rows = tiled_keys[0].shape[1]
    joined_width = 2 * query_heads.shape[1] * query_heads.shape[2]

    def grads_visit_tile(query_total, inputs_triple):
        key_heads, value_heads, key_scenes = inputs_triple

        def grads_compute(total_now):
            weights, score_grad = score_gradients(
                query_heads,
                key_heads,
                value_heads,
                grad_heads,
                query_scenes,
                key_scenes,
                normalizer,
                delta_rows,
            )
            total_now = total_now + jnp.einsum(
                "hqk,khd->qhd", score_grad, key_heads, preferred_element_type=jnp.float32
            )
            key_term = jnp.einsum(
                "hqk,qhd->khd", score_grad, query_heads, preferred_element_type=jnp.float32
            )
            value_term = jnp.einsum(
                "hqk,qhd->khd", weights, grad_heads, preferred_element_type=jnp.float32
            )
            joined = jnp.concatenate(
                [key_term.reshape(tile_rows, -1), value_term.reshape(tile_rows, -1)], axis=1
            )
            return (total_now, joined)

        def skipped(total_now):
            return (total_now, jnp.zeros((tile_rows, joined_width), jnp.float32))

        return lax.cond(scenes_meet(query_scenes, key_scenes), grads_compute, skipped, query_total)

    query_total, key_terms_all = lax.scan(
        grads_visit_tile, jnp.zeros(query_heads.shape, jnp.float32), tiled_keys
    )
    key_terms_all = key_terms_all.reshape(-1, key_terms_all.shape[-1])
    summed = lax.psum_scatter(key_terms_all, "seq", scatter_dimension=0, tiled=True)
    half_width = summed.shape[1] // 2
    return (
        query_total.reshape(query_total.shape[0], -1),
        summed[:, :half_width],
        summed[:, half_width:],
    )


def generic_body(
    tokens,
    scene_index,
    inward_weight,
    outward_weight,
    up_weight,
    down_weight,
    norm_gains,
    norm_shifts,
    cotangent,
):
    local_rows = tokens.shape[0]
    score_factor = HEAD_DIM ** (-0.5)
    query_scenes = lax.dynamic_slice_in_dim(
        scene_index, lax.axis_index("seq") * local_rows, local_rows
    )
    hidden = tokens.astype(jnp.float32)
    layer_number = 0
    gain_pair = norm_gains[layer_number]
    shift_pair = norm_shifts[layer_number]
    normed = layer_norm(hidden, gain_pair[0], shift_pair[0]).astype(jnp.bfloat16)
    projected = jnp.einsum(
        "td,cde->tce", normed, inward_weight[layer_number], preferred_element_type=jnp.float32
    ).astype(jnp.bfloat16)
    queries = projected[:, 0]
    key_local = projected[:, 1]
    value_local = projected[:, 2]
    key_all = lax.all_gather(key_local, "seq", axis=0, tiled=True)
    value_all = lax.all_gather(value_local, "seq", axis=0, tiled=True)
    tiled_keys = key_tiles(key_all, value_all, scene_index)
    query_heads = to_heads(queries)
    normalizer = log_normalizer(query_heads, query_scenes, tiled_keys)
    attended = attend_all(query_heads, query_scenes, tiled_keys, normalizer)
    attended_low = attended.astype(jnp.bfloat16)
    mixed_sum = lax.psum(
        jnp.dot(attended_low, outward_weight[layer_number], preferred_element_type=jnp.float32),
        "tp",
    )
    after_attention = hidden + mixed_sum
    normed_two = layer_norm(after_attention, gain_pair[1], shift_pair[1]).astype(jnp.bfloat16)
    preactivation = jnp.dot(normed_two, up_weight[layer_number], preferred_element_type=jnp.float32)
    activated = gelu_tanh(preactivation).astype(jnp.bfloat16)
    branch = lax.psum(
        jnp.dot(activated, down_weight[layer_number], preferred_element_type=jnp.float32), "tp"
    )
    kept_layers = [
        (
            hidden,
            after_attention,
            queries,
            key_local,
            value_local,
            tiled_keys,
            normalizer,
            attended,
            attended_low,
            preactivation,
            activated,
        )
    ]
    hidden = after_attention + branch
    upstream = cotangent.astype(jnp.float32)
    layer_grads = [None] * LAYERS
    for layer_number in reversed(range(LAYERS)):
        (
            hidden_in,
            after_attention,
            queries,
            key_local,
            value_local,
            tiled_keys,
            normalizer,
            attended,
            attended_low,
            preactivation,
            activated,
        ) = kept_layers[layer_number]
        gain_pair = norm_gains[layer_number]
        shift_pair = norm_shifts[layer_number]
        branch_grad = upstream.astype(jnp.bfloat16)
        down_grad = jnp.einsum(
            "tf,td->fd", activated, branch_grad, preferred_element_type=jnp.float32
        )
        act_grad = jnp.einsum(
            "td,fd->tf", branch_grad, down_weight[layer_number], preferred_element_type=jnp.float32
        )
        _, gelu_pull = jax.vjp(gelu_tanh, preactivation)
        preactivation_grad = gelu_pull(act_grad)[0].astype(jnp.bfloat16)
        normed_two_f, norm_pull_two = jax.vjp(
            layer_norm, after_attention, gain_pair[1], shift_pair[1]
        )
        normed_two = normed_two_f.astype(jnp.bfloat16)
        up_grad = jnp.einsum(
            "td,tf->df", normed_two, preactivation_grad, preferred_element_type=jnp.float32
        )
        normed_two_grad = lax.psum(
            jnp.einsum(
                "tf,df->td",
                preactivation_grad,
                up_weight[layer_number],
                preferred_element_type=jnp.float32,
            ),
            "tp",
        )
        middle_part, gain_two, shift_two = norm_pull_two(normed_two_grad)
        middle_grad = upstream + middle_part
        mixed_grad = middle_grad.astype(jnp.bfloat16)
        outward_grad = jnp.einsum(
            "te,td->ed", attended_low, mixed_grad, preferred_element_type=jnp.float32
        )
        attended_grad = jnp.einsum(
            "td,ed->te",
            mixed_grad,
            outward_weight[layer_number],
            preferred_element_type=jnp.float32,
        ).astype(jnp.bfloat16)
        delta_rows = jnp.sum(to_heads(attended_grad.astype(jnp.float32) * attended), axis=-1).T
        query_sum, key_sum, value_sum = grads_by_reduce(
            to_heads(queries),
            to_heads(attended_grad),
            query_scenes,
            tiled_keys,
            normalizer,
            delta_rows,
        )
        projected_grad = jnp.stack(
            [query_sum * score_factor, key_sum * score_factor, value_sum], axis=1
        ).astype(jnp.bfloat16)
        normed_f, norm_pull = jax.vjp(layer_norm, hidden_in, gain_pair[0], shift_pair[0])
        normed = normed_f.astype(jnp.bfloat16)
        inward_grad = jnp.einsum(
            "td,tce->cde", normed, projected_grad, preferred_element_type=jnp.float32
        )
        normed_grad = lax.psum(
            jnp.einsum(
                "tce,cde->td",
                projected_grad,
                inward_weight[layer_number],
                preferred_element_type=jnp.float32,
            ),
            "tp",
        )
        input_part, gain_one, shift_one = norm_pull(normed_grad)
        upstream = middle_grad + input_part
        layer_grads[layer_number] = (
            lax.psum_scatter(inward_grad, "seq", scatter_dimension=1, tiled=True),
            lax.psum_scatter(outward_grad, "seq", scatter_dimension=1, tiled=True),
            lax.psum_scatter(up_grad, "seq", scatter_dimension=0, tiled=True),
            lax.psum_scatter(down_grad, "seq", scatter_dimension=1, tiled=True),
            lax.psum_scatter(
                jnp.stack([gain_one, gain_two]), "seq", scatter_dimension=1, tiled=True
            ),
            lax.psum_scatter(
                jnp.stack([shift_one, shift_two]), "seq", scatter_dimension=1, tiled=True
            ),
        )
    return (
        hidden.astype(jnp.bfloat16),
        upstream,
        jnp.stack([layer_part[0] for layer_part in layer_grads]),
        jnp.stack([layer_part[1] for layer_part in layer_grads]),
        jnp.stack([layer_part[2] for layer_part in layer_grads]),
        jnp.stack([layer_part[3] for layer_part in layer_grads]),
        jnp.stack([layer_part[4] for layer_part in layer_grads]),
        jnp.stack([layer_part[5] for layer_part in layer_grads]),
    )


def solution(mesh):
    placed = (
        P("seq", None),
        P(),
        P(None, None, None, "tp"),
        P(None, "tp", None),
        P(None, None, "tp"),
        P(None, "tp", None),
        P(),
        P(),
        P("seq", None),
    )
    n_seq, n_tp = mesh.shape["seq"], mesh.shape["tp"]
    fits = n_seq == 8 and n_tp == 4
    return jax.shard_map(
        functools.partial(body, n_seq, n_tp) if fits else generic_body,
        mesh=mesh,
        in_specs=placed,
        out_specs=(
            P("seq", None),
            P("seq", None),
            P(None, None, "seq", "tp"),
            P(None, "tp", "seq"),
            P(None, "seq", "tp"),
            P(None, "tp", "seq"),
            P(None, None, "seq"),
            P(None, None, "seq"),
        ),
        check_vma=False,
    )
```

```python
import functools
import math
import jax
import jax.numpy as jnp
from jax import lax
from jax.experimental import pallas as pl
from jax.experimental.pallas import tpu as pltpu
from jax.sharding import PartitionSpec as P

HEAD_DIM = 64
LAYERS = 1
F32, BF16 = jnp.float32, jnp.bfloat16
NEG_FILL = -1e30
SCORE = HEAD_DIM ** -0.5
LOG2E = math.log2(math.e)
ANY = pl.BlockSpec(memory_space=pl.ANY)
VM = pl.BlockSpec(memory_space=pltpu.VMEM)
SM = pl.BlockSpec(memory_space=pltpu.SMEM)
FWD_PARAMS = pltpu.CompilerParams(vmem_limit_bytes=58 * 2**20)
BWD_PARAMS = pltpu.CompilerParams(vmem_limit_bytes=58 * 2**20)


def dot(a, b, dims):
    return lax.dot_general(a, b, (dims, ((), ())), preferred_element_type=F32)


def load_all(pairs, sems):
    copies = [pltpu.make_async_copy(s, d, sems.at[i]) for i, (s, d) in enumerate(pairs)]
    for c in copies:
        c.start()
    return copies


def for_tiles(first, last, starts, ends, bk, visit):
    edge = bk // 2
    begin, stop = starts[first], ends[last]
    low, high = begin // edge, (stop + edge - 1) // edge
    clear0 = jnp.where(ends[first] == stop, (begin + edge - 1) // edge, high)
    count = jnp.maximum(stop // edge - clear0, 0) // 2
    head = clear0 - low

    def masked(i, _):
        j = jnp.where(i < head, low + i, clear0 + 2 * count + i - head)
        visit(pl.multiple_of(j * edge, edge), edge, True)
        return 0

    def clear(i, _):
        visit(pl.multiple_of((clear0 + 2 * i) * edge, edge), bk, False)
        return 0

    lax.fori_loop(0, high - low - 2 * count, masked, 0)
    lax.fori_loop(0, count, clear, 0)


def low_half(x):
    lane = lax.broadcasted_iota(jnp.int32, x.shape, 1)
    return jnp.where(lane < HEAD_DIM, x, jnp.zeros_like(x))


def high_half(x):
    lane = lax.broadcasted_iota(jnp.int32, x.shape, 1)
    return jnp.where(lane < HEAD_DIM, jnp.zeros_like(x), x)


def swap_halves(x):
    return jnp.concatenate([x[:, HEAD_DIM:], x[:, :HEAD_DIM]], axis=1)


def fwd_kernel(bk, here, place, starts, ends, begin_rows, stop_rows, mine, other, *refs):
    n_q = mine.shape[0]
    q_in, refs = refs[:n_q], refs[n_q:]
    o_out, of_out, lse_out, kv, vt, qz, acc, top, ot, sems = refs
    half = q_in[0].shape[0]
    rows = 2 * half
    spots = [pl.ds(pl.multiple_of(place[i] * rows, 128), rows) for i in range(2 * n_q)]
    copies = load_all(
        [(mine.at[k], kv.at[spots[k]]) for k in range(n_q)]
        + [(other.at[k], kv.at[spots[n_q + k]]) for k in range(n_q)],
        sems,
    )
    for s in range(n_q):
        k = lax.rem(here[0] + n_q - s, n_q)
        q = q_in[s][...]
        qz[2 * k] = low_half(q)
        qz[2 * k + 1] = low_half(swap_halves(q))
    for c in copies:
        c.wait()

    def turn(j, _):
        spot = pl.ds(pl.multiple_of(j * 256, 256), 256)
        vt[:HEAD_DIM, spot] = kv[spot, :].T[HEAD_DIM:]
        vt[HEAD_DIM:, spot] = jnp.ones((16, 256), BF16)
        return 0

    lax.fori_loop(0, kv.shape[0] // 256, turn, 0)
    factor = SCORE * LOG2E

    def one(i, _):
        first = place[i // 2] * rows + (i % 2) * half
        query = qz[i]
        acc[...] = jnp.zeros_like(acc)
        top[0:1] = jnp.full((1, half), NEG_FILL, F32)
        slab = first // half

        def visit(at, size, mask):
            step = bk // 2
            spots = [pl.ds(pl.multiple_of(at + s * step, step), step) for s in range(size // step)]
            best, total = top[0:1], acc[...]
            ahead = dot(kv[spots[0], :], query, ((1,), (1,)))
            for s, spot in enumerate(spots):
                st = ahead
                if s + 1 < len(spots):
                    ahead = dot(kv[spots[s + 1], :], query, ((1,), (1,)))
                if mask:
                    key = at + s * step + lax.broadcasted_iota(jnp.int32, st.shape, 0)
                    inside = (key >= begin_rows[slab]) & (key < stop_rows[slab])
                    st = jnp.where(inside, st, NEG_FILL)
                new = jnp.maximum(best, jnp.max(st, axis=0, keepdims=True))
                p = jnp.exp2(st * factor - new * factor)
                shrink = jnp.exp2((best - new) * factor)
                best = new
                total = total * shrink + dot(vt[:, spot], p.astype(BF16), ((1,), (0,)))
            top[0:1] = best
            acc[...] = total

        for_tiles(first, first + half - 1, starts, ends, bk, visit)
        weight = acc[HEAD_DIM : HEAD_DIM + 1]
        ot[i] = acc[:HEAD_DIM] / weight
        lse_out[i] = top[0:1] * factor + jnp.log2(weight)
        return 0

    lax.fori_loop(0, 2 * n_q, one, 0)
    for k in range(n_q):
        joined = jnp.concatenate([ot[2 * k], ot[2 * k + 1]], axis=0).T
        of_out[k] = joined
        o_out[k] = joined.astype(BF16)


def attn_fwd(mine, other, q, here, place, starts, ends, bk):
    n_q, half = len(q), q[0].shape[0]
    total = starts.shape[0]
    return pl.pallas_call(
        functools.partial(fwd_kernel, bk),
        in_specs=[SM, SM, SM, SM, VM, VM, ANY, ANY] + [VM] * n_q,
        out_specs=[VM] * 4,
        out_shape=[
            jax.ShapeDtypeStruct((n_q, half, 128), BF16),
            jax.ShapeDtypeStruct((n_q, half, 128), F32),
            jax.ShapeDtypeStruct((2 * n_q, 1, half), F32),
            jax.ShapeDtypeStruct((total, 128), BF16),
        ],
        scratch_shapes=[
            pltpu.VMEM((HEAD_DIM + 16, total), BF16),
            pltpu.VMEM((2 * n_q, half, 128), BF16),
            pltpu.VMEM((HEAD_DIM + 16, half), F32),
            pltpu.VMEM((8, half), F32),
            pltpu.VMEM((2 * n_q, HEAD_DIM, half), F32),
            pltpu.SemaphoreType.DMA((2 * n_q,)),
        ],
        compiler_params=FWD_PARAMS,
        cost_estimate=pl.CostEstimate(flops=3 * 10**10, bytes_accessed=2**22, transcendentals=0),
        name="attend",
    )(
        here,
        place,
        starts,
        ends,
        starts.reshape(-1, 1, half),
        ends.reshape(-1, 1, half),
        mine,
        other,
        *q,
    )


def bwd_kernel(bk, here, place, starts, ends, begin_rows, stop_rows, kv_hbm, lse, of, *refs):
    n_q, half = of.shape[:2]
    q_in, g_in, refs = refs[:n_q], refs[n_q : 2 * n_q], refs[2 * n_q :]
    dq_out, dkv_out, theirs, kv, kt, qg, delta, dkv, dqt_all, acc, sems = refs
    rows = 2 * half
    copies = load_all([(kv_hbm, kv)], sems)
    for s in range(n_q):
        k = lax.rem(here[0] + n_q - s, n_q)
        q, g = q_in[s][...], g_in[s][...]
        qg[2 * k, :half] = low_half(q)
        qg[2 * k + 1, :half] = low_half(swap_halves(q))
        qg[2 * k, half:] = high_half(swap_halves(g))
        qg[2 * k + 1, half:] = high_half(g)
        prod = (g.astype(F32) * of[k]).T
        delta[2 * k] = jnp.sum(prod[:HEAD_DIM], axis=0, keepdims=True)
        delta[2 * k + 1] = jnp.sum(prod[HEAD_DIM:], axis=0, keepdims=True)
    copies[0].wait()

    def turn(j, _):
        spot = pl.ds(pl.multiple_of(j * 256, 256), 256)
        kt[:, spot] = kv[spot, :].T[:HEAD_DIM]
        dkv[spot, :] = jnp.zeros((256, 128), F32)
        return 0

    lax.fori_loop(0, kv.shape[0] // 256, turn, 0)
    factor = SCORE * LOG2E

    def one(i, _):
        first = place[i // 2] * rows + (i % 2) * half
        both, lse_row, delta_row = qg[i], lse[i], delta[i]
        query, grad = both[:half], both[half:]
        acc[...] = jnp.zeros_like(acc)
        slab = first // half

        def visit(at, size, mask):
            spot = pl.ds(at, size)
            pair = dot(kv[spot, :], both, ((1,), (1,)))
            p = jnp.exp2(pair[:, :half] * factor - lse_row)
            if mask:
                key = at + lax.broadcasted_iota(jnp.int32, p.shape, 0)
                p = jnp.where((key >= begin_rows[slab]) & (key < stop_rows[slab]), p, 0.0)
            ds = (p * (pair[:, half:] - delta_row)).astype(BF16)
            dkv[spot, :] += dot(ds, query, ((1,), (0,))) + dot(p.astype(BF16), grad, ((1,), (0,)))
            acc[...] += dot(kt[:, spot], ds, ((1,), (0,)))

        for_tiles(first, first + half - 1, starts, ends, bk, visit)
        dqt_all[i] = acc[...] * SCORE
        return 0

    lax.fori_loop(0, 2 * n_q, one, 0)
    for k in range(n_q):
        joined = jnp.concatenate([dqt_all[2 * k], dqt_all[2 * k + 1]], axis=0).T
        dq_out[k] = joined.astype(BF16)
    for k in range(n_q):
        dkv_out[k] = dkv[pl.ds(pl.multiple_of(place[k] * rows, 128), rows), :]
        other = pl.ds(pl.multiple_of(place[n_q + k] * rows, 128), rows)
        theirs[k] = dkv[other, :].astype(BF16)


def attn_bwd(kv, q, g, of, lse, here, place, starts, ends, bk):
    n_q, half = len(q), q[0].shape[0]
    total = starts.shape[0]
    return pl.pallas_call(
        functools.partial(bwd_kernel, bk),
        in_specs=[SM, SM, SM, SM, VM, VM, ANY] + [VM] * (2 + 2 * n_q),
        out_specs=[VM] * 3,
        out_shape=[
            jax.ShapeDtypeStruct((n_q, half, 128), BF16),
            jax.ShapeDtypeStruct((n_q, 2 * half, 128), F32),
            jax.ShapeDtypeStruct((n_q, 2 * half, 128), BF16),
        ],
        scratch_shapes=[
            pltpu.VMEM((total, 128), BF16),
            pltpu.VMEM((HEAD_DIM, total), BF16),
            pltpu.VMEM((2 * n_q, 2 * half, 128), BF16),
            pltpu.VMEM((2 * n_q, 1, half), F32),
            pltpu.VMEM((total, 128), F32),
            pltpu.VMEM((2 * n_q, HEAD_DIM, half), F32),
            pltpu.VMEM((HEAD_DIM, half), F32),
            pltpu.SemaphoreType.DMA((1,)),
        ],
        compiler_params=BWD_PARAMS,
        cost_estimate=pl.CostEstimate(flops=4 * 10**10, bytes_accessed=2**22, transcendentals=0),
        name="attend_back",
    )(
        here,
        place,
        starts,
        ends,
        starts.reshape(-1, 1, half),
        ends.reshape(-1, 1, half),
        kv,
        lse,
        of,
        *q,
        *g,
    )


SHIELD = 3 * 10**10
ROOM = 6 * 2**20
WIDE = 58 * 2**20


def stats(x):
    average = jnp.mean(x, axis=-1, keepdims=True)
    centered = x - average
    variance = jnp.mean(centered * centered, axis=-1, keepdims=True)
    return centered, lax.rsqrt(variance + 1e-05)


def norm_back(grad, xhat, rate, gain):
    scaled = grad * gain
    return rate * (
        scaled
        - jnp.mean(scaled, axis=-1, keepdims=True)
        - xhat * jnp.mean(scaled * xhat, axis=-1, keepdims=True)
    )


def column_sums(grad, xhat):
    return jnp.concatenate(
        [jnp.sum(grad * xhat, axis=0, keepdims=True), jnp.sum(grad, axis=0, keepdims=True)], axis=0
    )


def shape_of(*dims, dtype=BF16):
    return jax.ShapeDtypeStruct(dims, dtype)


def kernel_call(kernel, name, specs, outs, args, flops=0, scratch=(), room=ROOM):
    size = sum(a.size * a.dtype.itemsize for a in list(args) + list(outs))
    return pl.pallas_call(
        kernel,
        in_specs=specs,
        out_specs=[VM] * len(outs),
        out_shape=outs,
        scratch_shapes=list(scratch),
        compiler_params=pltpu.CompilerParams(vmem_limit_bytes=min(size + room, WIDE)),
        cost_estimate=pl.CostEstimate(flops=flops, bytes_accessed=size, transcendentals=0),
        name=name,
    )(*args)


def block_rows(index, count):
    return pl.ds(pl.multiple_of(index * count, 16), count)


def head_cut(h):
    return slice(h * HEAD_DIM, (h + 1) * HEAD_DIM)


def project_kernel(here, x, gain, shift, weight, normed_out, kv_out, *refs):
    q_out, q_flat = refs[:-1], refs[-1]
    n_z, half = len(q_out), x.shape[0] // 2
    for t in range(2):
        spot = slice(t * half, (t + 1) * half)
        centered, rate = stats(x[spot, :].astype(F32))
        normed = (centered * rate * gain[0, 0:1] + shift[0, 0:1]).astype(BF16)
        normed_out[spot, :] = normed
        q, k, v = [dot(normed, weight[0, c], ((1,), (0,))).astype(BF16) for c in range(3)]
        q_flat[spot, :] = q
        for h in range(n_z):
            kv_out[h, spot, :] = jnp.concatenate([k[:, head_cut(h)], v[:, head_cut(h)]], axis=1)
    put_slots(here, q_out, q_flat)


def put_slots(here, outs, flat):
    n_z, half = len(outs), outs[0].shape[0]
    for h in range(n_z):
        block = jnp.concatenate([flat[:half, head_cut(h)], flat[half:, head_cut(h)]], axis=1)
        for k, out in enumerate(outs):

            @pl.when(lax.rem(here[0] + k, n_z) == h)
            def _(out=out, block=block):
                out[...] = block


def project(n_z, here, x, gains, shifts, weight):
    rows, width = x.shape
    outs = kernel_call(
        project_kernel,
        "project",
        [SM] + [VM] * 4,
        [shape_of(rows, width), shape_of(n_z, rows, 128)] + [shape_of(rows // 2, 128)] * n_z,
        (here, x, gains, shifts, weight),
        2 * rows * weight.size,
        [pltpu.VMEM((rows, n_z * HEAD_DIM), BF16)],
        room=WIDE,
    )
    return outs[0], outs[1], outs[2:]


def spread_kernel(o_in, out):
    n_z, half = o_in.shape[:2]
    out[:half, :] = jnp.concatenate([o_in[h, :, :HEAD_DIM] for h in range(n_z)], axis=1)
    out[half:, :] = jnp.concatenate([o_in[h, :, HEAD_DIM:] for h in range(n_z)], axis=1)


def spread(o):
    n_z, half = o.shape[:2]
    return kernel_call(spread_kernel, "spread", [VM], [shape_of(2 * half, n_z * HEAD_DIM)], (o,))[0]


def pack_kernel(here, x, *outs):
    put_slots(here, outs, x)


def pack(n_z, here, x):
    return kernel_call(
        pack_kernel, "pack", [SM, VM], [shape_of(x.shape[0] // 2, 128)] * n_z, (here, x)
    )


def mix_kernel(here, x, gain, shift, parts, *refs):
    weights, (after_out, normed_out) = refs[:-2], refs[-2:]
    quarter = parts.shape[1]
    mixed = sum(dot(parts[here[1] ^ m], w[...], ((1,), (0,))) for m, w in enumerate(weights))
    after = x[block_rows(here[1], quarter), :].astype(F32) + mixed
    after_out[...] = after
    centered, rate = stats(after)
    normed_out[...] = (centered * rate * gain[0, 1:2] + shift[0, 1:2]).astype(BF16)


def mix(here, x, gains, shifts, parts, weights):
    n_t, quarter, width = parts.shape[0], parts.shape[1], x.shape[1]
    return kernel_call(
        mix_kernel,
        "mix",
        [SM] + [VM] * (4 + n_t),
        [shape_of(quarter, width, dtype=F32), shape_of(quarter, width)],
        (here, x, gains, shifts, parts, *weights),
        2 * quarter * width * width,
    )


def gelu_pair(u):
    c = math.sqrt(2.0 / math.pi)
    square = u * u
    t = jnp.tanh(c * (u + 0.044715 * square * u))
    slope = 0.5 * (1.0 + t) + 0.5 * u * (1.0 - t * t) * c * (1.0 + 3 * 0.044715 * square)
    return 0.5 * u * (1.0 + t), slope


def hidden_kernel(n_t, here, cot, up, down, *refs):
    slots, (act_out, pre_out, normed), parts = refs[:n_t], refs[n_t : n_t + 3], refs[n_t + 3 :]
    quarter, tile = slots[0].shape[0], 256
    for m, part in enumerate(slots):
        normed[block_rows(here[1] ^ m, quarter), :] = part[...]

    def one(j, _):
        cut = pl.ds(pl.multiple_of(j * tile, tile), tile)
        act, slope = gelu_pair(dot(normed[...], up[0, :, cut], ((1,), (0,))))
        act_out[:, cut] = act.astype(BF16)
        grad = dot(cot[...], down[0, cut, :], ((1,), (1,)))
        pre_out[:, cut] = (grad * slope).astype(BF16)
        return 0

    lax.fori_loop(0, up.shape[2] // tile, one, 0)
    for m, out in enumerate(parts):
        mine = pre_out[block_rows(here[1] ^ m, quarter), :]
        out[...] = dot(mine, up[0], ((1,), (1,))).astype(BF16)


def hidden_layer(here, slots, cot, up, down):
    quarter, width = slots[0].shape
    n_t, units = len(slots), up.shape[2]
    rows = n_t * quarter
    outs = kernel_call(
        functools.partial(hidden_kernel, n_t),
        "hidden_layer",
        [SM] + [VM] * (3 + n_t),
        [shape_of(rows, units), shape_of(rows, units), shape_of(rows, width)]
        + [shape_of(quarter, width)] * n_t,
        (here, cot, up, down, *slots),
        6 * rows * width * units,
    )
    return outs[0], outs[1], outs[2], outs[3:]


def branch_kernel(here, act, down, mixed, own, *sends):
    quarter = own.shape[0]
    for m, out in enumerate([own] + list(sends)):
        part = act[block_rows(here[1] ^ m, quarter), :]
        out[:quarter, :] = dot(part, down[0], ((1,), (0,))).astype(out.dtype)
        if m > 0:
            out[quarter:, :] = mixed[...]


def branch_parts(n_t, here, act, down, mixed):
    rows, (quarter, width) = act.shape[0], mixed.shape
    return kernel_call(
        branch_kernel,
        "branch",
        [SM] + [VM] * 3,
        [shape_of(quarter, width, dtype=F32)] + [shape_of(2 * quarter, width)] * (n_t - 1),
        (here, act, down, mixed),
        2 * rows * width * act.shape[1],
        room=WIDE,
    )


def middle_kernel(n_t, here, after, cot, gain, *refs):
    parts, weights, refs = refs[:n_t], refs[n_t : 2 * n_t], refs[2 * n_t :]
    middle_out, mixed_out, sums_out, grads = refs
    quarter = after.shape[0]
    grad = sum(part[...].astype(F32) for part in parts)
    centered, rate = stats(after[...])
    xhat = centered * rate
    sums_out[...] = column_sums(grad, xhat)
    upstream = cot[block_rows(here[1], quarter), :].astype(F32)
    middle = upstream + norm_back(grad, xhat, rate, gain[0, 1:2])
    middle_out[...] = middle
    mixed = middle.astype(BF16)
    mixed_out[...] = mixed
    for m in range(n_t):
        grads[here[1] ^ m] = dot(mixed, weights[m][...], ((1,), (1,))).astype(BF16)


def middle_back(here, after, cot, gains, parts, weights):
    n_t, (quarter, width) = len(parts), parts[0].shape
    return kernel_call(
        functools.partial(middle_kernel, n_t),
        "middle_back",
        [SM] + [VM] * (3 + 2 * n_t),
        [
            shape_of(quarter, width, dtype=F32),
            shape_of(quarter, width),
            shape_of(2, width, dtype=F32),
            shape_of(n_t, quarter, weights[0].shape[0]),
        ],
        (here, after, cot, gains, *parts, *weights),
        SHIELD,
    )


def join_kernel(mine, theirs, q, out):
    n_z, rows = mine.shape[:2]
    lane = lax.broadcasted_iota(jnp.int32, mine.shape[1:], 1)
    factor = jnp.where(lane < HEAD_DIM, SCORE, 1.0)
    for k in range(n_z):
        out[k, :rows] = ((mine[k] + theirs[k].astype(F32)) * factor).astype(BF16)
        out[k, rows:] = q[k]


def join(mine, theirs, q):
    n_z, rows = mine.shape[:2]
    return kernel_call(
        join_kernel,
        "join",
        [VM] * 3,
        [shape_of(n_z, rows + q.shape[1], 128)],
        (mine, theirs, q),
    )[0]


def unproject_kernel(weight, grads, flat, part):
    n_z, rows = grads.shape[0], flat.shape[0]
    half = rows // 2
    width = n_z * HEAD_DIM
    heads = range(n_z)
    low, high = slice(0, HEAD_DIM), slice(HEAD_DIM, 2 * HEAD_DIM)
    flat[:half, :width] = jnp.concatenate([grads[h, rows:, low] for h in heads], axis=1)
    flat[half:, :width] = jnp.concatenate([grads[h, rows:, high] for h in heads], axis=1)
    flat[:, width : 2 * width] = jnp.concatenate([grads[h, :rows, low] for h in heads], axis=1)
    flat[:, 2 * width :] = jnp.concatenate([grads[h, :rows, high] for h in heads], axis=1)
    total = sum(
        dot(flat[:, c * width : (c + 1) * width], weight[0, c], ((1,), (1,))) for c in range(3)
    )
    part[...] = total.astype(BF16)


def unproject(weight, grads):
    width = weight.shape[2]
    rows = grads.shape[1] * 2 // 3
    return kernel_call(
        unproject_kernel,
        "unproject",
        [VM] * 2,
        [shape_of(rows, 3 * weight.shape[3]), shape_of(rows, width)],
        (weight, grads),
        2 * rows * weight.size,
    )


def last_kernel(here, x, middle, gain, parts, out):
    quarter = middle.shape[0]
    grad = slot_sum(parts)
    centered, rate = stats(x[block_rows(here[1], quarter), :].astype(F32))
    out[...] = (middle[...] + norm_back(grad, centered * rate, rate, gain[0, 0:1])).astype(BF16)


def last_back(here, x, middle, gains, parts):
    return kernel_call(
        last_kernel,
        "last_back",
        [SM] + [VM] * 4,
        [shape_of(*middle.shape)],
        (here, x, middle, gains, parts),
        SHIELD,
    )[0]


def lay_kernel(here, *refs):
    parts, out = refs[:-1], refs[-1]
    for m, part in enumerate(parts):
        out[block_rows(here[1] ^ m, part.shape[0]), :] = part[...].astype(out.dtype)


def lay_rest_kernel(skip, here, *refs):
    n = (len(refs) - 3) // 2
    parts, out, rows, sems = refs[:n], refs[n + 1], refs[n + 2 : -1], refs[-1]
    spots = [block_rows(here[1] ^ (skip + m), part.shape[0]) for m, part in enumerate(parts)]
    for part, row in zip(parts, rows):
        row[...] = part[...].astype(row.dtype)
    for c in load_all([(row, out.at[spot]) for row, spot in zip(rows, spots)], sems):
        c.wait()


def lay_rest(skip, here, parts, base):
    return pl.pallas_call(
        functools.partial(lay_rest_kernel, skip),
        in_specs=[SM] + [VM] * len(parts) + [ANY],
        out_specs=ANY,
        out_shape=shape_of(*base.shape, dtype=base.dtype),
        scratch_shapes=[pltpu.VMEM(part.shape, base.dtype) for part in parts]
        + [pltpu.SemaphoreType.DMA((len(parts),))],
        input_output_aliases={1 + len(parts): 0},
        compiler_params=pltpu.CompilerParams(vmem_limit_bytes=10 * 2**20),
        name="lay_rest",
    )(here, *parts, base)


def lay(n_t, here, parts, dtype):
    quarter, width = parts[0].shape
    return kernel_call(
        lay_kernel,
        "lay",
        [SM] + [VM] * len(parts),
        [shape_of(n_t * quarter, width, dtype=dtype)],
        (here, *parts),
    )[0]


def for_sides(here, mine, theirs, work):
    for out, side in ((theirs, 1), (mine, 0)):

        def one(k, _, out=out, side=side):
            owner = 2 * k + (here[2] ^ side)
            work(out, k, pl.ds(pl.multiple_of(owner * 128, 128), 128))
            return 0

        lax.fori_loop(0, mine.shape[0], one, 0)


def sides(n_z, depth):
    return [shape_of(n_z, depth, 128, dtype=F32), shape_of(n_z, depth, 128)]


def put_lanes(out, k, first, block):
    for j in range(block.shape[1] // 128):
        out[k, first + j * 128 : first + (j + 1) * 128, :] = block[:, j * 128 : (j + 1) * 128]


def early_kernel(here, act, pre, normed, cot, mine, theirs):
    units = act.shape[1]

    def work(out, k, cut):
        out[k, :units, :] = dot(act[...], cot[:, cut], ((0,), (0,))).astype(out.dtype)
        put_lanes(out, k, units, dot(normed[:, cut], pre[...], ((0,), (0,))).astype(out.dtype))

    for_sides(here, mine, theirs, work)


def early_grads(n_z, here, act, pre, normed, cot):
    depth = 2 * act.shape[1]
    return kernel_call(
        early_kernel,
        "early_grads",
        [SM] + [VM] * 4,
        sides(n_z, depth),
        (here, act, pre, normed, cot),
        2 * act.shape[0] * depth * normed.shape[1],
    )


def halves(x):
    high = x.astype(BF16)
    return high, (x - high.astype(F32)).astype(BF16)


def outward_kernel(here, attended, *refs):
    mixed, (mine, theirs) = refs[:-2], refs[-2:]
    quarter = attended.shape[0] // len(mixed)

    def work(out, k, cut):
        outward = sum(
            dot(attended[block_rows(here[1] ^ m, quarter), :], part[-quarter:, cut], ((0,), (0,)))
            for m, part in enumerate(mixed)
        )
        out[k] = outward.astype(out.dtype)

    for_sides(here, mine, theirs, work)


def outward_grads(n_z, here, attended, mixed):
    rows, share = attended.shape
    return kernel_call(
        outward_kernel,
        "outward_grads",
        [SM] + [VM] * (1 + len(mixed)),
        sides(n_z, share),
        (here, attended, *mixed),
        2 * rows * share * mixed[0].shape[1],
    )


def fold_slots_kernel(here, mine, theirs, *outs):
    for k, out in enumerate(outs):
        at = lax.rem(here[0] + k, len(outs))
        out[...] = (mine[at] + theirs[at].astype(F32)).astype(out.dtype)


def fold_slots(here, mine, theirs):
    n_z, depth, _ = mine.shape
    return kernel_call(
        fold_slots_kernel,
        "fold_slots",
        [SM] + [VM] * 2,
        [shape_of(depth, 128, dtype=F32)] + [shape_of(depth, 128)] * (n_z - 1),
        (here, mine, theirs),
    )


def late_kernel(here, x, normed, grad, sums, part, mine, theirs, scratch):
    depth, step = grad.shape[1], 256
    total = jnp.zeros((2, x.shape[1]), F32)
    for m in range(x.shape[0] // step):
        spot = slice(m * step, (m + 1) * step)
        centered, rate = stats(x[spot, :].astype(F32))
        total = total + column_sums(part[spot, :].astype(F32), centered * rate)
    scratch[0:2, :] = total
    scratch[2:4, :] = sums[...]
    scratch[4:8, :] = jnp.zeros((4, x.shape[1]), F32)

    def work(out, k, cut):
        put_lanes(out, k, 0, dot(normed[:, cut], grad[...], ((0,), (0,))).astype(out.dtype))
        block = scratch[:, cut]
        if out.dtype == BF16:
            high, low = halves(block[0:4])
            block = jnp.concatenate([high.astype(F32), low.astype(F32)], axis=0).astype(BF16)
        out[k, depth:, :] = block

    for_sides(here, mine, theirs, work)


def late_grads(n_z, here, x, normed, grad, sums, part):
    depth = grad.shape[1] + 8
    return kernel_call(
        late_kernel,
        "late_grads",
        [SM] + [VM] * 5,
        sides(n_z, depth),
        (here, x, normed, grad, sums, part),
        2 * grad.shape[0] * depth * normed.shape[1],
        [pltpu.VMEM((8, x.shape[1]), F32)],
    )


def fold_kernel(mine, theirs, out):
    for k in range(mine.shape[0]):
        out[k] = (mine[k] + theirs[k].astype(F32)).astype(BF16)


def fold(mine, theirs):
    return kernel_call(
        fold_kernel, "fold", [VM] * 2, [shape_of(*mine.shape)], (mine, theirs)
    )[0]


def fold_late_kernel(mine, theirs, out):
    depth = mine.shape[1] - 8
    for k in range(mine.shape[0]):
        out[k, :depth] = (mine[k, :depth] + theirs[k, :depth].astype(F32)).astype(BF16)
        tail = mine[k, depth:] + theirs[k, depth:].astype(F32)
        high, low = halves(tail[0:4] + tail[4:8])
        both = jnp.concatenate([high.astype(F32), low.astype(F32)], axis=0)
        out[k, depth:] = both.astype(BF16)


def fold_late(mine, theirs):
    return kernel_call(
        fold_late_kernel, "fold_late", [VM] * 2, [shape_of(*mine.shape)], (mine, theirs)
    )[0]


def slot_sum(parts):
    return sum(parts[k].astype(F32) for k in range(parts.shape[0]))


def finish_early_kernel(parts, down_out, up_out):
    total = slot_sum(parts)
    units = down_out.shape[0]
    down_out[...] = total[:units]
    for j in range(units // 128):
        up_out[:, j * 128 : (j + 1) * 128] = total[units + j * 128 : units + (j + 1) * 128]


def finish_early(units, parts):
    return kernel_call(
        finish_early_kernel,
        "finish_early",
        [VM],
        [shape_of(units, 128, dtype=F32), shape_of(128, units, dtype=F32)],
        (parts,),
    )


def finish_late_kernel(parts, out, sums_out):
    total = slot_sum(parts)
    per = out.shape[2] // 128
    for c in range(3):
        for j in range(per):
            at = (c * per + j) * 128
            out[c, :, j * 128 : (j + 1) * 128] = total[at : at + 128]
    last = total.shape[0] - 8
    sums_out[...] = jnp.concatenate([total[last : last + 4] + total[last + 4 :]] * 2, axis=0)


def finish_late(share, parts):
    return kernel_call(
        finish_late_kernel,
        "finish_late",
        [VM],
        [
            shape_of(3, 128, share, dtype=F32),
            shape_of(8, 128, dtype=F32),
        ],
        (parts,),
    )


def scene_edges(scene_index):
    total = scene_index.shape[0]
    at = lax.iota(jnp.int32, total)
    edge = jnp.concatenate([jnp.ones((1,), jnp.bool_), scene_index[1:] != scene_index[:-1]])
    starts = lax.cummax(jnp.where(edge, at, 0))
    closing = jnp.concatenate([edge[1:], jnp.ones((1,), jnp.bool_)])
    return starts, lax.cummin(jnp.where(closing, at + 1, total), reverse=True)


def body(
    n_seq,
    n_tp,
    tokens,
    scene_index,
    inward_weight,
    outward_weight,
    up_weight,
    down_weight,
    norm_gains,
    norm_shifts,
    cotangent,
):
    n_z, rows, width = n_seq // 2, tokens.shape[0], tokens.shape[1]
    units, share = up_weight.shape[2], outward_weight.shape[1]
    quarter = rows // n_tp
    seq, tp = lax.axis_index("seq"), lax.axis_index("tp")
    z, c = seq // 2, seq % 2
    here = jnp.stack([z, tp, c]).astype(jnp.int32)
    lines = [list(range(b, n_seq, 2)) for b in range(2)]

    def line(x):
        return lax.all_to_all(x, "seq", 0, 0, axis_index_groups=lines, tiled=True)

    def plane(x):
        return lax.all_to_all(x, "tp", 0, 0, tiled=True)

    def across(x):
        return lax.ppermute(x, "seq", [(a, a ^ 1) for a in range(n_seq)])

    def along(x, k):
        return lax.ppermute(
            x, "seq", [(a * 2 + b, (a + k) % n_z * 2 + b) for a in range(n_z) for b in range(2)]
        )

    def over(x, m):
        return lax.ppermute(x, "tp", [(a, a ^ m) for a in range(n_tp)])

    def square(slots):
        return [slots[0]] + [over(slots[m], m) for m in range(1, n_tp)]

    place = jnp.stack([k * 2 + (c ^ g) for g in range(2) for k in range(n_z)]).astype(jnp.int32)
    starts, ends = scene_edges(scene_index)
    normed, kv_send, q_send = project(n_z, here, tokens, norm_gains, norm_shifts, inward_weight)
    kv_mine = line(kv_send)
    q = [q_send[0]] + [along(q_send[k], k) for k in range(1, n_z)]
    (kv_mine, starts, ends, place, q) = lax.optimization_barrier((kv_mine, starts, ends, place, q))
    kv_other = across(kv_mine)
    outward_all = square([outward_weight[0]] * n_tp)
    o, o_full, lse, kv_full = attn_fwd(kv_mine, kv_other, q, here, place, starts, ends, 1024)
    (o, outward_all) = lax.optimization_barrier((o, outward_all))
    attended = spread(line(o))
    parts = plane(attended.reshape(n_tp, quarter, share))
    after, normed_two = mix(here, tokens, norm_gains, norm_shifts, parts, outward_all)
    act, pre, normed_two, grad_parts = hidden_layer(
        here, square([normed_two] * n_tp), cotangent, up_weight, down_weight
    )
    middle, mixed, sums_two, grads = middle_back(
        here, after, cotangent, norm_gains, square(grad_parts), outward_all
    )
    mine, theirs = early_grads(n_z, here, act, pre, normed_two, cotangent)
    early = fold(mine, across(theirs))
    branch = branch_parts(n_tp, here, act, down_weight, mixed)
    grads = plane(grads)
    (grads, early, branch) = lax.optimization_barrier((grads, early, branch))
    g = pack(n_z, here, grads.reshape(rows, share))
    g = [g[0]] + [along(g[k], k) for k in range(1, n_z)]
    (g, early) = lax.optimization_barrier((g, early))
    early = line(early)
    branch = square(branch)
    dq, dkv, dkv_theirs = attn_bwd(kv_full, q, g, o_full, lse, here, place, starts, ends, 1024)
    (dq, dkv, dkv_theirs, branch) = lax.optimization_barrier((dq, dkv, dkv_theirs, branch))
    mixed = [mixed] + branch[1:]
    back = join(dkv, across(dkv_theirs), dq)
    (back, early) = lax.optimization_barrier((back, early))
    back = line(back)
    out_own = (after + sum(part[:quarter].astype(F32) for part in branch)).astype(BF16)
    out_slots = square([out_own] * n_tp)
    down_grad, up_grad = finish_early(units, early)
    activations = lay(n_tp, here, out_slots, BF16)
    mine, theirs = outward_grads(n_z, here, attended, mixed)
    side = fold_slots(here, mine, across(theirs))
    (back, activations, down_grad, up_grad, side) = lax.optimization_barrier(
        (back, activations, down_grad, up_grad, side)
    )
    side = [side[0]] + [along(side[k], k) for k in range(1, n_z)]
    flat, back_part = unproject(inward_weight, back)
    mine, theirs = late_grads(n_z, here, tokens, normed, flat, sums_two, back_part)
    late = fold_late(mine, across(theirs))
    back_part = plane(back_part.reshape(n_tp, quarter, width))
    (back_part, late, side) = lax.optimization_barrier((back_part, late, side))
    outward_grad = sum(part.astype(F32) for part in side)
    token_own = last_back(here, tokens, middle, norm_gains, back_part)
    late = line(late)
    token_slots = square([token_own] * n_tp)
    token_grad = lay(n_tp, here, token_slots[:2], F32)
    (late, token_grad, outward_grad) = lax.optimization_barrier((late, token_grad, outward_grad))
    inward_grad, sums = finish_late(share, late)
    sums = square([sums] * n_tp)
    (sums, token_slots) = lax.optimization_barrier((sums, token_slots))
    token_grad = lay_rest(2, here, token_slots[2:], token_grad)
    while len(sums) > 1:
        sums = [sums[m] + sums[m + 1] for m in range(0, len(sums), 2)]
    sums = sums[0]
    gain_grad = jnp.stack([sums[0], sums[2]])
    shift_grad = jnp.stack([sums[1], sums[3]])
    return (
        activations,
        token_grad,
        inward_grad[None],
        outward_grad[None],
        up_grad[None],
        down_grad[None],
        gain_grad[None],
        shift_grad[None],
    )


def layer_norm(hidden, gain_row, shift_row):
    average = jnp.mean(hidden, axis=-1, keepdims=True)
    centered = hidden - average
    variance = jnp.mean(centered * centered, axis=-1, keepdims=True)
    return centered * lax.rsqrt(variance + 1e-05) * gain_row + shift_row


def gelu_tanh(preactivation):
    return jax.nn.gelu(preactivation, approximate=True)


def to_heads(flat_rows):
    return flat_rows.reshape(flat_rows.shape[0], -1, HEAD_DIM)


def scenes_meet(query_scenes, key_scenes):
    return jnp.logical_and(key_scenes[0] <= query_scenes[-1], key_scenes[-1] >= query_scenes[0])


def score_rows(query_heads, key_heads, query_scenes, key_scenes):
    scores = jnp.einsum(
        "qhd,khd->hqk", query_heads, key_heads, preferred_element_type=jnp.float32
    ) * HEAD_DIM ** (-0.5)
    same_scene = (query_scenes[:, None] == key_scenes[None, :])[None]
    return (scores, same_scene)


def probabilities(scores, same_scene, normalizer):
    return jnp.where(same_scene, jnp.exp(scores - normalizer[:, :, None]), 0.0)


def key_tiles(key_all, value_all, scene_index):
    tile_rows = min(1024, key_all.shape[0])
    tile_count = key_all.shape[0] // tile_rows
    return (
        key_all.reshape(tile_count, tile_rows, -1, HEAD_DIM),
        value_all.reshape(tile_count, tile_rows, -1, HEAD_DIM),
        scene_index.reshape(tile_count, tile_rows),
    )


def log_normalizer(query_heads, query_scenes, tiled_keys):

    def log_visit_tile(running_pair, inputs_pair):
        key_heads, key_scenes = inputs_pair

        def log_compute(pair_now):
            running_max, running_sum = pair_now
            scores, same_scene = score_rows(query_heads, key_heads, query_scenes, key_scenes)
            masked = jnp.where(same_scene, scores, NEG_FILL)
            new_max = jnp.maximum(running_max, jnp.max(masked, axis=-1))
            weights = jnp.where(same_scene, jnp.exp(masked - new_max[:, :, None]), 0.0)
            return (
                new_max,
                running_sum * jnp.exp(running_max - new_max) + jnp.sum(weights, axis=-1),
            )

        return (
            lax.cond(
                scenes_meet(query_scenes, key_scenes),
                log_compute,
                lambda pair_now: pair_now,
                running_pair,
            ),
            None,
        )

    stat_shape = (query_heads.shape[1], query_heads.shape[0])
    start_pair = (jnp.full(stat_shape, NEG_FILL, jnp.float32), jnp.zeros(stat_shape, jnp.float32))
    final_pair, _ = lax.scan(log_visit_tile, start_pair, (tiled_keys[0], tiled_keys[2]))
    return final_pair[0] + jnp.log(final_pair[1])


def attend_all(query_heads, query_scenes, tiled_keys, normalizer):

    def attend_visit_tile(running_total, inputs_triple):
        key_heads, value_heads, key_scenes = inputs_triple

        def attend_compute(total_now):
            scores, same_scene = score_rows(query_heads, key_heads, query_scenes, key_scenes)
            weights = probabilities(scores, same_scene, normalizer).astype(jnp.bfloat16)
            return total_now + jnp.einsum(
                "hqk,khd->qhd", weights, value_heads, preferred_element_type=jnp.float32
            )

        return (
            lax.cond(
                scenes_meet(query_scenes, key_scenes),
                attend_compute,
                lambda total_now: total_now,
                running_total,
            ),
            None,
        )

    running_total, _ = lax.scan(
        attend_visit_tile, jnp.zeros(query_heads.shape, jnp.float32), tiled_keys
    )
    return running_total.reshape(running_total.shape[0], -1)


def score_gradients(
    query_heads,
    key_heads,
    value_heads,
    grad_heads,
    query_scenes,
    key_scenes,
    normalizer,
    delta_rows,
):
    scores, same_scene = score_rows(query_heads, key_heads, query_scenes, key_scenes)
    weights = probabilities(scores, same_scene, normalizer)
    weight_grad = jnp.einsum(
        "qhd,khd->hqk", grad_heads, value_heads, preferred_element_type=jnp.float32
    )
    score_grad = (weights * (weight_grad - delta_rows[:, :, None])).astype(jnp.bfloat16)
    return (weights.astype(jnp.bfloat16), score_grad)


def grads_by_reduce(query_heads, grad_heads, query_scenes, tiled_keys, normalizer, delta_rows):
    tile_rows = tiled_keys[0].shape[1]
    joined_width = 2 * query_heads.shape[1] * query_heads.shape[2]

    def grads_visit_tile(query_total, inputs_triple):
        key_heads, value_heads, key_scenes = inputs_triple

        def grads_compute(total_now):
            weights, score_grad = score_gradients(
                query_heads,
                key_heads,
                value_heads,
                grad_heads,
                query_scenes,
                key_scenes,
                normalizer,
                delta_rows,
            )
            total_now = total_now + jnp.einsum(
                "hqk,khd->qhd", score_grad, key_heads, preferred_element_type=jnp.float32
            )
            key_term = jnp.einsum(
                "hqk,qhd->khd", score_grad, query_heads, preferred_element_type=jnp.float32
            )
            value_term = jnp.einsum(
                "hqk,qhd->khd", weights, grad_heads, preferred_element_type=jnp.float32
            )
            joined = jnp.concatenate(
                [key_term.reshape(tile_rows, -1), value_term.reshape(tile_rows, -1)], axis=1
            )
            return (total_now, joined)

        def skipped(total_now):
            return (total_now, jnp.zeros((tile_rows, joined_width), jnp.float32))

        return lax.cond(scenes_meet(query_scenes, key_scenes), grads_compute, skipped, query_total)

    query_total, key_terms_all = lax.scan(
        grads_visit_tile, jnp.zeros(query_heads.shape, jnp.float32), tiled_keys
    )
    key_terms_all = key_terms_all.reshape(-1, key_terms_all.shape[-1])
    summed = lax.psum_scatter(key_terms_all, "seq", scatter_dimension=0, tiled=True)
    half_width = summed.shape[1] // 2
    return (
        query_total.reshape(query_total.shape[0], -1),
        summed[:, :half_width],
        summed[:, half_width:],
    )


def generic_body(
    tokens,
    scene_index,
    inward_weight,
    outward_weight,
    up_weight,
    down_weight,
    norm_gains,
    norm_shifts,
    cotangent,
):
    local_rows = tokens.shape[0]
    score_factor = HEAD_DIM ** (-0.5)
    query_scenes = lax.dynamic_slice_in_dim(
        scene_index, lax.axis_index("seq") * local_rows, local_rows
    )
    hidden = tokens.astype(jnp.float32)
    layer_number = 0
    gain_pair = norm_gains[layer_number]
    shift_pair = norm_shifts[layer_number]
    normed = layer_norm(hidden, gain_pair[0], shift_pair[0]).astype(jnp.bfloat16)
    projected = jnp.einsum(
        "td,cde->tce", normed, inward_weight[layer_number], preferred_element_type=jnp.float32
    ).astype(jnp.bfloat16)
    queries = projected[:, 0]
    key_local = projected[:, 1]
    value_local = projected[:, 2]
    key_all = lax.all_gather(key_local, "seq", axis=0, tiled=True)
    value_all = lax.all_gather(value_local, "seq", axis=0, tiled=True)
    tiled_keys = key_tiles(key_all, value_all, scene_index)
    query_heads = to_heads(queries)
    normalizer = log_normalizer(query_heads, query_scenes, tiled_keys)
    attended = attend_all(query_heads, query_scenes, tiled_keys, normalizer)
    attended_low = attended.astype(jnp.bfloat16)
    mixed_sum = lax.psum(
        jnp.dot(attended_low, outward_weight[layer_number], preferred_element_type=jnp.float32),
        "tp",
    )
    after_attention = hidden + mixed_sum
    normed_two = layer_norm(after_attention, gain_pair[1], shift_pair[1]).astype(jnp.bfloat16)
    preactivation = jnp.dot(normed_two, up_weight[layer_number], preferred_element_type=jnp.float32)
    activated = gelu_tanh(preactivation).astype(jnp.bfloat16)
    branch = lax.psum(
        jnp.dot(activated, down_weight[layer_number], preferred_element_type=jnp.float32), "tp"
    )
    kept_layers = [
        (
            hidden,
            after_attention,
            queries,
            key_local,
            value_local,
            tiled_keys,
            normalizer,
            attended,
            attended_low,
            preactivation,
            activated,
        )
    ]
    hidden = after_attention + branch
    upstream = cotangent.astype(jnp.float32)
    layer_grads = [None] * LAYERS
    for layer_number in reversed(range(LAYERS)):
        (
            hidden_in,
            after_attention,
            queries,
            key_local,
            value_local,
            tiled_keys,
            normalizer,
            attended,
            attended_low,
            preactivation,
            activated,
        ) = kept_layers[layer_number]
        gain_pair = norm_gains[layer_number]
        shift_pair = norm_shifts[layer_number]
        branch_grad = upstream.astype(jnp.bfloat16)
        down_grad = jnp.einsum(
            "tf,td->fd", activated, branch_grad, preferred_element_type=jnp.float32
        )
        act_grad = jnp.einsum(
            "td,fd->tf", branch_grad, down_weight[layer_number], preferred_element_type=jnp.float32
        )
        _, gelu_pull = jax.vjp(gelu_tanh, preactivation)
        preactivation_grad = gelu_pull(act_grad)[0].astype(jnp.bfloat16)
        normed_two_f, norm_pull_two = jax.vjp(
            layer_norm, after_attention, gain_pair[1], shift_pair[1]
        )
        normed_two = normed_two_f.astype(jnp.bfloat16)
        up_grad = jnp.einsum(
            "td,tf->df", normed_two, preactivation_grad, preferred_element_type=jnp.float32
        )
        normed_two_grad = lax.psum(
            jnp.einsum(
                "tf,df->td",
                preactivation_grad,
                up_weight[layer_number],
                preferred_element_type=jnp.float32,
            ),
            "tp",
        )
        middle_part, gain_two, shift_two = norm_pull_two(normed_two_grad)
        middle_grad = upstream + middle_part
        mixed_grad = middle_grad.astype(jnp.bfloat16)
        outward_grad = jnp.einsum(
            "te,td->ed", attended_low, mixed_grad, preferred_element_type=jnp.float32
        )
        attended_grad = jnp.einsum(
            "td,ed->te",
            mixed_grad,
            outward_weight[layer_number],
            preferred_element_type=jnp.float32,
        ).astype(jnp.bfloat16)
        delta_rows = jnp.sum(to_heads(attended_grad.astype(jnp.float32) * attended), axis=-1).T
        query_sum, key_sum, value_sum = grads_by_reduce(
            to_heads(queries),
            to_heads(attended_grad),
            query_scenes,
            tiled_keys,
            normalizer,
            delta_rows,
        )
        projected_grad = jnp.stack(
            [query_sum * score_factor, key_sum * score_factor, value_sum], axis=1
        ).astype(jnp.bfloat16)
        normed_f, norm_pull = jax.vjp(layer_norm, hidden_in, gain_pair[0], shift_pair[0])
        normed = normed_f.astype(jnp.bfloat16)
        inward_grad = jnp.einsum(
            "td,tce->cde", normed, projected_grad, preferred_element_type=jnp.float32
        )
        normed_grad = lax.psum(
            jnp.einsum(
                "tce,cde->td",
                projected_grad,
                inward_weight[layer_number],
                preferred_element_type=jnp.float32,
            ),
            "tp",
        )
        input_part, gain_one, shift_one = norm_pull(normed_grad)
        upstream = middle_grad + input_part
        layer_grads[layer_number] = (
            lax.psum_scatter(inward_grad, "seq", scatter_dimension=1, tiled=True),
            lax.psum_scatter(outward_grad, "seq", scatter_dimension=1, tiled=True),
            lax.psum_scatter(up_grad, "seq", scatter_dimension=0, tiled=True),
            lax.psum_scatter(down_grad, "seq", scatter_dimension=1, tiled=True),
            lax.psum_scatter(
                jnp.stack([gain_one, gain_two]), "seq", scatter_dimension=1, tiled=True
            ),
            lax.psum_scatter(
                jnp.stack([shift_one, shift_two]), "seq", scatter_dimension=1, tiled=True
            ),
        )
    return (
        hidden.astype(jnp.bfloat16),
        upstream,
        jnp.stack([layer_part[0] for layer_part in layer_grads]),
        jnp.stack([layer_part[1] for layer_part in layer_grads]),
        jnp.stack([layer_part[2] for layer_part in layer_grads]),
        jnp.stack([layer_part[3] for layer_part in layer_grads]),
        jnp.stack([layer_part[4] for layer_part in layer_grads]),
        jnp.stack([layer_part[5] for layer_part in layer_grads]),
    )


def solution(mesh):
    placed = (
        P("seq", None),
        P(),
        P(None, None, None, "tp"),
        P(None, "tp", None),
        P(None, None, "tp"),
        P(None, "tp", None),
        P(),
        P(),
        P("seq", None),
    )
    n_seq, n_tp = mesh.shape["seq"], mesh.shape["tp"]
    fits = n_seq == 8 and n_tp == 4
    return jax.shard_map(
        functools.partial(body, n_seq, n_tp) if fits else generic_body,
        mesh=mesh,
        in_specs=placed,
        out_specs=(
            P("seq", None),
            P("seq", None),
            P(None, None, "seq", "tp"),
            P(None, "tp", "seq"),
            P(None, "seq", "tp"),
            P(None, "tp", "seq"),
            P(None, None, "seq"),
            P(None, None, "seq"),
        ),
        check_vma=False,
    )
```
